32 devices in a mesh: seg: 16 (over z, y, core), row: 2 (over x).
Axes of the slice: x: 2, y: 2, z: 4, core: 2. Of those that a mesh axis runs over, the one named last changes fastest.
Arguments:
- tokens: bfloat16 [16, 512, 1024], P('seg', 'row'), may hold values from -6 to 6
- cotangent: bfloat16 [16, 512, 1024], P('seg', 'row'), may hold values from -6 to 6
- memory_keys: bfloat16 [16, 4096, 1024], P('seg'), may hold values from -6 to 6
- memory_values: bfloat16 [16, 4096, 1024], P('seg'), may hold values from -6 to 6
- memory_choice: int32 [16, 1, 8, 128], P('seg'), may hold values from 0 to 4095
- memory_flag: int32 [16], P('seg'), may hold values 0 or 1
- w_query: bfloat16 [1024, 1024], P(('seg', 'row')), may hold values from -0.1875 to 0.1875
- w_key: bfloat16 [1024, 1024], P(('seg', 'row')), may hold values from -0.1875 to 0.1875
- w_value: bfloat16 [1024, 1024], P(('seg', 'row')), may hold values from -0.1875 to 0.1875
- w_out: bfloat16 [1024, 1024], P(('seg', 'row')), may hold values from -1.5 to 1.5
- w_gate: bfloat16 [1024, 2816], P(('seg', 'row')), may hold values from -0.1875 to 0.1875
- w_up: bfloat16 [1024, 2816], P(('seg', 'row')), may hold values from -0.1875 to 0.1875
- w_down: bfloat16 [2816, 1024], P(('seg', 'row')), may hold values from -0.109375 to 0.109375
- norm_attn: bfloat16 [1024], P(('seg', 'row')), may hold values from 0.5 to 1.5
- norm_ffn: bfloat16 [1024], P(('seg', 'row')), may hold values from 0.5 to 1.5
Outputs:
- layer_out: bfloat16 [16, 512, 1024], P('seg', 'row')
- grad_tokens: bfloat16 [16, 512, 1024], P('seg', 'row')
- grad_query: float32 [1024, 1024], P(('seg', 'row'))
- grad_key: float32 [1024, 1024], P(('seg', 'row'))
- grad_value: float32 [1024, 1024], P(('seg', 'row'))
- grad_out: float32 [1024, 1024], P(('seg', 'row'))
- grad_gate: float32 [1024, 2816], P(('seg', 'row'))
- grad_up: float32 [1024, 2816], P(('seg', 'row'))
- grad_down: float32 [2816, 1024], P(('seg', 'row'))
- grad_norm_attn: float32 [1024], P(('seg', 'row'))
- grad_norm_ffn: float32 [1024], P(('seg', 'row'))
The draws below stay inside these ranges and needn't reach their ends.
All inputs are finite; a program needn't handle non-finite values. No bound on the sum of `memory_flag` on one device may be relied on, other than what follows from the above.
Results may differ from the reference program's by a relative error of at most 0.02.
Values may be sent and summed in bfloat16 or wider, within the bound.
A program may use at most 192 MiB of HBM per device.

```python
import jax
import jax.numpy as jnp
from jax import lax

D = 1024
HEADS = 8
HD = 128
FF = 2816
QBLK = 512
MEM = 4096
CHOSEN_KEY_COUNT = 128
LEN = 512
NSEG = 16
NQB = 1


def plant(drawn, key, smallest, top_value):
    dims = drawn.shape
    place = [jax.random.randint(jax.random.fold_in(key, axis), (), 0, dims[axis]) for axis in range(len(dims))]
    drawn = drawn.at[tuple(place)].set(smallest)
    longest = dims.index(max(dims))
    place[longest] = (place[longest] + 1) % dims[longest]
    return drawn.at[tuple(place)].set(top_value)


def shard_levels(rng, extent, cuts, least, largest):
    def one(axis_at, shards_of):
        steps = jax.random.uniform(jax.random.fold_in(jax.random.fold_in(rng, 6), axis_at), (shards_of,), jnp.float32, least / len(cuts), largest / len(cuts))
        return jnp.repeat(jnp.exp(steps), extent[axis_at] // shards_of).reshape((-1,) + (1,) * (len(extent) - axis_at - 1))

    level = one(*cuts[0])
    for cut in cuts[1:]:
        level = level * one(*cut)
    return level


def noise(rng, dims, deviation, reach, cuts=(), dtype=jnp.bfloat16):
    drawn = deviation * jax.random.normal(rng, dims, jnp.float32)
    if cuts:
        drawn = drawn * shard_levels(rng, dims, cuts, -0.22, 0.18)
    return jnp.clip(drawn, -reach, reach).astype(dtype)


def setup_inputs(seed: int = 0) -> dict:
    splits = jax.random.split(jax.random.key(seed), 16)
    tokens = noise(splits[0], (NSEG, LEN, D), 1.0, 6.0, ((0, 16), (1, 2)))
    cotangent = noise(splits[1], (NSEG, LEN, D), 1.0, 6.0, ((0, 16), (1, 2)))
    memory_keys = noise(splits[2], (NSEG, MEM, D), 1.0, 6.0, ((0, 16),))
    memory_values = noise(splits[3], (NSEG, MEM, D), 1.0, 6.0, ((0, 16),))
    memory_choice = plant(jax.random.randint(splits[4], (NSEG, NQB, HEADS, CHOSEN_KEY_COUNT), 0, MEM), jax.random.fold_in(splits[4], 1), 0, MEM - 1).astype(jnp.int32)
    memory_flag = plant((jax.random.randint(splits[5], (NSEG,), 0, 2) < 1).astype(jnp.int32), jax.random.fold_in(splits[5], 1), 0, 1)
    w_query = noise(splits[6], (D, D), D ** -0.5, 0.1875, ((0, 32),))
    w_key = noise(splits[7], (D, D), D ** -0.5, 0.1875, ((0, 32),))
    w_value = noise(splits[8], (D, D), D ** -0.5, 0.1875, ((0, 32),))
    w_out = noise(splits[9], (D, D), (D // 64) ** -0.5, 1.5, ((0, 32),))
    w_gate = noise(splits[10], (D, FF), D ** -0.5, 0.1875, ((0, 32),))
    w_up = noise(splits[11], (D, FF), D ** -0.5, 0.1875, ((0, 32),))
    w_down = noise(splits[12], (FF, D), FF ** -0.5, 0.109375, ((0, 32),))
    norm_attn = jnp.clip(1.0 + 0.1 * jax.random.normal(splits[13], (D,), jnp.float32), 0.5, 1.5).astype(jnp.bfloat16)
    norm_ffn = jnp.clip(1.0 + 0.1 * jax.random.normal(splits[14], (D,), jnp.float32), 0.5, 1.5).astype(jnp.bfloat16)
    return {"tokens": tokens, "cotangent": cotangent, "memory_keys": memory_keys, "memory_values": memory_values, "memory_choice": memory_choice, "memory_flag": memory_flag, "w_query": w_query, "w_key": w_key, "w_value": w_value, "w_out": w_out, "w_gate": w_gate, "w_up": w_up, "w_down": w_down, "norm_attn": norm_attn, "norm_ffn": norm_ffn}


@jax.custom_vjp
def low(v):
    return lax.optimization_barrier(v.astype(jnp.bfloat16)).astype(jnp.float32)

@jax.custom_vjp
def low_back(v):
    return v

def low_keep(v):
    return (low(v), None)

def low_pass(kept, grad):
    return (grad,)

def back_keep(v):
    return (v, None)

def back_low(kept, grad):
    return (low(grad),)
low.defvjp(low_keep, low_pass)
low_back.defvjp(back_keep, back_low)
EPS = 1e-06
NEG = -1000000000.0

def hot(a, b):
    return jnp.dot(a, b, precision=lax.Precision.HIGHEST)

def rms_norm(v, gain):
    return v * lax.rsqrt(lax.optimization_barrier(jnp.mean(v * v, axis=-1, keepdims=True)) + EPS) * gain

def segment_layer(params, pieces):
    wq, wk, wv, wo, wg, wu, wd, g1, g2 = params
    x, mem_k, mem_v, chosen, flag = pieces
    score_scale = HD ** (-0.5)
    a1 = low(rms_norm(x, g1))
    q = low(low_back(hot(a1, wq)))
    k = low(low_back(hot(a1, wk)))
    v = low(low_back(hot(a1, wv)))
    keys = k.reshape(LEN, HEADS, HD)
    vals = v.reshape(LEN, HEADS, HD)
    mem_kh = mem_k.reshape(MEM, HEADS, HD)
    mem_vh = mem_v.reshape(MEM, HEADS, HD)
    head_ids = jnp.arange(HEADS).astype(jnp.int32)[:, None]
    key_pos = jnp.arange(LEN).astype(jnp.int32)

    def block(args):
        query_block, sel, first = args
        memory_key_rows = mem_kh[sel, head_ids]
        memory_value_rows = mem_vh[sel, head_ids]
        local = low_back(jnp.einsum('qhd,khd->hqk', query_block, keys, precision=lax.Precision.HIGHEST) * score_scale)
        distant_memory = low_back(jnp.einsum('grv,rbv->rgb', query_block, memory_key_rows, precision=lax.Precision.HIGHEST) * score_scale)
        pos = first + jnp.arange(QBLK).astype(jnp.int32)
        local = jnp.where(key_pos[None, None, :] <= pos[None, :, None], local, NEG)
        distant_memory = jnp.where(flag > 0, distant_memory, NEG)
        softmax_weights = low(jax.nn.softmax(jnp.concatenate([distant_memory, local], axis=-1), axis=-1))
        attention_output = jnp.einsum('rpv,rvb->prb', softmax_weights[..., :CHOSEN_KEY_COUNT], memory_value_rows, precision=lax.Precision.HIGHEST)
        attention_output = attention_output + jnp.einsum('hqk,khd->qhd', softmax_weights[..., CHOSEN_KEY_COUNT:], vals, precision=lax.Precision.HIGHEST)
        return attention_output.reshape(QBLK, D)
    starts = (jnp.arange(NQB) * QBLK).astype(jnp.int32)
    outs = lax.map(jax.checkpoint(block), (q.reshape(NQB, QBLK, HEADS, HD), chosen, starts))
    ao = low(low_back(outs.reshape(LEN, D)))
    h = x + low_back(hot(ao, wo))
    a2 = low(rms_norm(h, g2))
    gate = low_back(hot(a2, wg))
    up = low_back(hot(a2, wu))
    hid = low(jax.nn.silu(gate) * up)
    return h + hot(hid, wd)

def reference(tokens, cotangent, memory_keys, memory_values, memory_choice, memory_flag, w_query, w_key, w_value, w_out, w_gate, w_up, w_down, norm_attn, norm_ffn):
    x32 = tokens.astype(jnp.float32)
    mem_k = memory_keys.astype(jnp.float32)
    mem_v = memory_values.astype(jnp.float32)
    params = tuple((w.astype(jnp.float32) for w in (w_query, w_key, w_value, w_out, w_gate, w_up, w_down, norm_attn, norm_ffn)))

    def forward(inputs, weights):

        def one(pieces):
            return jax.checkpoint(segment_layer)(weights, pieces)
        return lax.map(one, (inputs, mem_k, mem_v, memory_choice, memory_flag))
    result, pull = jax.vjp(forward, x32, params)
    grad_x, grads = pull(cotangent.astype(jnp.float32))
    return (result.astype(jnp.bfloat16), grad_x.astype(jnp.bfloat16), grads[0], grads[1], grads[2], grads[3], grads[4], grads[5], grads[6], grads[7], grads[8])
```

```python
import functools

import jax
import jax.numpy as jnp
from jax import lax
from jax.experimental import pallas as pl
from jax.experimental.pallas import tpu as pltpu
from jax.sharding import PartitionSpec as P

HEADS = 8
HD = 128
QBLK = 512


EPS = 1e-06
NEG = -1000000000.0


def for_sending(array):

    def short(part):
        return part.astype(jnp.bfloat16) if part.dtype == jnp.float32 else part

    return jax.tree.map(short, array)


def plain_dot(left, right):
    return jnp.dot(left, right, preferred_element_type=jnp.float32)


def dot_left(left, right):
    return lax.dot_general(
        left, right, (((0,), (0,)), ((), ())), preferred_element_type=jnp.float32
    )


def dot_right(left, right):
    return lax.dot_general(
        left, right, (((1,), (1,)), ((), ())), preferred_element_type=jnp.float32
    )


def norm_apply(value, gain):
    inverse = lax.rsqrt(jnp.mean(value * value, axis=-1, keepdims=True) + EPS)
    return (value * inverse * gain, inverse)


def norm_back(value, gain, inverse, grad):
    unit = value * inverse
    gain_grad = jnp.sum(grad * unit, axis=0)
    scaled = grad * gain
    return (inverse * (scaled - unit * jnp.mean(scaled * unit, axis=-1, keepdims=True)), gain_grad)


def score_block(queries, keys, memory_key_rows, flag, first, length):
    score_scale = HD ** (-0.5)
    local = (
        jnp.einsum("bqhd,khd->bhqk", queries, keys, preferred_element_type=jnp.float32)
        * score_scale
    )
    distant_memory = (
        jnp.einsum("bqhd,bhmd->bhqm", queries, memory_key_rows, preferred_element_type=jnp.float32)
        * score_scale
    )
    nblocks, per_block = (queries.shape[0], queries.shape[1])
    pos = first + jnp.arange(nblocks * per_block).reshape(nblocks, 1, per_block, 1)
    key_pos = jnp.arange(length)
    local = jnp.where(key_pos[None, None, None, :] <= pos, local, NEG)
    distant_memory = jnp.where(flag > 0, distant_memory, NEG)
    return (local, distant_memory)


def row_stat(stat, rows):
    return jnp.transpose(stat[..., 0], (0, 2, 1)).reshape(rows, HEADS)


def general_body(
    tokens,
    cotangent,
    memory_keys,
    memory_values,
    memory_choice,
    memory_flag,
    w_query,
    w_key,
    w_value,
    w_out,
    w_gate,
    w_up,
    w_down,
    norm_attn,
    norm_ffn,
):
    segs, rows, width = tokens.shape
    group = lax.axis_size("row")
    seg_count = lax.axis_size("seg")
    length = rows * group
    first = lax.axis_index("row") * rows
    nblocks = max(rows // QBLK, 1)
    per_block = rows // nblocks
    score_scale = HD ** (-0.5)
    shards = (w_query, w_key, w_value, w_out, w_gate, w_up, w_down, norm_attn, norm_ffn)
    wq, wk, wv, wo, wg, wu, wd, gain_one, gain_two = (
        lax.all_gather(shards[0], ("seg", "row"), axis=0, tiled=True),
        lax.all_gather(shards[1], ("seg", "row"), axis=0, tiled=True),
        lax.all_gather(shards[2], ("seg", "row"), axis=0, tiled=True),
        lax.all_gather(shards[3], ("seg", "row"), axis=0, tiled=True),
        lax.all_gather(shards[4], ("seg", "row"), axis=0, tiled=True),
        lax.all_gather(shards[5], ("seg", "row"), axis=0, tiled=True),
        lax.all_gather(shards[6], ("seg", "row"), axis=0, tiled=True),
        lax.all_gather(shards[7], ("seg", "row"), axis=0, tiled=True),
        lax.all_gather(shards[8], ("seg", "row"), axis=0, tiled=True),
    )
    gain_attn = gain_one.astype(jnp.float32)
    gain_ffn = gain_two.astype(jnp.float32)
    x = tokens.reshape(segs * rows, width).astype(jnp.float32)
    normed, inv_one = norm_apply(x, gain_attn)
    a_one = normed.astype(jnp.bfloat16)
    query = plain_dot(a_one, wq).astype(jnp.bfloat16)
    key_local = plain_dot(a_one, wk).astype(jnp.bfloat16).reshape(segs, rows, width)
    value_local = plain_dot(a_one, wv).astype(jnp.bfloat16).reshape(segs, rows, width)
    keys_all, values_all = (
        lax.all_gather(key_local, "row", axis=1, tiled=True),
        lax.all_gather(value_local, "row", axis=1, tiled=True),
    )
    block_first = first // QBLK
    chosen = lax.dynamic_slice_in_dim(memory_choice, block_first, nblocks, axis=1)
    head_col = jnp.arange(HEADS)[None, :, None]
    seg_id = 0
    memory_key_rows = memory_keys[seg_id].reshape(-1, HEADS, HD)[chosen[seg_id], head_col]
    memory_value_rows = memory_values[seg_id].reshape(-1, HEADS, HD)[chosen[seg_id], head_col]
    qseg = query.reshape(nblocks, per_block, HEADS, HD)
    keys = keys_all[seg_id].reshape(length, HEADS, HD)
    vals = values_all[seg_id].reshape(length, HEADS, HD)
    local, distant_memory = score_block(
        qseg, keys, memory_key_rows, memory_flag[seg_id], first, length
    )
    top = jnp.maximum(
        jnp.max(local, axis=-1, keepdims=True), jnp.max(distant_memory, axis=-1, keepdims=True)
    )
    summed = jnp.sum(jnp.exp(local - top), axis=-1, keepdims=True) + jnp.sum(
        jnp.exp(distant_memory - top), axis=-1, keepdims=True
    )
    total = top + jnp.log(summed)
    p_local = jnp.exp(local - total).astype(jnp.bfloat16)
    p_remote = jnp.exp(distant_memory - total).astype(jnp.bfloat16)
    attention_output = jnp.einsum(
        "bhqk,khd->bqhd", p_local, vals, preferred_element_type=jnp.float32
    )
    attention_output = attention_output + jnp.einsum(
        "bhqm,bhmd->bqhd", p_remote, memory_value_rows, preferred_element_type=jnp.float32
    )
    outputs = attention_output.reshape(rows, width)
    mem_keys = [memory_key_rows]
    mem_vals = [memory_value_rows]
    queries = [qseg]
    totals = [total]
    attended = outputs.astype(jnp.bfloat16)
    hidden_in = x + plain_dot(attended, wo)
    normed_two, inv_two = norm_apply(hidden_in, gain_ffn)
    a_two = normed_two.astype(jnp.bfloat16)
    gate = plain_dot(a_two, wg)
    up = plain_dot(a_two, wu)
    act = jax.nn.silu(gate)
    hid = (act * up).astype(jnp.bfloat16)
    layer_out = (hidden_in + plain_dot(hid, wd)).astype(jnp.bfloat16).reshape(segs, rows, width)
    wq, wk, wv, wo, wg, wu, wd, gain_one, gain_two = (
        lax.all_gather(shards[0], ("seg", "row"), axis=0, tiled=True),
        lax.all_gather(shards[1], ("seg", "row"), axis=0, tiled=True),
        lax.all_gather(shards[2], ("seg", "row"), axis=0, tiled=True),
        lax.all_gather(shards[3], ("seg", "row"), axis=0, tiled=True),
        lax.all_gather(shards[4], ("seg", "row"), axis=0, tiled=True),
        lax.all_gather(shards[5], ("seg", "row"), axis=0, tiled=True),
        lax.all_gather(shards[6], ("seg", "row"), axis=0, tiled=True),
        lax.all_gather(shards[7], ("seg", "row"), axis=0, tiled=True),
        lax.all_gather(shards[8], ("seg", "row"), axis=0, tiled=True),
    )
    gain_attn = gain_one.astype(jnp.float32)
    gain_ffn = gain_two.astype(jnp.float32)
    grad_y = cotangent.reshape(segs * rows, width)
    grad_down = dot_left(hid, grad_y)
    d_hid = dot_right(grad_y, wd)
    sig = jax.nn.sigmoid(gate)
    d_gate = (d_hid * up * sig * (1.0 + gate * (1.0 - sig))).astype(jnp.bfloat16)
    d_up = (d_hid * act).astype(jnp.bfloat16)
    grad_gate = dot_left(a_two, d_gate)
    grad_up = dot_left(a_two, d_up)
    d_a_two = dot_right(d_gate, wg) + dot_right(d_up, wu)
    d_norm_two, grad_gain_ffn = norm_back(hidden_in, gain_ffn, inv_two, d_a_two)
    d_hidden = grad_y.astype(jnp.float32) + d_norm_two
    d_proj = d_hidden.astype(jnp.bfloat16)
    grad_out = dot_left(attended, d_proj)
    d_attended = dot_right(d_proj, wo).astype(jnp.bfloat16)
    seg_id = 0
    qseg = queries[seg_id]
    keys = keys_all[seg_id].reshape(length, HEADS, HD)
    vals = values_all[seg_id].reshape(length, HEADS, HD)
    memory_key_rows = mem_keys[seg_id]
    memory_value_rows = mem_vals[seg_id]
    d_out = d_attended.reshape(nblocks, per_block, HEADS, HD)
    local, distant_memory = score_block(
        qseg, keys, memory_key_rows, memory_flag[seg_id], first, length
    )
    p_local = jnp.exp(local - totals[seg_id])
    p_remote = jnp.exp(distant_memory - totals[seg_id])
    dp_local = jnp.einsum("bqhd,khd->bhqk", d_out, vals, preferred_element_type=jnp.float32)
    dp_remote = jnp.einsum(
        "bqhd,bhmd->bhqm", d_out, memory_value_rows, preferred_element_type=jnp.float32
    )
    delta = jnp.sum(p_local * dp_local, axis=-1, keepdims=True) + jnp.sum(
        p_remote * dp_remote, axis=-1, keepdims=True
    )
    ds_local = (p_local * (dp_local - delta)).astype(jnp.bfloat16)
    ds_remote = (p_remote * (dp_remote - delta)).astype(jnp.bfloat16)
    d_query = jnp.einsum("bhqk,khd->bqhd", ds_local, keys, preferred_element_type=jnp.float32)
    d_query = (
        d_query
        + jnp.einsum(
            "bhqm,bhmd->bqhd", ds_remote, memory_key_rows, preferred_element_type=jnp.float32
        )
    ) * score_scale
    d_queries = d_query.astype(jnp.bfloat16).reshape(rows, width)
    lse_rows = [row_stat(totals[seg_id], rows)]
    delta_rows = [row_stat(delta, rows)]
    query_seg = query.reshape(segs, rows, width)
    dout_seg = d_attended.reshape(segs, rows, width)
    query_full, dout_full = (
        lax.all_gather(query_seg, "row", axis=1, tiled=True),
        lax.all_gather(dout_seg, "row", axis=1, tiled=True),
    )
    lse_full, delta_full = (
        lax.all_gather(jnp.stack(lse_rows, axis=0), "row", axis=1, tiled=True),
        lax.all_gather(jnp.stack(delta_rows, axis=0), "row", axis=1, tiled=True),
    )
    query_pos = jnp.arange(length)
    own_pos = first + jnp.arange(rows)
    visible = own_pos[None, None, :] <= query_pos[None, :, None]
    seg_id = 0
    q_whole = query_full[seg_id].reshape(length, HEADS, HD)
    o_whole = dout_full[seg_id].reshape(length, HEADS, HD)
    own_keys = key_local[seg_id].reshape(rows, HEADS, HD)
    own_vals = value_local[seg_id].reshape(rows, HEADS, HD)
    scores = (
        jnp.einsum("qhd,khd->hqk", q_whole, own_keys, preferred_element_type=jnp.float32)
        * score_scale
    )
    scores = jnp.where(visible, scores, NEG)
    softmax_weights = jnp.exp(scores - jnp.transpose(lse_full[seg_id])[:, :, None])
    d_probs = jnp.einsum("qhd,khd->hqk", o_whole, own_vals, preferred_element_type=jnp.float32)
    d_scores = (softmax_weights * (d_probs - jnp.transpose(delta_full[seg_id])[:, :, None])).astype(
        jnp.bfloat16
    )
    d_key = (
        jnp.einsum("hqk,qhd->khd", d_scores, q_whole, preferred_element_type=jnp.float32)
        * score_scale
    )
    d_val = jnp.einsum(
        "hqk,qhd->khd",
        softmax_weights.astype(jnp.bfloat16),
        o_whole,
        preferred_element_type=jnp.float32,
    )
    key_parts = d_key.reshape(rows, width)
    value_parts = d_val.reshape(rows, width)
    d_key_all = key_parts.astype(jnp.bfloat16)
    d_value_all = value_parts.astype(jnp.bfloat16)
    grad_query = dot_left(a_one, d_queries)
    grad_key = dot_left(a_one, d_key_all)
    grad_value = dot_left(a_one, d_value_all)
    d_a_one = dot_right(d_queries, wq) + dot_right(d_key_all, wk) + dot_right(d_value_all, wv)
    d_norm_one, grad_gain_attn = norm_back(x, gain_attn, inv_one, d_a_one)
    grad_tokens = (d_hidden + d_norm_one).astype(jnp.bfloat16).reshape(segs, rows, width)
    full_grads = (
        grad_query,
        grad_key,
        grad_value,
        grad_out,
        grad_gate,
        grad_up,
        grad_down,
        grad_gain_attn,
        grad_gain_ffn,
    )
    split_grads = tuple((g.reshape(seg_count, group, -1) for g in full_grads))
    row_summed = jax.tree.map(
        lambda part: part.astype(jnp.float32),
        lax.psum_scatter(for_sending(split_grads), "row", scatter_dimension=1, tiled=True),
    )
    owned_flat = jax.tree.map(
        lambda part: part.astype(jnp.float32),
        lax.psum_scatter(for_sending(row_summed), "seg", scatter_dimension=0, tiled=True),
    )
    owned = []
    for whole_grad, piece in zip(full_grads, owned_flat):
        own_rows = whole_grad.shape[0] // (seg_count * group)
        owned.append(piece.reshape((own_rows,) + whole_grad.shape[1:]))
    return (
        layer_out,
        grad_tokens,
        owned[0],
        owned[1],
        owned[2],
        owned[3],
        owned[4],
        owned[5],
        owned[6],
        owned[7],
        owned[8],
    )


MESH = pl.DeviceIdType.MESH
BF = jnp.bfloat16
F32 = jnp.float32


def place():
    seg = lax.axis_index("seg")
    row = lax.axis_index("row")
    return seg // 4, (seg // 2) % 2, seg % 2, row


def device(z, y, c, x):
    return ((z * 2 + y) * 2 + c, x)


def greet(barrier):
    z, y, c, x = place()
    for d in range(1, 4):
        pl.semaphore_signal(barrier, inc=1, device_id=device((z + d) % 4, y, c, x), device_id_type=MESH)
    pl.semaphore_signal(barrier, inc=1, device_id=device(z, 1 - y, c, x), device_id_type=MESH)
    pl.semaphore_signal(barrier, inc=1, device_id=device(z, y, 1 - c, x), device_id_type=MESH)
    pl.semaphore_signal(barrier, inc=1, device_id=device(z, y, c, 1 - x), device_id_type=MESH)
    pl.semaphore_wait(barrier, 6)


def remote(src, dst, send, recv, where):
    return pltpu.make_async_remote_copy(
        src_ref=src, dst_ref=dst, send_sem=send, recv_sem=recv, device_id=where, device_id_type=MESH
    )


def gather_kernel(
    tok, cot, keep_a, send_a, keep_b, send_b, down,
    out_tok, out_cot, wa, wb, wc,
    own_sem, sx, rx, sz, rz, sy, ry, sc, rc,
):
    z, y, c, x = place()
    seg = (z * 2 + y) * 2 + c
    greet(pltpu.get_barrier_semaphore())
    over_x, over_y, over_c = device(z, y, c, 1 - x), device(z, 1 - y, c, x), device(z, y, 1 - c, x)
    groups = [(keep_a, send_a, wa), (keep_b, send_b, wb)]
    first, local = [], []
    for g, (keep, send, w) in enumerate(groups):
        first.append(remote(send, w.at[seg, x], sx.at[g], rx.at[g], over_x))
        local.append(pltpu.make_async_copy(keep, w.at[seg, x], own_sem.at[g]))
    first.append(remote(tok, out_tok, sx.at[3], rx.at[3], over_x))
    first.append(remote(cot, out_cot, sx.at[4], rx.at[4], over_x))
    for cp in first:
        cp.start()
    for cp in local:
        cp.start()
    chip = z * 2 + y
    last = remote(down, wc.at[chip, x], sx.at[2], rx.at[2], over_x)
    lastl = pltpu.make_async_copy(down, wc.at[chip, x], own_sem.at[2])
    mine = x == c

    @pl.when(mine)
    def _():
        lastl.start()

    @pl.when(jnp.logical_not(mine))
    def _():
        last.start()

    def block(g, zz, yy):
        if g == 2:
            return wc.at[zz * 2 + yy]
        return groups[g][2].at[(zz * 2 + yy) * 2 + c]

    def to_z(g, d):
        b = block(g, z, y)
        return remote(b, b, sz.at[g, d - 1], rz.at[g, d - 1], device((z + d) % 4, y, c, x))

    def to_y(g, d):
        b = block(g, (z + 4 - d) % 4, y)
        return remote(b, b, sy.at[g, d], ry.at[g, d], over_y)

    def to_c(g, d, f):
        b = block(g, (z + 4 - d) % 4, (y + f) % 2)
        return remote(b, b, sc.at[g, d, f], rc.at[g, d, f], over_c)

    def spread(g):
        for d in range(1, 4):
            to_z(g, d).start()
        to_y(g, 0).start()
        to_c(g, 0, 0).start()

    def pass_z(g, d):
        to_z(g, d).wait_recv()
        to_y(g, d).start()
        to_c(g, d, 0).start()

    def pass_y(g, d):
        to_y(g, d).wait_recv()
        to_c(g, d, 1).start()

    def end_send(g):
        for d in range(1, 4):
            to_z(g, d).wait_send()
        for d in range(4):
            to_y(g, d).wait_send()
            for f in range(2):
                to_c(g, d, f).wait_send()

    def end_recv(g):
        for d in range(4):
            for f in range(2):
                to_c(g, d, f).wait_recv()

    for g in range(2):
        first[g].wait_recv()
        local[g].wait()
        spread(g)

    @pl.when(mine)
    def _():
        last.wait_recv()
        lastl.wait()
        spread(2)

    for g in range(2):
        for d in range(1, 4):
            pass_z(g, d)

    @pl.when(mine)
    def _():
        for d in range(1, 4):
            pass_z(2, d)

    for g in range(2):
        for d in range(4):
            pass_y(g, d)

    @pl.when(mine)
    def _():
        for d in range(4):
            pass_y(2, d)
        end_send(2)

    @pl.when(jnp.logical_not(mine))
    def _():
        last.wait_send()
        end_recv(2)

    for g in range(2):
        end_recv(g)
    for g in range(2):
        end_send(g)
    for cp in first:
        cp.wait_send()
    first[2].wait_recv()
    first[3].wait_recv()


def gather(tok, cot, keep_a, send_a, keep_b, send_b, down):
    na, nb = keep_a.shape[1], keep_b.shape[1]
    hbm = pl.BlockSpec(memory_space=pl.ANY)
    dma = pltpu.SemaphoreType.DMA
    return pl.pallas_call(
        gather_kernel,
        name="gather_weights",
        out_shape=(
            jax.ShapeDtypeStruct(tok.shape, BF),
            jax.ShapeDtypeStruct(cot.shape, BF),
            jax.ShapeDtypeStruct((16, 2, 32, na), BF),
            jax.ShapeDtypeStruct((16, 2, 32, nb), BF),
            jax.ShapeDtypeStruct((8, 2, 88, 1024), BF),
        ),
        in_specs=[hbm] * 7,
        out_specs=(hbm,) * 5,
        scratch_shapes=[
            dma((3,)), dma((5,)), dma((5,)), dma((3, 3)), dma((3, 3)), dma((3, 4)), dma((3, 4)),
            dma((3, 4, 2)), dma((3, 4, 2)),
        ],
        compiler_params=pltpu.CompilerParams(collective_id=0, has_side_effects=True),
    )(tok, cot, keep_a, send_a, keep_b, send_b, down)


def scatter_kernel(
    ga, gb, gc,
    keep_a, got_a, keep_b, got_b, keep_c,
    ca, cb, cc, ya, yb, yc, za, zb, zc, xa, xb, xc, hold_a, hold_b, hold_c,
    sx, rx, sz, rz, sy, ry, sc, rc,
):
    z, y, c, x = place()
    greet(pltpu.get_barrier_semaphore())
    over_x, over_y, over_c = device(z, y, c, 1 - x), device(z, 1 - y, c, x), device(z, y, 1 - c, x)
    mine = x == c
    other = jnp.logical_not(mine)
    to_c = [
        remote(ga.at[:, :, 1 - c], ca, sc.at[0], rc.at[0], over_c),
        remote(gb.at[:, :, 1 - c], cb, sc.at[1], rc.at[1], over_c),
        remote(gc, cc, sc.at[2], rc.at[2], over_c),
    ]
    csum, ysum, zbuf = [ca, cb, cc], [ya, yb, yc], [za, zb, zc]

    def to_y(g):
        return remote(csum[g].at[:, 1 - y], ysum[g], sy.at[g], ry.at[g], over_y)

    def to_z(g, d):
        return remote(
            ysum[g].at[(z + d) % 4], zbuf[g].at[d - 1], sz.at[g, d - 1], rz.at[g, d - 1],
            device((z + d) % 4, y, c, x),
        )

    to_c[0].start()
    to_c[1].start()

    @pl.when(other)
    def _():
        to_c[2].start()

    def sum_c(g):
        to_c[g].wait_recv()
        src = [ga, gb, gc][g]

        @pl.loop(0, 8)
        def _(i):
            a = src[i // 2, i % 2, c] if g < 2 else src[i // 2, i % 2]
            csum[g][i // 2, i % 2] = (csum[g][i // 2, i % 2].astype(F32) + a.astype(F32)).astype(BF)

        to_y(g).start()

    def sum_y(g):
        to_y(g).wait_recv()

        @pl.loop(0, 4)
        def _(i):
            ysum[g][i] = (ysum[g][i].astype(F32) + csum[g][i, y].astype(F32)).astype(BF)

        for d in range(1, 4):
            to_z(g, d).start()

    def sum_z(g, hold):
        for d in range(1, 4):
            to_z(g, d).wait_recv()
        hold[...] = (
            ysum[g][z].astype(F32) + zbuf[g][0].astype(F32) + zbuf[g][1].astype(F32) + zbuf[g][2].astype(F32)
        )

    holds, xbufs, keeps = [hold_a, hold_b, hold_c], [xa, xb, xc], [keep_a, keep_b, keep_c]
    gots = [got_a, got_b, keep_c]

    def to_x(g):
        return remote(xbufs[g].at[0], xbufs[g].at[1], sx.at[g], rx.at[g], over_x)

    def send_x(g):
        n = 88 if g == 2 else 32
        xbufs[g][0] = holds[g][1 - x].astype(BF)
        to_x(g).start()
        keeps[g][...] = holds[g][x]

    sum_c(0)
    sum_c(1)
    pl.when(mine)(lambda: sum_c(2))
    sum_y(0)
    sum_y(1)
    pl.when(mine)(lambda: sum_y(2))
    for g in range(2):
        sum_z(g, holds[g])
        send_x(g)

    @pl.when(mine)
    def _():
        sum_z(2, hold_c)
        send_x(2)

    for g in range(2):
        to_x(g).wait_recv()
        gots[g][...] = xbufs[g][1].astype(F32)

    @pl.when(other)
    def _():
        to_x(2).wait_recv()
        keep_c[...] = xbufs[2][1].astype(F32)
        to_c[2].wait_send()

    def done(g):
        to_x(g).wait_send()
        to_y(g).wait_send()
        for d in range(1, 4):
            to_z(g, d).wait_send()

    for g in range(2):
        to_c[g].wait_send()
        done(g)
    pl.when(mine)(lambda: done(2))


def scatter(ga, gb, gc):
    na, nb = ga.shape[-1], gb.shape[-1]
    vm = pl.BlockSpec(memory_space=pltpu.VMEM)
    dma = pltpu.SemaphoreType.DMA
    shapes = [(2, 32, na), (2, 32, nb), (2, 88, 1024)]
    V = pltpu.VMEM
    return pl.pallas_call(
        scatter_kernel,
        name="scatter_grads",
        out_shape=(
            jax.ShapeDtypeStruct((32, na), F32),
            jax.ShapeDtypeStruct((32, na), F32),
            jax.ShapeDtypeStruct((32, nb), F32),
            jax.ShapeDtypeStruct((32, nb), F32),
            jax.ShapeDtypeStruct((88, 1024), F32),
        ),
        in_specs=[vm] * 3,
        out_specs=(vm,) * 5,
        scratch_shapes=[V((4, 2) + s, BF) for s in shapes]
        + [V((4,) + s, BF) for s in shapes]
        + [V((3,) + s, BF) for s in shapes]
        + [V(s, BF) for s in shapes]
        + [V(s, F32) for s in shapes]
        + [
            dma((3,)), dma((3,)), dma((3, 3)), dma((3, 3)), dma((3,)), dma((3,)), dma((3,)), dma((3,)),
        ],
        compiler_params=pltpu.CompilerParams(collective_id=1, has_side_effects=True, vmem_limit_bytes=60 << 20),
    )(ga, gb, gc)


def half(array, r, width):
    return lax.dynamic_slice_in_dim(array, r * width, width, axis=1)


def swap_rows(array):
    n = array.shape[0] // 2
    return jnp.concatenate([array[n:], array[:n]], axis=0)


def fast_body(
    tokens, cotangent, memory_keys, memory_values, memory_choice, memory_flag,
    w_query, w_key, w_value, w_out, w_gate, w_up, w_down, norm_attn, norm_ffn,
):
    _, rows, width = tokens.shape
    length = 2 * rows
    r = lax.axis_index("row")
    heads, cols, hidden = HEADS // 2, width // 2, w_gate.shape[1] // 2
    strip = w_down.shape[0] * 2
    own_rows = w_query.shape[0]
    scale = HD ** (-0.5)

    def strips(w, k):
        return lax.dynamic_index_in_dim(w.reshape(own_rows, -1, 2, strip), k, 2, False).reshape(own_rows, hidden)

    gains = jnp.zeros((own_rows, 128), BF).at[:, 0].set(norm_attn).at[:, 1].set(norm_ffn)

    def pack_a(k):
        return jnp.concatenate([half(w_query, k, cols), half(w_key, k, cols), half(w_value, k, cols), w_out, gains], axis=1)

    def pack_b(k):
        return jnp.concatenate([strips(w_gate, k), strips(w_up, k)], axis=1)

    tok_peer, cot_peer, wa, wb, wc = gather(
        tokens[0], cotangent[0], pack_a(r), pack_a(1 - r), pack_b(r), pack_b(1 - r), w_down
    )
    wa = wa.reshape(width, -1)
    wb = wb.reshape(width, -1)
    wd = wc.reshape(hidden, width)
    wq, wk, wv, wo = wa[:, :cols], wa[:, cols : 2 * cols], wa[:, 2 * cols : 3 * cols], wa[:, 3 * cols : 3 * cols + width]
    gain_attn = wa[:, 3 * cols + width].astype(F32)
    gain_ffn = wa[:, 3 * cols + width + 1].astype(F32)
    wg, wu = wb[:, :hidden], wb[:, hidden:]
    x = jnp.concatenate([tokens[0], tok_peer], axis=0).astype(F32)
    dy = jnp.concatenate([cotangent[0], cot_peer], axis=0)
    pos = jnp.concatenate([r * rows + jnp.arange(rows), (1 - r) * rows + jnp.arange(rows)])
    normed, inv_one = norm_apply(x, gain_attn)
    a_one = normed.astype(BF)
    q = plain_dot(a_one, wq).astype(BF).reshape(length, heads, HD)
    k = plain_dot(a_one, wk).astype(BF).reshape(length, heads, HD)
    v = plain_dot(a_one, wv).astype(BF).reshape(length, heads, HD)
    choice = lax.dynamic_slice_in_dim(memory_choice[0, 0], r * heads, heads, axis=0)
    hot = (choice[:, :, None] == jnp.arange(memory_keys.shape[1])[None, None, :]).astype(BF)
    mem_k = lax.dynamic_slice_in_dim(memory_keys[0], r * cols, cols, axis=1).reshape(-1, heads, HD)
    mem_v = lax.dynamic_slice_in_dim(memory_values[0], r * cols, cols, axis=1).reshape(-1, heads, HD)
    mk = jnp.einsum("hms,shd->mhd", hot, mem_k, preferred_element_type=F32).astype(BF)
    mv = jnp.einsum("hms,shd->mhd", hot, mem_v, preferred_element_type=F32).astype(BF)
    keys = jnp.concatenate([k, mk], axis=0)
    vals = jnp.concatenate([v, mv], axis=0)
    mem = mk.shape[0]
    seen = jnp.concatenate(
        [pos[None, :] <= pos[:, None], jnp.broadcast_to(memory_flag[0] > 0, (length, mem))], axis=1
    )
    scores = jnp.einsum("qhd,khd->hqk", q, keys, preferred_element_type=F32) * scale
    scores = jnp.where(seen[None], scores, NEG)
    top = jnp.max(scores, axis=-1, keepdims=True)
    weight = jnp.exp(scores - top)
    p = weight / jnp.sum(weight, axis=-1, keepdims=True)
    pr = p.astype(BF)
    ao = jnp.einsum("hqk,khd->qhd", pr, vals, preferred_element_type=F32).astype(BF).reshape(length, cols)
    across = [((s * 2 + t), (s * 2 + 1 - t)) for s in range(16) for t in range(2)]

    def swap(array):
        return lax.ppermute(array, ("seg", "row"), across)

    ao_peer = swap_rows(swap(ao))
    ao_full = jnp.where(r == 0, jnp.concatenate([ao, ao_peer], axis=1), jnp.concatenate([ao_peer, ao], axis=1))
    h = x + plain_dot(ao_full, wo)
    normed_two, inv_two = norm_apply(h, gain_ffn)
    a_two = normed_two.astype(BF)
    gate = plain_dot(a_two, wg)
    up = plain_dot(a_two, wu)
    sig = jax.nn.sigmoid(gate)
    act = gate * sig
    hid = (act * up).astype(BF)
    y_part = plain_dot(hid, wd)
    layer_out = (h[:rows] + y_part[:rows] + swap(y_part[rows:].astype(BF)).astype(F32)).astype(BF)
    grad_down = dot_left(hid, dy)
    d_hid = dot_right(dy, wd)
    d_gate = (d_hid * up * sig * (1.0 + gate * (1.0 - sig))).astype(BF)
    d_up = (d_hid * act).astype(BF)
    grad_gate = dot_left(a_two, d_gate)
    grad_up = dot_left(a_two, d_up)
    da_part = dot_right(d_gate, wg) + dot_right(d_up, wu)
    d_a_two = da_part + swap_rows(swap(da_part.astype(BF))).astype(F32)
    d_norm_two, _ = norm_back(h, gain_ffn, inv_two, d_a_two)
    grad_gain_ffn = jnp.sum(d_a_two[:rows] * (h * inv_two)[:rows], axis=0)
    d_hidden = dy.astype(F32) + d_norm_two
    d_proj = d_hidden.astype(BF)
    grad_out = dot_left(ao_full, half(d_proj, r, cols))
    d_att = dot_right(d_proj, lax.dynamic_slice_in_dim(wo, r * cols, cols, axis=0)).astype(BF)
    d_att = d_att.reshape(length, heads, HD)
    dp = jnp.einsum("qhd,khd->hqk", d_att, vals, preferred_element_type=F32)
    delta = jnp.sum(p * dp, axis=-1, keepdims=True)
    ds = (p * (dp - delta)).astype(BF)
    dq = (jnp.einsum("hqk,khd->qhd", ds, keys, preferred_element_type=F32) * scale).astype(BF).reshape(length, cols)
    dk = (jnp.einsum("hqk,qhd->khd", ds[:, :, :length], q, preferred_element_type=F32) * scale).astype(BF)
    dv = jnp.einsum("hqk,qhd->khd", pr[:, :, :length], d_att, preferred_element_type=F32).astype(BF)
    dk, dv = dk.reshape(length, cols), dv.reshape(length, cols)
    grad_query, grad_key, grad_value = dot_left(a_one, dq), dot_left(a_one, dk), dot_left(a_one, dv)
    d1_part = dot_right(dq, wq) + dot_right(dk, wk) + dot_right(dv, wv)
    d_a_one = d1_part[:rows] + swap(d1_part[rows:].astype(BF)).astype(F32)
    d_norm_one, grad_gain_attn = norm_back(x[:rows], gain_attn, inv_one[:rows], d_a_one)
    grad_tokens = (d_hidden[:rows] + d_norm_one).astype(BF)
    gain_grads = jnp.zeros((width, 128), F32).at[:, 0].set(grad_gain_attn).at[:, 1].set(grad_gain_ffn)
    ga = jnp.concatenate([grad_query, grad_key, grad_value, grad_out, gain_grads], axis=1).astype(BF)
    gb = jnp.concatenate([grad_gate, grad_up], axis=1).astype(BF)
    keep_a, got_a, keep_b, got_b, own_c = scatter(
        ga.reshape(4, 2, 2, 2, own_rows, -1),
        gb.reshape(4, 2, 2, 2, own_rows, -1),
        grad_down.astype(BF).reshape(4, 2, 2, -1, width),
    )
    low_a, high_a = jnp.where(r == 0, keep_a, got_a), jnp.where(r == 0, got_a, keep_a)
    low_b, high_b = jnp.where(r == 0, keep_b, got_b), jnp.where(r == 0, got_b, keep_b)

    def join(i):
        return jnp.concatenate([low_a[:, i * cols : (i + 1) * cols], high_a[:, i * cols : (i + 1) * cols]], axis=1)

    def weave(i):
        lo = low_b[:, i * hidden : (i + 1) * hidden].reshape(own_rows, -1, 1, strip)
        hi = high_b[:, i * hidden : (i + 1) * hidden].reshape(own_rows, -1, 1, strip)
        return jnp.concatenate([lo, hi], axis=2).reshape(own_rows, -1)

    gain_total = keep_a[:, 4 * cols :] + got_a[:, 4 * cols :]
    return (
        layer_out[None],
        grad_tokens[None],
        join(0),
        join(1),
        join(2),
        join(3),
        weave(0),
        weave(1),
        own_c,
        gain_total[:, 0],
        gain_total[:, 1],
    )


def solution(mesh):
    in_specs = (
        P("seg", "row", None),
        P("seg", "row", None),
        P("seg", None, None),
        P("seg", None, None),
        P("seg", None, None, None),
        P("seg"),
        P(("seg", "row"), None),
        P(("seg", "row"), None),
        P(("seg", "row"), None),
        P(("seg", "row"), None),
        P(("seg", "row"), None),
        P(("seg", "row"), None),
        P(("seg", "row"), None),
        P(("seg", "row")),
        P(("seg", "row")),
    )
    out_specs = (
        P("seg", "row", None),
        P("seg", "row", None),
        P(("seg", "row"), None),
        P(("seg", "row"), None),
        P(("seg", "row"), None),
        P(("seg", "row"), None),
        P(("seg", "row"), None),
        P(("seg", "row"), None),
        P(("seg", "row"), None),
        P(("seg", "row")),
        P(("seg", "row")),
    )

    def body(*args):
        segs, rows, width = args[0].shape
        fits = (
            mesh.shape["row"] == 2
            and mesh.shape["seg"] == 16
            and segs == 1
            and (rows, width) == (256, 1024)
            and args[4].shape[1] == 1
        )
        return (fast_body if fits else general_body)(*args)

    return jax.shard_map(body, mesh=mesh, in_specs=in_specs, out_specs=out_specs, check_vma=False)
```

```python
import functools

import jax
import jax.numpy as jnp
from jax import lax
from jax.experimental import pallas as pl
from jax.experimental.pallas import tpu as pltpu
from jax.sharding import PartitionSpec as P

HEADS = 8
HD = 128
QBLK = 512


EPS = 1e-06
NEG = -1000000000.0


def for_sending(array):

    def short(part):
        return part.astype(jnp.bfloat16) if part.dtype == jnp.float32 else part

    return jax.tree.map(short, array)


def plain_dot(left, right):
    return jnp.dot(left, right, preferred_element_type=jnp.float32)


def dot_left(left, right):
    return lax.dot_general(
        left, right, (((0,), (0,)), ((), ())), preferred_element_type=jnp.float32
    )


def dot_right(left, right):
    return lax.dot_general(
        left, right, (((1,), (1,)), ((), ())), preferred_element_type=jnp.float32
    )


def norm_apply(value, gain):
    inverse = lax.rsqrt(jnp.mean(value * value, axis=-1, keepdims=True) + EPS)
    return (value * inverse * gain, inverse)


def norm_back(value, gain, inverse, grad):
    unit = value * inverse
    gain_grad = jnp.sum(grad * unit, axis=0)
    scaled = grad * gain
    return (inverse * (scaled - unit * jnp.mean(scaled * unit, axis=-1, keepdims=True)), gain_grad)


def score_block(queries, keys, memory_key_rows, flag, first, length):
    score_scale = HD ** (-0.5)
    local = (
        jnp.einsum("bqhd,khd->bhqk", queries, keys, preferred_element_type=jnp.float32)
        * score_scale
    )
    distant_memory = (
        jnp.einsum("bqhd,bhmd->bhqm", queries, memory_key_rows, preferred_element_type=jnp.float32)
        * score_scale
    )
    nblocks, per_block = (queries.shape[0], queries.shape[1])
    pos = first + jnp.arange(nblocks * per_block).reshape(nblocks, 1, per_block, 1)
    key_pos = jnp.arange(length)
    local = jnp.where(key_pos[None, None, None, :] <= pos, local, NEG)
    distant_memory = jnp.where(flag > 0, distant_memory, NEG)
    return (local, distant_memory)


def row_stat(stat, rows):
    return jnp.transpose(stat[..., 0], (0, 2, 1)).reshape(rows, HEADS)


def general_body(
    tokens,
    cotangent,
    memory_keys,
    memory_values,
    memory_choice,
    memory_flag,
    w_query,
    w_key,
    w_value,
    w_out,
    w_gate,
    w_up,
    w_down,
    norm_attn,
    norm_ffn,
):
    segs, rows, width = tokens.shape
    group = lax.axis_size("row")
    seg_count = lax.axis_size("seg")
    length = rows * group
    first = lax.axis_index("row") * rows
    nblocks = max(rows // QBLK, 1)
    per_block = rows // nblocks
    score_scale = HD ** (-0.5)
    shards = (w_query, w_key, w_value, w_out, w_gate, w_up, w_down, norm_attn, norm_ffn)
    wq, wk, wv, wo, wg, wu, wd, gain_one, gain_two = (
        lax.all_gather(shards[0], ("seg", "row"), axis=0, tiled=True),
        lax.all_gather(shards[1], ("seg", "row"), axis=0, tiled=True),
        lax.all_gather(shards[2], ("seg", "row"), axis=0, tiled=True),
        lax.all_gather(shards[3], ("seg", "row"), axis=0, tiled=True),
        lax.all_gather(shards[4], ("seg", "row"), axis=0, tiled=True),
        lax.all_gather(shards[5], ("seg", "row"), axis=0, tiled=True),
        lax.all_gather(shards[6], ("seg", "row"), axis=0, tiled=True),
        lax.all_gather(shards[7], ("seg", "row"), axis=0, tiled=True),
        lax.all_gather(shards[8], ("seg", "row"), axis=0, tiled=True),
    )
    gain_attn = gain_one.astype(jnp.float32)
    gain_ffn = gain_two.astype(jnp.float32)
    x = tokens.reshape(segs * rows, width).astype(jnp.float32)
    normed, inv_one = norm_apply(x, gain_attn)
    a_one = normed.astype(jnp.bfloat16)
    query = plain_dot(a_one, wq).astype(jnp.bfloat16)
    key_local = plain_dot(a_one, wk).astype(jnp.bfloat16).reshape(segs, rows, width)
    value_local = plain_dot(a_one, wv).astype(jnp.bfloat16).reshape(segs, rows, width)
    keys_all, values_all = (
        lax.all_gather(key_local, "row", axis=1, tiled=True),
        lax.all_gather(value_local, "row", axis=1, tiled=True),
    )
    block_first = first // QBLK
    chosen = lax.dynamic_slice_in_dim(memory_choice, block_first, nblocks, axis=1)
    head_col = jnp.arange(HEADS)[None, :, None]
    seg_id = 0
    memory_key_rows = memory_keys[seg_id].reshape(-1, HEADS, HD)[chosen[seg_id], head_col]
    memory_value_rows = memory_values[seg_id].reshape(-1, HEADS, HD)[chosen[seg_id], head_col]
    qseg = query.reshape(nblocks, per_block, HEADS, HD)
    keys = keys_all[seg_id].reshape(length, HEADS, HD)
    vals = values_all[seg_id].reshape(length, HEADS, HD)
    local, distant_memory = score_block(
        qseg, keys, memory_key_rows, memory_flag[seg_id], first, length
    )
    top = jnp.maximum(
        jnp.max(local, axis=-1, keepdims=True), jnp.max(distant_memory, axis=-1, keepdims=True)
    )
    summed = jnp.sum(jnp.exp(local - top), axis=-1, keepdims=True) + jnp.sum(
        jnp.exp(distant_memory - top), axis=-1, keepdims=True
    )
    total = top + jnp.log(summed)
    p_local = jnp.exp(local - total).astype(jnp.bfloat16)
    p_remote = jnp.exp(distant_memory - total).astype(jnp.bfloat16)
    attention_output = jnp.einsum(
        "bhqk,khd->bqhd", p_local, vals, preferred_element_type=jnp.float32
    )
    attention_output = attention_output + jnp.einsum(
        "bhqm,bhmd->bqhd", p_remote, memory_value_rows, preferred_element_type=jnp.float32
    )
    outputs = attention_output.reshape(rows, width)
    mem_keys = [memory_key_rows]
    mem_vals = [memory_value_rows]
    queries = [qseg]
    totals = [total]
    attended = outputs.astype(jnp.bfloat16)
    hidden_in = x + plain_dot(attended, wo)
    normed_two, inv_two = norm_apply(hidden_in, gain_ffn)
    a_two = normed_two.astype(jnp.bfloat16)
    gate = plain_dot(a_two, wg)
    up = plain_dot(a_two, wu)
    act = jax.nn.silu(gate)
    hid = (act * up).astype(jnp.bfloat16)
    layer_out = (hidden_in + plain_dot(hid, wd)).astype(jnp.bfloat16).reshape(segs, rows, width)
    wq, wk, wv, wo, wg, wu, wd, gain_one, gain_two = (
        lax.all_gather(shards[0], ("seg", "row"), axis=0, tiled=True),
        lax.all_gather(shards[1], ("seg", "row"), axis=0, tiled=True),
        lax.all_gather(shards[2], ("seg", "row"), axis=0, tiled=True),
        lax.all_gather(shards[3], ("seg", "row"), axis=0, tiled=True),
        lax.all_gather(shards[4], ("seg", "row"), axis=0, tiled=True),
        lax.all_gather(shards[5], ("seg", "row"), axis=0, tiled=True),
        lax.all_gather(shards[6], ("seg", "row"), axis=0, tiled=True),
        lax.all_gather(shards[7], ("seg", "row"), axis=0, tiled=True),
        lax.all_gather(shards[8], ("seg", "row"), axis=0, tiled=True),
    )
    gain_attn = gain_one.astype(jnp.float32)
    gain_ffn = gain_two.astype(jnp.float32)
    grad_y = cotangent.reshape(segs * rows, width)
    grad_down = dot_left(hid, grad_y)
    d_hid = dot_right(grad_y, wd)
    sig = jax.nn.sigmoid(gate)
    d_gate = (d_hid * up * sig * (1.0 + gate * (1.0 - sig))).astype(jnp.bfloat16)
    d_up = (d_hid * act).astype(jnp.bfloat16)
    grad_gate = dot_left(a_two, d_gate)
    grad_up = dot_left(a_two, d_up)
    d_a_two = dot_right(d_gate, wg) + dot_right(d_up, wu)
    d_norm_two, grad_gain_ffn = norm_back(hidden_in, gain_ffn, inv_two, d_a_two)
    d_hidden = grad_y.astype(jnp.float32) + d_norm_two
    d_proj = d_hidden.astype(jnp.bfloat16)
    grad_out = dot_left(attended, d_proj)
    d_attended = dot_right(d_proj, wo).astype(jnp.bfloat16)
    seg_id = 0
    qseg = queries[seg_id]
    keys = keys_all[seg_id].reshape(length, HEADS, HD)
    vals = values_all[seg_id].reshape(length, HEADS, HD)
    memory_key_rows = mem_keys[seg_id]
    memory_value_rows = mem_vals[seg_id]
    d_out = d_attended.reshape(nblocks, per_block, HEADS, HD)
    local, distant_memory = score_block(
        qseg, keys, memory_key_rows, memory_flag[seg_id], first, length
    )
    p_local = jnp.exp(local - totals[seg_id])
    p_remote = jnp.exp(distant_memory - totals[seg_id])
    dp_local = jnp.einsum("bqhd,khd->bhqk", d_out, vals, preferred_element_type=jnp.float32)
    dp_remote = jnp.einsum(
        "bqhd,bhmd->bhqm", d_out, memory_value_rows, preferred_element_type=jnp.float32
    )
    delta = jnp.sum(p_local * dp_local, axis=-1, keepdims=True) + jnp.sum(
        p_remote * dp_remote, axis=-1, keepdims=True
    )
    ds_local = (p_local * (dp_local - delta)).astype(jnp.bfloat16)
    ds_remote = (p_remote * (dp_remote - delta)).astype(jnp.bfloat16)
    d_query = jnp.einsum("bhqk,khd->bqhd", ds_local, keys, preferred_element_type=jnp.float32)
    d_query = (
        d_query
        + jnp.einsum(
            "bhqm,bhmd->bqhd", ds_remote, memory_key_rows, preferred_element_type=jnp.float32
        )
    ) * score_scale
    d_queries = d_query.astype(jnp.bfloat16).reshape(rows, width)
    lse_rows = [row_stat(totals[seg_id], rows)]
    delta_rows = [row_stat(delta, rows)]
    query_seg = query.reshape(segs, rows, width)
    dout_seg = d_attended.reshape(segs, rows, width)
    query_full, dout_full = (
        lax.all_gather(query_seg, "row", axis=1, tiled=True),
        lax.all_gather(dout_seg, "row", axis=1, tiled=True),
    )
    lse_full, delta_full = (
        lax.all_gather(jnp.stack(lse_rows, axis=0), "row", axis=1, tiled=True),
        lax.all_gather(jnp.stack(delta_rows, axis=0), "row", axis=1, tiled=True),
    )
    query_pos = jnp.arange(length)
    own_pos = first + jnp.arange(rows)
    visible = own_pos[None, None, :] <= query_pos[None, :, None]
    seg_id = 0
    q_whole = query_full[seg_id].reshape(length, HEADS, HD)
    o_whole = dout_full[seg_id].reshape(length, HEADS, HD)
    own_keys = key_local[seg_id].reshape(rows, HEADS, HD)
    own_vals = value_local[seg_id].reshape(rows, HEADS, HD)
    scores = (
        jnp.einsum("qhd,khd->hqk", q_whole, own_keys, preferred_element_type=jnp.float32)
        * score_scale
    )
    scores = jnp.where(visible, scores, NEG)
    softmax_weights = jnp.exp(scores - jnp.transpose(lse_full[seg_id])[:, :, None])
    d_probs = jnp.einsum("qhd,khd->hqk", o_whole, own_vals, preferred_element_type=jnp.float32)
    d_scores = (softmax_weights * (d_probs - jnp.transpose(delta_full[seg_id])[:, :, None])).astype(
        jnp.bfloat16
    )
    d_key = (
        jnp.einsum("hqk,qhd->khd", d_scores, q_whole, preferred_element_type=jnp.float32)
        * score_scale
    )
    d_val = jnp.einsum(
        "hqk,qhd->khd",
        softmax_weights.astype(jnp.bfloat16),
        o_whole,
        preferred_element_type=jnp.float32,
    )
    key_parts = d_key.reshape(rows, width)
    value_parts = d_val.reshape(rows, width)
    d_key_all = key_parts.astype(jnp.bfloat16)
    d_value_all = value_parts.astype(jnp.bfloat16)
    grad_query = dot_left(a_one, d_queries)
    grad_key = dot_left(a_one, d_key_all)
    grad_value = dot_left(a_one, d_value_all)
    d_a_one = dot_right(d_queries, wq) + dot_right(d_key_all, wk) + dot_right(d_value_all, wv)
    d_norm_one, grad_gain_attn = norm_back(x, gain_attn, inv_one, d_a_one)
    grad_tokens = (d_hidden + d_norm_one).astype(jnp.bfloat16).reshape(segs, rows, width)
    full_grads = (
        grad_query,
        grad_key,
        grad_value,
        grad_out,
        grad_gate,
        grad_up,
        grad_down,
        grad_gain_attn,
        grad_gain_ffn,
    )
    split_grads = tuple((g.reshape(seg_count, group, -1) for g in full_grads))
    row_summed = jax.tree.map(
        lambda part: part.astype(jnp.float32),
        lax.psum_scatter(for_sending(split_grads), "row", scatter_dimension=1, tiled=True),
    )
    owned_flat = jax.tree.map(
        lambda part: part.astype(jnp.float32),
        lax.psum_scatter(for_sending(row_summed), "seg", scatter_dimension=0, tiled=True),
    )
    owned = []
    for whole_grad, piece in zip(full_grads, owned_flat):
        own_rows = whole_grad.shape[0] // (seg_count * group)
        owned.append(piece.reshape((own_rows,) + whole_grad.shape[1:]))
    return (
        layer_out,
        grad_tokens,
        owned[0],
        owned[1],
        owned[2],
        owned[3],
        owned[4],
        owned[5],
        owned[6],
        owned[7],
        owned[8],
    )


MESH = pl.DeviceIdType.MESH
BF = jnp.bfloat16
F32 = jnp.float32
VM = pltpu.VMEM
DMA = pltpu.SemaphoreType.DMA


def device(z, y, c, x):
    return ((z * 2 + y) * 2 + c, x)


def remote(src, dst, send, recv, where):
    return pltpu.make_async_remote_copy(
        src_ref=src, dst_ref=dst, send_sem=send, recv_sem=recv, device_id=where, device_id_type=MESH
    )


def aligned(value, unit):
    return pl.multiple_of(value, unit)


def layer_kernel(
    tok, cot, mem_k, mem_v, choice, flag, w_q, w_k, w_v, w_o, w_b, w_d, gains,
    out_y, out_x, out_q, out_k, out_v, out_o, out_b, out_d, out_g,
    wa, wo, wb, wc, w_land, gc, go, c_a, c_o, c_b, c_d, y_a, y_o, y_b, y_d, z_a, z_o, z_b, z_d, x_n, x_d,
    xf, dyf, act, tr, qkv, aof, h, hid, dgu, part, swap_r, swap_s, dqkv, kv_acc, mk, mv,
    row_s, row_r, gain, gain_acc,
    own_s, xs, xr, zs, zr, ys, yr, cs, cr, mem_s, es, er, rcs, rcr, rys, ryr, rzs, rzr, rxs, rxr,
):
    seg = lax.axis_index("seg")
    x = lax.axis_index("row")
    c = seg % 2
    y = (seg // 2) % 2
    z = seg // 4
    rows, width = tok.shape
    length = 2 * rows
    heads = choice.shape[1]
    cols = heads * HD
    ff = wc.shape[0]
    blk = wc.shape[0] // 8
    scale = HD ** (-0.5)
    over_x, over_y, over_c = device(z, y, c, 1 - x), device(z, 1 - y, c, x), device(z, y, 1 - c, x)
    mine = x == c
    other = jnp.logical_not(mine)
    col0 = aligned(x * cols, cols)

    barrier = pltpu.get_barrier_semaphore()
    for d in range(1, 4):
        pl.semaphore_signal(barrier, inc=1, device_id=device((z + d) % 4, y, c, x), device_id_type=MESH)
    for peer in (over_x, over_y, over_c):
        pl.semaphore_signal(barrier, inc=1, device_id=peer, device_id_type=MESH)
    pl.semaphore_wait(barrier, 6)

    def chunk(n):
        return [(i, min(512, n - i)) for i in range(0, n, 512)]

    groups = [(wa, 0, 512), (wa, 512, 512), (wa, 1024, 640)]
    groups += [(wo, i, n) for i, n in chunk(width)] + [(wb, i, n) for i, n in chunk(2 * ff)]
    n_groups = len(groups)

    def block(g, zz, yy):
        if g >= n_groups:
            p = zz * 2 + yy
            return wc.at[pl.ds(aligned(p * blk, 16), blk), pl.ds((g - n_groups) * 512, 512)]
        ref, at, n = groups[g]
        return ref.at[zz, yy, c, :, pl.ds(at, n)]

    def part_of(g, which):
        peer_half = aligned(which * cols, cols)
        if g < 3:
            return [w_q, w_k, w_v][g].at[:, pl.ds(peer_half, cols)]
        ref, at, n = groups[g]
        return w_o.at[:, pl.ds(at, n)] if ref is wo else w_b.at[which, :, pl.ds(at, n)]

    def my_rows(g):
        ref, at, n = groups[g]
        n = min(n, 512)
        return ref.at[z, y, c, pl.ds(aligned(x * 32, 32), 32), pl.ds(at, n)]

    my_gain = wa.at[z, y, c, pl.ds(aligned(x * 32, 32), 32), pl.ds(3 * cols, 128)]
    my_down = w_land.at[x]
    gx, tx, dx, cx = n_groups, n_groups + 1, n_groups + 2, n_groups + 3
    first = [remote(part_of(g, 1 - x), my_rows(g), xs.at[g], xr.at[g], over_x) for g in range(n_groups)]
    local = [pltpu.make_async_copy(part_of(g, x), my_rows(g), own_s.at[g]) for g in range(n_groups)]
    first.append(remote(gains, my_gain, xs.at[gx], xr.at[gx], over_x))
    local.append(pltpu.make_async_copy(gains, my_gain, own_s.at[gx]))
    first.append(remote(tok, xf.at[pl.ds(rows, rows)], xs.at[tx], xr.at[tx], over_x))
    local.append(pltpu.make_async_copy(tok, xf.at[pl.ds(0, rows)], own_s.at[tx]))
    first.append(remote(cot, dyf.at[pl.ds(rows, rows)], xs.at[dx], xr.at[dx], over_x))
    local.append(pltpu.make_async_copy(cot, dyf.at[pl.ds(0, rows)], own_s.at[dx]))
    down_x = remote(w_d, my_down, xs.at[cx], xr.at[cx], over_x)
    down_l = pltpu.make_async_copy(w_d, my_down, own_s.at[cx])

    def to_z(g, d):
        b = block(g, z, y)
        return remote(b, b, zs.at[g, d - 1], zr.at[g, d - 1], device((z + d) % 4, y, c, x))

    def to_y(g, d):
        b = block(g, (z + 4 - d) % 4, y)
        return remote(b, b, ys.at[g, d], yr.at[g, d], over_y)

    def to_c(g, d, f):
        b = block(g, (z + 4 - d) % 4, (y + f) % 2)
        return remote(b, b, cs.at[g, d, f], cr.at[g, d, f], over_c)

    def gated(fn):
        def run(g, *rest):
            if g >= n_groups:
                pl.when(mine)(lambda: fn(g, *rest))
            else:
                fn(g, *rest)

        return run

    @gated
    def spread(g):
        if g < n_groups:
            first[g].wait_recv()
            local[g].wait()
            if g == 2:
                first[gx].wait_recv()
                local[gx].wait()
        elif g == n_groups:
            down_x.wait_recv()
            down_l.wait()
            pair = jnp.concatenate([w_land[0].astype(F32), w_land[1].astype(F32)], axis=0)
            wc[pl.ds(aligned((z * 2 + y) * blk, 16), blk)] = pair.astype(BF)
        for d in range(1, 4):
            to_z(g, d).start()
        to_y(g, 0).start()
        to_c(g, 0, 0).start()

    @gated
    def pass_z(g):
        for d in range(1, 4):
            to_z(g, d).wait_recv()
            to_y(g, d).start()
            to_c(g, d, 0).start()

    @gated
    def pass_y(g):
        for d in range(4):
            to_y(g, d).wait_recv()
            to_c(g, d, 1).start()

    def arrived(g):
        for d in range(4):
            for f in range(2):
                to_c(g, d, f).wait_recv()

    @gated
    def sent(g):
        for d in range(1, 4):
            to_z(g, d).wait_send()
        for d in range(4):
            to_y(g, d).wait_send()
            for f in range(2):
                to_c(g, d, f).wait_send()

    last_group = n_groups + 1

    def step(g):
        if g <= last_group:
            pass_z(g)
        if g + 2 <= last_group:
            spread(g + 2)
        if 1 <= g <= last_group + 1:
            pass_y(g - 1)

    for g in (0, 1, 2, gx):
        first[g].start()
        local[g].start()
    local[tx].start()
    local[dx].start()
    mem_bufs = [[dqkv.at[pl.ds(256 * s, 256), pl.ds(512 * i, 512)] for i in range(2)] for s in range(2)]

    def mem_copy(i, s):
        at = aligned(i * 256, 256)
        return [
            pltpu.make_async_copy(m.at[pl.ds(at, 256), pl.ds(col0, cols)], mem_bufs[s][j], mem_s.at[s, j])
            for j, m in enumerate((mem_k, mem_v))
        ]

    for cp in mem_copy(0, 0):
        cp.start()
    spread(0)
    spread(1)
    for g in list(range(3, n_groups)):
        first[g].start()
        local[g].start()

    @pl.when(mine)
    def _():
        down_l.start()

    @pl.when(other)
    def _():
        down_x.start()

    first[tx].start()

    kv_acc[...] = jnp.zeros_like(kv_acc)
    n_mem = mem_k.shape[0] // 256

    @pl.loop(0, n_mem // 2)
    def _(t):
        for s in range(2):
            i = t * 2 + s
            if s == 0:
                for cp in mem_copy(i + 1, 1):
                    cp.start()
            else:

                @pl.when(i + 1 < n_mem)
                def _():
                    for cp in mem_copy(i + 1, 0):
                        cp.start()

            for cp in mem_copy(i, s):
                cp.wait()
            at = lax.broadcasted_iota(jnp.int32, (HD, 256), 1) + i * 256
            for hh in range(heads):
                hot = (choice[:, hh : hh + 1] == at).astype(F32).astype(BF)
                lanes = slice(hh * HD, (hh + 1) * HD)
                for j in range(2):
                    kv_acc[j * HD : (j + 1) * HD, lanes] += plain_dot(hot, mem_bufs[s][j][:, lanes])

    mk[...] = kv_acc[0:HD].astype(BF)
    mv[...] = kv_acc[HD : 2 * HD].astype(BF)

    step(0)
    step(1)
    step(2)
    first[tx].wait_recv()
    local[tx].wait()
    first[dx].start()
    step(3)
    for g in range(3):
        arrived(g)

    @pl.loop(0, 8)
    def _(p):
        block_t = jnp.transpose(
            wa[p // 2, p % 2, :, :, 3 * cols : 3 * cols + 128].reshape(128, 128).astype(F32)
        )
        gain[:, pl.ds(aligned(p * 128, 128), 128)] = block_t[0:8]

    def norm_rows(at, n):
        xc = xf[pl.ds(at, n)].astype(F32)
        inv = lax.rsqrt(jnp.mean(xc * xc, axis=-1, keepdims=True) + EPS)
        return xc * inv, inv

    def norm_one(i):
        at = aligned(i * 64, 64)
        u, _ = norm_rows(at, 64)
        return at, (u * gain[0:1]).astype(BF)

    @pl.loop(0, length // 64)
    def _(i):
        at, a = norm_one(i)
        act[pl.ds(at, 64)] = a

    def w_cols(ref, at, n):
        return ref[:, :, :, :, pl.ds(at, n)].reshape(width, n)

    @pl.loop(0, 3 * cols // 256)
    def _(i):
        at = aligned(i * 256, 256)
        qkv[:, pl.ds(at, 256)] = plain_dot(act[...], w_cols(wa, at, 256)).astype(BF)

    step(4)
    shift = lax.broadcasted_iota(jnp.int32, (HD, length), 1)
    key_pos = shift + jnp.where(shift < rows, x * rows, (1 - x) * rows - rows)
    sub = lax.broadcasted_iota(jnp.int32, (HD, length), 0)

    def probs(hh, i):
        at = aligned(i * HD, HD)
        lane = aligned(hh * HD, HD)
        query = qkv[pl.ds(at, HD), pl.ds(lane, HD)]
        key = qkv[:, pl.ds(aligned(cols + hh * HD, HD), HD)]
        local_s = dot_right(query, key) * scale
        base = i * HD + jnp.where(i * HD < rows, x * rows, (1 - x) * rows - rows)
        local_s = jnp.where(key_pos <= sub + base, local_s, NEG)
        far = dot_right(query, mk[:, pl.ds(lane, HD)]) * scale
        far = jnp.where(flag[0:1] > 0, far, NEG)
        top = jnp.maximum(jnp.max(local_s, axis=-1, keepdims=True), jnp.max(far, axis=-1, keepdims=True))
        local_e, far_e = jnp.exp(local_s - top), jnp.exp(far - top)
        total = jnp.sum(local_e, axis=-1, keepdims=True) + jnp.sum(far_e, axis=-1, keepdims=True)
        inv = 1.0 / total
        return query, key, local_e * inv, far_e * inv, at, lane

    def att_copy(hh, f):
        lanes = pl.ds(aligned(col0 + hh * HD, HD), HD)
        return remote(
            aof.at[pl.ds(f * rows, rows), lanes], aof.at[pl.ds((1 - f) * rows, rows), lanes],
            es.at[hh * 2 + f], er.at[hh * 2 + f], over_x,
        )

    def attend(hh):
        @pl.loop(0, length // HD)
        def _(i):
            _, _, pl_, pm_, at, lane = probs(hh, i)
            value = qkv[:, pl.ds(2 * cols + hh * HD, HD)]
            out = plain_dot(pl_.astype(BF), value) + plain_dot(pm_.astype(BF), mv[:, pl.ds(lane, HD)])
            aof[pl.ds(at, HD), pl.ds(aligned(col0 + hh * HD, HD), HD)] = out.astype(BF)

        att_copy(hh, 0).start()
        att_copy(hh, 1).start()

    attend(0)
    attend(1)
    step(5)
    attend(2)
    attend(3)
    step(6)
    arrived(3)
    arrived(4)
    for hh in range(heads):
        for f in range(2):
            att_copy(hh, f).wait_recv()

    @pl.loop(0, width // 256)
    def _(i):
        at = aligned(i * 256, 256)
        h[:, pl.ds(at, 256)] = xf[:, pl.ds(at, 256)].astype(F32) + plain_dot(aof[...], w_cols(wo, at, 256))

    @pl.loop(0, length // 64)
    def _(i):
        at = aligned(i * 64, 64)
        hc = h[pl.ds(at, 64)]
        inv = lax.rsqrt(jnp.mean(hc * hc, axis=-1, keepdims=True) + EPS)
        act[pl.ds(at, 64)] = (hc * inv * gain[1:2]).astype(BF)

    def up_tile(j):
        at = aligned(j * 256, 256)
        both = plain_dot(act[...], w_cols(wb, at, 256))
        gate, up = both[:, :128], both[:, 128:]
        sig = 1.0 / (1.0 + jnp.exp(-gate))
        silu = gate * sig
        tile = (silu * up).astype(BF)
        lanes = pl.ds(aligned(j * 128, 128), 128)
        hid[:, lanes] = tile
        tr[lanes] = jnp.transpose(tile)
        dgu[:, pl.ds(at, 128)] = (up * sig * (1.0 + gate * (1.0 - sig))).astype(BF)
        dgu[:, pl.ds(aligned(at + 128, 128), 128)] = silu.astype(BF)

    for g in range(5, n_groups):
        step(g + 2)
        arrived(g)
        pl.loop((g - 5) * 2, (g - 5) * 2 + groups[g][2] // 256)(up_tile)

    first[dx].wait_recv()
    local[dx].wait()

    red = [(None, c_d, y_d, z_d, 0, 512), (None, c_d, y_d, z_d, 512, 512)]
    red += [(wb, c_b, y_b, z_b, i, n) for i, n in chunk(2 * ff)]
    red += [(go, c_o, y_o, z_o, 0, 512)]
    red += [(wa, c_a, y_a, z_a, 0, 512), (wa, c_a, y_a, z_a, 512, 512), (wa, c_a, y_a, z_a, 1024, 640)]
    n_red = len(red)
    x_at = [0, 512]
    for g in range(2, n_red):
        x_at.append(sum(red[i][5] for i in range(2, g)))

    def red_c(g):
        src, cb, _, _, at, n = red[g]
        lanes = pl.ds(at, n)
        source = gc.at[:, :, :, lanes] if g < 2 else src.at[:, :, 1 - c, :, lanes]
        return remote(source, cb.at[:, :, :, lanes], rcs.at[g], rcr.at[g], over_c)

    def red_y(g):
        _, cb, yb, _, at, n = red[g]
        lanes = pl.ds(at, n)
        return remote(cb.at[:, 1 - y, :, lanes], yb.at[:, :, lanes], rys.at[g], ryr.at[g], over_y)

    def red_z(g, d):
        _, _, yb, zb, at, n = red[g]
        lanes = pl.ds(at, n)
        zz = (z + d) % 4
        return remote(
            yb.at[zz, :, lanes], zb.at[d - 1, :, lanes], rzs.at[g, d - 1], rzr.at[g, d - 1], device(zz, y, c, x)
        )

    def red_x(g):
        lanes = pl.ds(x_at[g], red[g][5])
        buf = x_d if g < 2 else x_n
        return remote(buf.at[0, :, lanes], buf.at[1, :, lanes], rxs.at[g], rxr.at[g], over_x)

    def only_mine(fn):
        def run(g):
            if g < 2:
                pl.when(mine)(lambda: fn(g))
            else:
                fn(g)

        return run

    def start_c(g):
        if g < 2:
            pl.when(other)(lambda: red_c(g).start())
        else:
            red_c(g).start()

    @only_mine
    def sum_c(g):
        red_c(g).wait_recv()
        src, cb, _, _, at, n = red[g]
        lanes = pl.ds(at, n)

        @pl.loop(0, 8)
        def _(i):
            own = gc[i // 2, i % 2, :, lanes] if g < 2 else src[i // 2, i % 2, c, :, lanes]
            cb[i // 2, i % 2, :, lanes] = (cb[i // 2, i % 2, :, lanes].astype(F32) + own.astype(F32)).astype(BF)

        red_y(g).start()

    @only_mine
    def sum_y(g):
        red_y(g).wait_recv()
        _, cb, yb, _, at, n = red[g]
        lanes = pl.ds(at, n)

        @pl.loop(0, 4)
        def _(i):
            yb[i, :, lanes] = (yb[i, :, lanes].astype(F32) + cb[i, y, :, lanes].astype(F32)).astype(BF)

        for d in range(1, 4):
            red_z(g, d).start()

    def result(g, which, value):
        at, n = red[g][4], red[g][5]
        if g < 2:
            out_d[:, at : at + n] = value
        elif g < n_red - 4:
            out_b[which, :, at : at + n] = value
        else:
            out = [out_o, out_q, out_k, out_v][g - (n_red - 4)]
            out[:, pl.ds(aligned(which * cols, cols), cols)] = value[:, :cols]
            if n > cols:
                out_g[which] = value[:, cols:]

    @only_mine
    def sum_z(g):
        for d in range(1, 4):
            red_z(g, d).wait_recv()
        _, _, yb, zb, at, n = red[g]
        lanes = pl.ds(at, n)
        size = yb.shape[1] // 2
        total = yb[z, :, lanes].astype(F32)
        for d in range(3):
            total = total + zb[d, :, lanes].astype(F32)
        low, high = total[:size], total[size:]
        buf = x_d if g < 2 else x_n
        buf[0, :, pl.ds(x_at[g], n)] = jnp.where(x == 0, high, low).astype(BF)
        red_x(g).start()
        result(g, x, jnp.where(x == 0, low, high))

    def finish(g):
        lanes = pl.ds(x_at[g], red[g][5])

        def take():
            red_x(g).wait_recv()
            result(g, 1 - x, (x_d if g < 2 else x_n)[1, :, lanes].astype(F32))

        if g < 2:
            pl.when(other)(take)
        else:
            take()

    @only_mine
    def red_sent(g):
        red_y(g).wait_send()
        for d in range(1, 4):
            red_z(g, d).wait_send()
        red_x(g).wait_send()

    def tick(k):
        if k < n_red:
            sum_c(k)
        if 0 <= k - 1 < n_red:
            sum_y(k - 1)
        if 0 <= k - 3 < n_red:
            sum_z(k - 3)
        if 0 <= k - 4 < n_red:
            finish(k - 4)

    for i in range(2):

        @pl.loop(0, 4)
        def _(t):
            res = plain_dot(tr[pl.ds(aligned(t * 2 * blk, 32), 2 * blk)], dyf[:, i * 512 : (i + 1) * 512])
            gc[t, :, :, i * 512 : (i + 1) * 512] = res.reshape(2, blk, 512).astype(BF)

        start_c(i)
    for g in range(n_groups, last_group + 1):
        step(g + 2) if g + 2 > n_groups + 1 else None

    def wait_down():
        for g in range(n_groups, last_group + 1):
            arrived(g)

    pl.when(other)(wait_down)

    def dhid_tile(j, n):
        lanes = aligned(j * 128, 128)
        res = dot_right(dyf[...], wc[pl.ds(lanes, 128 * n)])
        for t in range(n):
            at = aligned((j + t) * 256, 256)
            d = res[:, t * 128 : (t + 1) * 128]
            for s in range(2):
                where = pl.ds(aligned(at + 128 * s, 128), 128)
                dgu[:, where] = (d * dgu[:, where].astype(F32)).astype(BF)

    n_tiles = ff // 128

    @pl.loop(0, n_tiles // 2)
    def _(t):
        dhid_tile(t * 2, 2)

    if n_tiles % 2:
        dhid_tile(n_tiles - 1, 1)

    gain_acc[...] = jnp.zeros_like(gain_acc)

    def swap_copy(i):
        at = 128 * i
        to = (at + rows) % length
        return remote(
            swap_s.at[pl.ds(at, 128)], swap_r.at[pl.ds(to, 128)], es.at[8 + i], er.at[8 + to // 128], over_x
        )

    for f in range(2):

        @pl.loop(0, width // 256)
        def _(i):
            at = aligned(i * 256, 256)
            res = dot_right(dgu[f * rows : (f + 1) * rows], wb[i, :, :, :, :].reshape(256, 2 * ff))
            part[f * rows : (f + 1) * rows, pl.ds(at, 256)] = res
            swap_s[f * rows : (f + 1) * rows, pl.ds(at, 256)] = res.astype(BF)

        swap_copy(2 * f).start()
        swap_copy(2 * f + 1).start()

    for f in (1,):

        @pl.loop(0, width // 256)
        def _(i):
            at = aligned(i * 256, 256)
            row_s[:, pl.ds(at, 256)] = plain_dot(hid[rows:], wc[:, pl.ds(at, 256)]).astype(BF)

    row_y = remote(row_s, row_r.at[0], es.at[12], er.at[12], over_x)
    row_y.start()

    @pl.loop(0, length // 128)
    def _(i):
        at = aligned(i * 128, 128)
        tr[0:width, pl.ds(at, 128)] = jnp.transpose(act[pl.ds(at, 128)])

    def add_gain(k, grad, unit):
        prod = grad * unit
        gain_acc[k] += jnp.sum(prod.reshape(prod.shape[0] // 8, 8, width), axis=0)

    @pl.loop(0, length // 64)
    def _(i):
        at = aligned(i * 64, 64)
        hc = h[pl.ds(at, 64)]
        inv = lax.rsqrt(jnp.mean(hc * hc, axis=-1, keepdims=True) + EPS)
        add_gain(1, part[pl.ds(at, 64)], hc * inv)

    def grad_tile(dst, lhs_rows, value, at):
        res = plain_dot(tr[0:lhs_rows], value)
        dst[:, :, :, :, pl.ds(at, 256)] = res.reshape(4, 2, 2, 64, 256).astype(BF)

    n_b = len(chunk(2 * ff))
    for g in range(5, n_groups):
        sent(g)
    for g in range(n_b):
        at0, n = red[2 + g][4], red[2 + g][5]
        for t in range(n // 256):
            grad_tile(wb, width, dgu[:, at0 + t * 256 : at0 + (t + 1) * 256], at0 + t * 256)
        start_c(2 + g)
        if g >= 1:
            tick(g - 1)

    def d_hidden_rows(i):
        at = aligned(i * 64, 64)
        hc = h[pl.ds(at, 64)]
        inv = lax.rsqrt(jnp.mean(hc * hc, axis=-1, keepdims=True) + EPS)
        u = hc * inv
        e = (part[pl.ds(at, 64)] + swap_r[pl.ds(at, 64)].astype(F32)) * gain[1:2]
        dh = dyf[pl.ds(at, 64)].astype(F32) + inv * (e - u * jnp.mean(e * u, axis=-1, keepdims=True))
        part[pl.ds(at, 64)] = dh
        act[pl.ds(at, 64)] = dh.astype(BF)

    row_y.wait_recv()

    @pl.loop(0, width // 256)
    def _(i):
        at = aligned(i * 256, 256)
        own = plain_dot(hid[:rows], wc[:, pl.ds(at, 256)]) + h[:rows, pl.ds(at, 256)]
        out_y[:, pl.ds(at, 256)] = (own + row_r[0, :, pl.ds(at, 256)].astype(F32)).astype(BF)

    d_att = swap_s
    for f in (1, 0):
        for i in (2 * f, 2 * f + 1):
            swap_copy(i).wait_recv()
    for f in range(2):
        pl.loop(f * rows // 64, (f + 1) * rows // 64)(d_hidden_rows)
    for i in range(4):
        swap_copy(i).wait_send()
    w_own = wo.at[pl.ds(x * 2, 2)]
    res = dot_right(act[...], w_own[...].reshape(cols, width))
    d_att[:, 0:cols] = res.astype(BF)

    def attend_back(hh):
        kv_acc[...] = jnp.zeros_like(kv_acc)

        @pl.loop(0, length // HD)
        def _(i):
            query, key, p_l, p_m, at, lane = probs(hh, i)
            value = qkv[:, pl.ds(2 * cols + hh * HD, HD)]
            grad = d_att[pl.ds(at, HD), pl.ds(lane, HD)]
            dp_l = dot_right(grad, value)
            dp_m = dot_right(grad, mv[:, pl.ds(lane, HD)])
            delta = jnp.sum(p_l * dp_l, axis=-1, keepdims=True) + jnp.sum(p_m * dp_m, axis=-1, keepdims=True)
            ds_l = (p_l * (dp_l - delta)).astype(BF)
            ds_m = (p_m * (dp_m - delta)).astype(BF)
            dq = (plain_dot(ds_l, key) + plain_dot(ds_m, mk[:, pl.ds(lane, HD)])) * scale
            dqkv[pl.ds(at, HD), pl.ds(lane, HD)] = dq.astype(BF)
            kv_acc[0:length, 0:HD] += dot_left(ds_l, query)
            kv_acc[0:length, HD : 2 * HD] += dot_left(p_l.astype(BF), grad)

        dqkv[:, pl.ds(cols + hh * HD, HD)] = (kv_acc[0:length, 0:HD] * scale).astype(BF)
        dqkv[:, pl.ds(2 * cols + hh * HD, HD)] = kv_acc[0:length, HD : 2 * HD].astype(BF)

    @pl.loop(0, length // 128)
    def _(i):
        at = aligned(i * 128, 128)
        tr[0:width, pl.ds(at, 128)] = jnp.transpose(aof[pl.ds(at, 128)])

    for t in range(2):
        grad_tile(go, width, act[:, pl.ds(aligned(col0 + t * 256, 256), 256)], t * 256)
    start_c(2 + n_b)
    base = n_b - 1
    for hh in range(heads):
        attend_back(hh)
        tick(base + hh)
    row_y.wait_send()

    for f in (1, 0):

        @pl.loop(0, width // 256)
        def _(i):
            at = aligned(i * 256, 256)
            res = dot_right(
                dqkv[f * rows : (f + 1) * rows], wa[i, :, :, :, 0 : 3 * cols].reshape(256, 3 * cols)
            )
            swap = pl.ds(at, 256)
            if f == 1:
                row_s[:, swap] = res.astype(BF)
            h[f * rows : (f + 1) * rows, swap] = res

        if f == 1:
            row_x = remote(row_s, row_r.at[1], es.at[13], er.at[13], over_x)
            row_x.start()

    @pl.loop(0, length // 64)
    def _(i):
        at = aligned(i * 64, 64)
        u, _ = norm_rows(at, 64)
        add_gain(0, h[pl.ds(at, 64)], u)

    @pl.loop(0, length // 128)
    def _(i):
        at = aligned(i * 128, 128)
        u, _ = norm_rows(at, 128)
        tr[0:width, pl.ds(at, 128)] = jnp.transpose((u * gain[0:1]).astype(BF))

    for g in range(3):
        sent(g)
    sums = [jnp.sum(gain_acc[k], axis=0, keepdims=True) for k in range(2)]
    tall = lax.broadcasted_iota(jnp.int32, (128, 128), 0)
    for p in range(8):
        lanes = slice(p * 128, (p + 1) * 128)
        both = jnp.where(tall == 0, sums[0][:, lanes], jnp.where(tall == 1, sums[1][:, lanes], 0.0))
        wa[p // 2, p % 2, :, :, 3 * cols :] = jnp.transpose(both).reshape(2, 64, 128).astype(BF)
    base += heads
    for g in range(3):
        for t in range(2):
            at = g * cols + t * 256
            grad_tile(wa, width, dqkv[:, at : at + 256], at)
        start_c(3 + n_b + g)
        if base < n_red:
            tick(base)
            base += 1
    row_x.wait_recv()

    @pl.loop(0, rows // 64)
    def _(i):
        at = aligned(i * 64, 64)
        u, inv = norm_rows(at, 64)
        e = (h[pl.ds(at, 64)] + row_r[1, pl.ds(at, 64)].astype(F32)) * gain[0:1]
        out = part[pl.ds(at, 64)] + inv * (e - u * jnp.mean(e * u, axis=-1, keepdims=True))
        out_x[pl.ds(at, 64)] = out.astype(BF)

    for k in range(base, n_red + 4):
        tick(k)
    for cp in first:
        cp.wait_send()
    pl.when(other)(lambda: down_x.wait_send())
    for g in [3, 4] + list(range(n_groups, last_group + 1)):
        sent(g)
    for hh in range(heads):
        for f in range(2):
            att_copy(hh, f).wait_send()
    row_x.wait_send()
    for g in range(n_red):
        if g < 2:
            pl.when(other)(lambda: red_c(g).wait_send())
        else:
            red_c(g).wait_send()
        red_sent(g)


def layer(tok, cot, mem_k, mem_v, choice, flag, w_q, w_k, w_v, w_o, w_b, w_d, gains):
    rows, width = tok.shape
    length = 2 * rows
    cols = choice.shape[1] * HD
    ff2 = w_b.shape[2]
    ff = ff2 // 2
    blk = ff // 8
    na = 3 * cols + 128
    hbm, vm = pl.BlockSpec(memory_space=pl.ANY), pl.BlockSpec(memory_space=pltpu.VMEM)
    own = w_q.shape[0]
    shape = jax.ShapeDtypeStruct
    return pl.pallas_call(
        layer_kernel,
        name="layer",
        out_shape=(
            shape((rows, width), BF),
            shape((rows, width), BF),
            shape((own, width), F32),
            shape((own, width), F32),
            shape((own, width), F32),
            shape((own, width), F32),
            shape((2, own, ff2), F32),
            shape((blk // 2, width), F32),
            shape((2, own, 128), F32),
        ),
        in_specs=[hbm] * 4 + [vm] * 2 + [hbm] * 7,
        out_specs=(vm,) * 9,
        scratch_shapes=[
            VM((4, 2, 2, 64, na), BF), VM((4, 2, 2, 64, width), BF), VM((4, 2, 2, 64, ff2), BF), VM((ff, width), BF), VM((2, blk // 2, width), BF),
            VM((4, 2, blk, width), BF), VM((4, 2, 2, 64, cols), BF),
            VM((4, 2, 64, na), BF), VM((4, 2, 64, cols), BF), VM((4, 2, 64, ff2), BF), VM((4, 2, blk, width), BF),
            VM((4, 64, na), BF), VM((4, 64, cols), BF), VM((4, 64, ff2), BF), VM((4, blk, width), BF),
            VM((3, 64, na), BF), VM((3, 64, cols), BF), VM((3, 64, ff2), BF), VM((3, blk, width), BF),
            VM((2, own, ff2 + na + cols), BF), VM((2, blk // 2, width), BF),
            VM((length, width), BF), VM((length, width), BF), VM((length, width), BF), VM((ff, length), BF),
            VM((length, 3 * cols), BF), VM((length, width), BF), VM((length, width), F32), VM((length, ff), BF),
            VM((length, ff2), BF), VM((length, width), F32), VM((length, width), BF), VM((length, width), BF),
            VM((length, 3 * cols), BF), VM((length, cols), F32), VM((HD, cols), BF), VM((HD, cols), BF),
            VM((rows, width), BF), VM((2, rows, width), BF), VM((8, width), F32), VM((2, 8, width), F32),
            DMA((16,)), DMA((16,)), DMA((16,)), DMA((13, 3)), DMA((13, 3)), DMA((13, 4)), DMA((13, 4)),
            DMA((13, 4, 2)), DMA((13, 4, 2)), DMA((2, 2)), DMA((14,)), DMA((14,)),
            DMA((12,)), DMA((12,)), DMA((12,)), DMA((12,)), DMA((12, 3)), DMA((12, 3)), DMA((12,)), DMA((12,)),
        ],
        compiler_params=pltpu.CompilerParams(collective_id=0, has_side_effects=True, vmem_limit_bytes=63 << 20),
    )(tok, cot, mem_k, mem_v, choice, flag, w_q, w_k, w_v, w_o, w_b, w_d, gains)


def fast_body(
    tokens, cotangent, memory_keys, memory_values, memory_choice, memory_flag,
    w_query, w_key, w_value, w_out, w_gate, w_up, w_down, norm_attn, norm_ffn,
):
    own_rows, ffw = w_gate.shape
    heads = HEADS // 2
    strip = w_down.shape[0] * 2
    hidden = ffw // 2
    r = lax.axis_index("row")
    gains = jnp.zeros((own_rows, 128), BF).at[:, 0].set(norm_attn).at[:, 1].set(norm_ffn)

    def strips(w):
        w = jnp.transpose(w.reshape(own_rows, -1, 2, strip), (2, 0, 1, 3))
        return w.reshape(2, own_rows, hidden // 128, 1, 128)

    w_b = jnp.concatenate([strips(w_gate), strips(w_up)], axis=3).reshape(2, own_rows, 2 * hidden)
    choice = jnp.transpose(lax.dynamic_slice_in_dim(memory_choice[0, 0], r * heads, heads, axis=0))
    flag = jnp.broadcast_to(memory_flag[:, None], (8, 128))
    out_y, out_x, g_q, g_k, g_v, g_o, g_b, g_d, g_n = layer(
        tokens[0], cotangent[0], memory_keys[0], memory_values[0], choice, flag,
        w_query, w_key, w_value, w_out, w_b, w_down, gains,
    )
    g_b = g_b.reshape(2, own_rows, hidden // 128, 2, 128)

    def weave(i):
        g = g_b[:, :, :, i].reshape(2, own_rows, -1, strip)
        return jnp.transpose(g, (1, 2, 0, 3)).reshape(own_rows, ffw)

    g_n = g_n[0] + g_n[1]
    return (out_y[None], out_x[None], g_q, g_k, g_v, g_o, weave(0), weave(1), g_d, g_n[:, 0], g_n[:, 1])


def solution(mesh):
    in_specs = (
        P("seg", "row", None),
        P("seg", "row", None),
        P("seg", None, None),
        P("seg", None, None),
        P("seg", None, None, None),
        P("seg"),
        P(("seg", "row"), None),
        P(("seg", "row"), None),
        P(("seg", "row"), None),
        P(("seg", "row"), None),
        P(("seg", "row"), None),
        P(("seg", "row"), None),
        P(("seg", "row"), None),
        P(("seg", "row")),
        P(("seg", "row")),
    )
    out_specs = (
        P("seg", "row", None),
        P("seg", "row", None),
        P(("seg", "row"), None),
        P(("seg", "row"), None),
        P(("seg", "row"), None),
        P(("seg", "row"), None),
        P(("seg", "row"), None),
        P(("seg", "row"), None),
        P(("seg", "row"), None),
        P(("seg", "row")),
        P(("seg", "row")),
    )

    def body(*args):
        segs, rows, width = args[0].shape
        fits = (
            mesh.shape["row"] == 2
            and mesh.shape["seg"] == 16
            and segs == 1
            and (rows, width) == (256, 1024)
            and args[4].shape[1] == 1
        )
        return (fast_body if fits else general_body)(*args)

    return jax.shard_map(body, mesh=mesh, in_specs=in_specs, out_specs=out_specs, check_vma=False)
```

```python
import functools

import jax
import jax.numpy as jnp
from jax import lax
from jax.experimental import pallas as pl
from jax.experimental.pallas import tpu as pltpu
from jax.sharding import PartitionSpec as P

HEADS = 8
HD = 128
QBLK = 512


EPS = 1e-06
NEG = -1000000000.0


def for_sending(array):

    def short(part):
        return part.astype(jnp.bfloat16) if part.dtype == jnp.float32 else part

    return jax.tree.map(short, array)


def plain_dot(left, right):
    return jnp.dot(left, right, preferred_element_type=jnp.float32)


def dot_left(left, right):
    return lax.dot_general(
        left, right, (((0,), (0,)), ((), ())), preferred_element_type=jnp.float32
    )


def dot_right(left, right):
    return lax.dot_general(
        left, right, (((1,), (1,)), ((), ())), preferred_element_type=jnp.float32
    )


def norm_apply(value, gain):
    inverse = lax.rsqrt(jnp.mean(value * value, axis=-1, keepdims=True) + EPS)
    return (value * inverse * gain, inverse)


def norm_back(value, gain, inverse, grad):
    unit = value * inverse
    gain_grad = jnp.sum(grad * unit, axis=0)
    scaled = grad * gain
    return (inverse * (scaled - unit * jnp.mean(scaled * unit, axis=-1, keepdims=True)), gain_grad)


def score_block(queries, keys, memory_key_rows, flag, first, length):
    score_scale = HD ** (-0.5)
    local = (
        jnp.einsum("bqhd,khd->bhqk", queries, keys, preferred_element_type=jnp.float32)
        * score_scale
    )
    distant_memory = (
        jnp.einsum("bqhd,bhmd->bhqm", queries, memory_key_rows, preferred_element_type=jnp.float32)
        * score_scale
    )
    nblocks, per_block = (queries.shape[0], queries.shape[1])
    pos = first + jnp.arange(nblocks * per_block).reshape(nblocks, 1, per_block, 1)
    key_pos = jnp.arange(length)
    local = jnp.where(key_pos[None, None, None, :] <= pos, local, NEG)
    distant_memory = jnp.where(flag > 0, distant_memory, NEG)
    return (local, distant_memory)


def row_stat(stat, rows):
    return jnp.transpose(stat[..., 0], (0, 2, 1)).reshape(rows, HEADS)


def general_body(
    tokens,
    cotangent,
    memory_keys,
    memory_values,
    memory_choice,
    memory_flag,
    w_query,
    w_key,
    w_value,
    w_out,
    w_gate,
    w_up,
    w_down,
    norm_attn,
    norm_ffn,
):
    segs, rows, width = tokens.shape
    group = lax.axis_size("row")
    seg_count = lax.axis_size("seg")
    length = rows * group
    first = lax.axis_index("row") * rows
    nblocks = max(rows // QBLK, 1)
    per_block = rows // nblocks
    score_scale = HD ** (-0.5)
    shards = (w_query, w_key, w_value, w_out, w_gate, w_up, w_down, norm_attn, norm_ffn)
    wq, wk, wv, wo, wg, wu, wd, gain_one, gain_two = (
        lax.all_gather(shards[0], ("seg", "row"), axis=0, tiled=True),
        lax.all_gather(shards[1], ("seg", "row"), axis=0, tiled=True),
        lax.all_gather(shards[2], ("seg", "row"), axis=0, tiled=True),
        lax.all_gather(shards[3], ("seg", "row"), axis=0, tiled=True),
        lax.all_gather(shards[4], ("seg", "row"), axis=0, tiled=True),
        lax.all_gather(shards[5], ("seg", "row"), axis=0, tiled=True),
        lax.all_gather(shards[6], ("seg", "row"), axis=0, tiled=True),
        lax.all_gather(shards[7], ("seg", "row"), axis=0, tiled=True),
        lax.all_gather(shards[8], ("seg", "row"), axis=0, tiled=True),
    )
    gain_attn = gain_one.astype(jnp.float32)
    gain_ffn = gain_two.astype(jnp.float32)
    x = tokens.reshape(segs * rows, width).astype(jnp.float32)
    normed, inv_one = norm_apply(x, gain_attn)
    a_one = normed.astype(jnp.bfloat16)
    query = plain_dot(a_one, wq).astype(jnp.bfloat16)
    key_local = plain_dot(a_one, wk).astype(jnp.bfloat16).reshape(segs, rows, width)
    value_local = plain_dot(a_one, wv).astype(jnp.bfloat16).reshape(segs, rows, width)
    keys_all, values_all = (
        lax.all_gather(key_local, "row", axis=1, tiled=True),
        lax.all_gather(value_local, "row", axis=1, tiled=True),
    )
    block_first = first // QBLK
    chosen = lax.dynamic_slice_in_dim(memory_choice, block_first, nblocks, axis=1)
    head_col = jnp.arange(HEADS)[None, :, None]
    seg_id = 0
    memory_key_rows = memory_keys[seg_id].reshape(-1, HEADS, HD)[chosen[seg_id], head_col]
    memory_value_rows = memory_values[seg_id].reshape(-1, HEADS, HD)[chosen[seg_id], head_col]
    qseg = query.reshape(nblocks, per_block, HEADS, HD)
    keys = keys_all[seg_id].reshape(length, HEADS, HD)
    vals = values_all[seg_id].reshape(length, HEADS, HD)
    local, distant_memory = score_block(
        qseg, keys, memory_key_rows, memory_flag[seg_id], first, length
    )
    top = jnp.maximum(
        jnp.max(local, axis=-1, keepdims=True), jnp.max(distant_memory, axis=-1, keepdims=True)
    )
    summed = jnp.sum(jnp.exp(local - top), axis=-1, keepdims=True) + jnp.sum(
        jnp.exp(distant_memory - top), axis=-1, keepdims=True
    )
    total = top + jnp.log(summed)
    p_local = jnp.exp(local - total).astype(jnp.bfloat16)
    p_remote = jnp.exp(distant_memory - total).astype(jnp.bfloat16)
    attention_output = jnp.einsum(
        "bhqk,khd->bqhd", p_local, vals, preferred_element_type=jnp.float32
    )
    attention_output = attention_output + jnp.einsum(
        "bhqm,bhmd->bqhd", p_remote, memory_value_rows, preferred_element_type=jnp.float32
    )
    outputs = attention_output.reshape(rows, width)
    mem_keys = [memory_key_rows]
    mem_vals = [memory_value_rows]
    queries = [qseg]
    totals = [total]
    attended = outputs.astype(jnp.bfloat16)
    hidden_in = x + plain_dot(attended, wo)
    normed_two, inv_two = norm_apply(hidden_in, gain_ffn)
    a_two = normed_two.astype(jnp.bfloat16)
    gate = plain_dot(a_two, wg)
    up = plain_dot(a_two, wu)
    act = jax.nn.silu(gate)
    hid = (act * up).astype(jnp.bfloat16)
    layer_out = (hidden_in + plain_dot(hid, wd)).astype(jnp.bfloat16).reshape(segs, rows, width)
    wq, wk, wv, wo, wg, wu, wd, gain_one, gain_two = (
        lax.all_gather(shards[0], ("seg", "row"), axis=0, tiled=True),
        lax.all_gather(shards[1], ("seg", "row"), axis=0, tiled=True),
        lax.all_gather(shards[2], ("seg", "row"), axis=0, tiled=True),
        lax.all_gather(shards[3], ("seg", "row"), axis=0, tiled=True),
        lax.all_gather(shards[4], ("seg", "row"), axis=0, tiled=True),
        lax.all_gather(shards[5], ("seg", "row"), axis=0, tiled=True),
        lax.all_gather(shards[6], ("seg", "row"), axis=0, tiled=True),
        lax.all_gather(shards[7], ("seg", "row"), axis=0, tiled=True),
        lax.all_gather(shards[8], ("seg", "row"), axis=0, tiled=True),
    )
    gain_attn = gain_one.astype(jnp.float32)
    gain_ffn = gain_two.astype(jnp.float32)
    grad_y = cotangent.reshape(segs * rows, width)
    grad_down = dot_left(hid, grad_y)
    d_hid = dot_right(grad_y, wd)
    sig = jax.nn.sigmoid(gate)
    d_gate = (d_hid * up * sig * (1.0 + gate * (1.0 - sig))).astype(jnp.bfloat16)
    d_up = (d_hid * act).astype(jnp.bfloat16)
    grad_gate = dot_left(a_two, d_gate)
    grad_up = dot_left(a_two, d_up)
    d_a_two = dot_right(d_gate, wg) + dot_right(d_up, wu)
    d_norm_two, grad_gain_ffn = norm_back(hidden_in, gain_ffn, inv_two, d_a_two)
    d_hidden = grad_y.astype(jnp.float32) + d_norm_two
    d_proj = d_hidden.astype(jnp.bfloat16)
    grad_out = dot_left(attended, d_proj)
    d_attended = dot_right(d_proj, wo).astype(jnp.bfloat16)
    seg_id = 0
    qseg = queries[seg_id]
    keys = keys_all[seg_id].reshape(length, HEADS, HD)
    vals = values_all[seg_id].reshape(length, HEADS, HD)
    memory_key_rows = mem_keys[seg_id]
    memory_value_rows = mem_vals[seg_id]
    d_out = d_attended.reshape(nblocks, per_block, HEADS, HD)
    local, distant_memory = score_block(
        qseg, keys, memory_key_rows, memory_flag[seg_id], first, length
    )
    p_local = jnp.exp(local - totals[seg_id])
    p_remote = jnp.exp(distant_memory - totals[seg_id])
    dp_local = jnp.einsum("bqhd,khd->bhqk", d_out, vals, preferred_element_type=jnp.float32)
    dp_remote = jnp.einsum(
        "bqhd,bhmd->bhqm", d_out, memory_value_rows, preferred_element_type=jnp.float32
    )
    delta = jnp.sum(p_local * dp_local, axis=-1, keepdims=True) + jnp.sum(
        p_remote * dp_remote, axis=-1, keepdims=True
    )
    ds_local = (p_local * (dp_local - delta)).astype(jnp.bfloat16)
    ds_remote = (p_remote * (dp_remote - delta)).astype(jnp.bfloat16)
    d_query = jnp.einsum("bhqk,khd->bqhd", ds_local, keys, preferred_element_type=jnp.float32)
    d_query = (
        d_query
        + jnp.einsum(
            "bhqm,bhmd->bqhd", ds_remote, memory_key_rows, preferred_element_type=jnp.float32
        )
    ) * score_scale
    d_queries = d_query.astype(jnp.bfloat16).reshape(rows, width)
    lse_rows = [row_stat(totals[seg_id], rows)]
    delta_rows = [row_stat(delta, rows)]
    query_seg = query.reshape(segs, rows, width)
    dout_seg = d_attended.reshape(segs, rows, width)
    query_full, dout_full = (
        lax.all_gather(query_seg, "row", axis=1, tiled=True),
        lax.all_gather(dout_seg, "row", axis=1, tiled=True),
    )
    lse_full, delta_full = (
        lax.all_gather(jnp.stack(lse_rows, axis=0), "row", axis=1, tiled=True),
        lax.all_gather(jnp.stack(delta_rows, axis=0), "row", axis=1, tiled=True),
    )
    query_pos = jnp.arange(length)
    own_pos = first + jnp.arange(rows)
    visible = own_pos[None, None, :] <= query_pos[None, :, None]
    seg_id = 0
    q_whole = query_full[seg_id].reshape(length, HEADS, HD)
    o_whole = dout_full[seg_id].reshape(length, HEADS, HD)
    own_keys = key_local[seg_id].reshape(rows, HEADS, HD)
    own_vals = value_local[seg_id].reshape(rows, HEADS, HD)
    scores = (
        jnp.einsum("qhd,khd->hqk", q_whole, own_keys, preferred_element_type=jnp.float32)
        * score_scale
    )
    scores = jnp.where(visible, scores, NEG)
    softmax_weights = jnp.exp(scores - jnp.transpose(lse_full[seg_id])[:, :, None])
    d_probs = jnp.einsum("qhd,khd->hqk", o_whole, own_vals, preferred_element_type=jnp.float32)
    d_scores = (softmax_weights * (d_probs - jnp.transpose(delta_full[seg_id])[:, :, None])).astype(
        jnp.bfloat16
    )
    d_key = (
        jnp.einsum("hqk,qhd->khd", d_scores, q_whole, preferred_element_type=jnp.float32)
        * score_scale
    )
    d_val = jnp.einsum(
        "hqk,qhd->khd",
        softmax_weights.astype(jnp.bfloat16),
        o_whole,
        preferred_element_type=jnp.float32,
    )
    key_parts = d_key.reshape(rows, width)
    value_parts = d_val.reshape(rows, width)
    d_key_all = key_parts.astype(jnp.bfloat16)
    d_value_all = value_parts.astype(jnp.bfloat16)
    grad_query = dot_left(a_one, d_queries)
    grad_key = dot_left(a_one, d_key_all)
    grad_value = dot_left(a_one, d_value_all)
    d_a_one = dot_right(d_queries, wq) + dot_right(d_key_all, wk) + dot_right(d_value_all, wv)
    d_norm_one, grad_gain_attn = norm_back(x, gain_attn, inv_one, d_a_one)
    grad_tokens = (d_hidden + d_norm_one).astype(jnp.bfloat16).reshape(segs, rows, width)
    full_grads = (
        grad_query,
        grad_key,
        grad_value,
        grad_out,
        grad_gate,
        grad_up,
        grad_down,
        grad_gain_attn,
        grad_gain_ffn,
    )
    split_grads = tuple((g.reshape(seg_count, group, -1) for g in full_grads))
    row_summed = jax.tree.map(
        lambda part: part.astype(jnp.float32),
        lax.psum_scatter(for_sending(split_grads), "row", scatter_dimension=1, tiled=True),
    )
    owned_flat = jax.tree.map(
        lambda part: part.astype(jnp.float32),
        lax.psum_scatter(for_sending(row_summed), "seg", scatter_dimension=0, tiled=True),
    )
    owned = []
    for whole_grad, piece in zip(full_grads, owned_flat):
        own_rows = whole_grad.shape[0] // (seg_count * group)
        owned.append(piece.reshape((own_rows,) + whole_grad.shape[1:]))
    return (
        layer_out,
        grad_tokens,
        owned[0],
        owned[1],
        owned[2],
        owned[3],
        owned[4],
        owned[5],
        owned[6],
        owned[7],
        owned[8],
    )


MESH = pl.DeviceIdType.MESH
BF = jnp.bfloat16
F32 = jnp.float32
VM = pltpu.VMEM
DMA = pltpu.SemaphoreType.DMA


def device(z, y, c, x):
    return ((z * 2 + y) * 2 + c, x)


def remote(src, dst, send, recv, where):
    return pltpu.make_async_remote_copy(
        src_ref=src, dst_ref=dst, send_sem=send, recv_sem=recv, device_id=where, device_id_type=MESH
    )


def aligned(value, unit):
    return pl.multiple_of(value, unit)


def layer_kernel(
    tok, cot, mem_k, mem_v, choice, flag, w_q, w_k, w_v, w_o, w_b, w_d, gains,
    out_y, out_x, out_q, out_k, out_v, out_o, out_b, out_d, out_g,
    wa, wo, wb, wc, w_land, gc, go, c_a, c_o, c_b, c_d, y_a, y_o, y_b, y_d, z_a, z_o, z_b, z_d, x_n, x_d,
    xf, dyf, act, tr, qkv, aof, h, hid, dgu, part, swap_r, swap_s, dqkv, kv_acc, mk, mv, tr_one, lse,
    row_s, row_r, gain, gain_acc,
    own_s, xs, xr, zs, zr, ys, yr, cs, cr, mem_s, es, er, rcs, rcr, rys, ryr, rzs, rzr, rxs, rxr,
):
    seg = lax.axis_index("seg")
    x = lax.axis_index("row")
    c = seg % 2
    y = (seg // 2) % 2
    z = seg // 4
    rows, width = tok.shape
    length = 2 * rows
    cols = width // 2
    heads = cols // HD
    own, peer = aligned(x * rows, rows), aligned((1 - x) * rows, rows)
    ff = wc.shape[0]
    blk = wc.shape[0] // 8
    scale = HD ** (-0.5)
    over_x, over_y, over_c = device(z, y, c, 1 - x), device(z, 1 - y, c, x), device(z, y, 1 - c, x)
    mine = x == c
    other = jnp.logical_not(mine)
    col0 = aligned(x * cols, cols)

    barrier = pltpu.get_barrier_semaphore()
    for d in range(1, 4):
        pl.semaphore_signal(barrier, inc=1, device_id=device((z + d) % 4, y, c, x), device_id_type=MESH)
    for near in (over_x, over_y, over_c):
        pl.semaphore_signal(barrier, inc=1, device_id=near, device_id_type=MESH)
    pl.semaphore_wait(barrier, 6)

    def chunk(n):
        return [(i, min(512, n - i)) for i in range(0, n, 512)]

    groups = [(wa, 0, 512), (wa, 512, 512), (wa, 1024, 640)]
    groups += [(wo, i, n) for i, n in chunk(width)] + [(wb, i, n) for i, n in chunk(2 * ff)]
    n_groups = len(groups)

    def block(g, zz, yy):
        if g >= n_groups:
            p = zz * 2 + yy
            return wc.at[pl.ds(aligned(p * blk, 16), blk), pl.ds((g - n_groups) * 512, 512)]
        ref, at, n = groups[g]
        return ref.at[zz, yy, c, :, pl.ds(at, n)]

    def part_of(g, which):
        peer_half = aligned(which * cols, cols)
        if g < 3:
            return [w_q, w_k, w_v][g].at[:, pl.ds(peer_half, cols)]
        ref, at, n = groups[g]
        return w_o.at[:, pl.ds(at, n)] if ref is wo else w_b.at[which, :, pl.ds(at, n)]

    def my_rows(g):
        ref, at, n = groups[g]
        n = min(n, 512)
        return ref.at[z, y, c, pl.ds(aligned(x * 32, 32), 32), pl.ds(at, n)]

    my_gain = wa.at[z, y, c, pl.ds(aligned(x * 32, 32), 32), pl.ds(3 * cols, 128)]
    my_down = w_land.at[x]
    gx, tx, dx, cx = n_groups, n_groups + 1, n_groups + 2, n_groups + 3
    first = [remote(part_of(g, 1 - x), my_rows(g), xs.at[g], xr.at[g], over_x) for g in range(n_groups)]
    local = [pltpu.make_async_copy(part_of(g, x), my_rows(g), own_s.at[g]) for g in range(n_groups)]
    first.append(remote(gains, my_gain, xs.at[gx], xr.at[gx], over_x))
    local.append(pltpu.make_async_copy(gains, my_gain, own_s.at[gx]))
    first.append(remote(tok, xf.at[pl.ds(own, rows)], xs.at[tx], xr.at[tx], over_x))
    local.append(pltpu.make_async_copy(tok, xf.at[pl.ds(own, rows)], own_s.at[tx]))
    first.append(remote(cot, dyf.at[pl.ds(own, rows)], xs.at[dx], xr.at[dx], over_x))
    local.append(pltpu.make_async_copy(cot, dyf.at[pl.ds(own, rows)], own_s.at[dx]))
    down_x = remote(w_d, my_down, xs.at[cx], xr.at[cx], over_x)
    down_l = pltpu.make_async_copy(w_d, my_down, own_s.at[cx])

    def to_z(g, d):
        b = block(g, z, y)
        return remote(b, b, zs.at[g, d - 1], zr.at[g, d - 1], device((z + d) % 4, y, c, x))

    def to_y(g, d):
        b = block(g, (z + 4 - d) % 4, y)
        return remote(b, b, ys.at[g, d], yr.at[g, d], over_y)

    def to_c(g, d, f):
        b = block(g, (z + 4 - d) % 4, (y + f) % 2)
        return remote(b, b, cs.at[g, d, f], cr.at[g, d, f], over_c)

    def gated(fn):
        def run(g, *rest):
            if g >= n_groups:
                pl.when(mine)(lambda: fn(g, *rest))
            else:
                fn(g, *rest)

        return run

    @gated
    def spread(g):
        if g < n_groups:
            first[g].wait_recv()
            local[g].wait()
            if g == 2:
                first[gx].wait_recv()
                local[gx].wait()
        elif g == n_groups:
            down_x.wait_recv()
            down_l.wait()
            pair = jnp.concatenate([w_land[0].astype(F32), w_land[1].astype(F32)], axis=0)
            wc[pl.ds(aligned((z * 2 + y) * blk, 16), blk)] = pair.astype(BF)
        for d in range(1, 4):
            to_z(g, d).start()
        to_y(g, 0).start()
        to_c(g, 0, 0).start()

    @gated
    def pass_z(g):
        for d in range(1, 4):
            to_z(g, d).wait_recv()
            to_y(g, d).start()
            to_c(g, d, 0).start()

    @gated
    def pass_y(g):
        for d in range(4):
            to_y(g, d).wait_recv()
            to_c(g, d, 1).start()

    def arrived(g):
        for d in range(4):
            for f in range(2):
                to_c(g, d, f).wait_recv()

    @gated
    def sent(g):
        for d in range(1, 4):
            to_z(g, d).wait_send()
        for d in range(4):
            to_y(g, d).wait_send()
            for f in range(2):
                to_c(g, d, f).wait_send()

    last_group = n_groups + 1

    def step(g):
        if g <= last_group:
            pass_z(g)
        if g + 2 <= last_group:
            spread(g + 2)
        if 1 <= g <= last_group + 1:
            pass_y(g - 1)

    for g in (0, 1, 2, gx):
        first[g].start()
        local[g].start()
    local[tx].start()
    local[dx].start()
    mem_bufs = [dqkv, hid]
    n_mem = mem_k.shape[0] // length

    def mem_copy(i):
        buf = mem_bufs[i % 2]
        return [
            pltpu.make_async_copy(
                m.at[pl.ds(i * length, length), pl.ds(aligned(col0 + hh * HD, HD), HD)],
                buf.at[:, pl.ds((hh * 2 + j) * HD, HD)],
                mem_s.at[i % 2, hh * 2 + j],
            )
            for hh in range(heads)
            for j, m in enumerate((mem_k, mem_v))
        ]

    for i in range(2):
        for cp in mem_copy(i):
            cp.start()
    spread(0)
    spread(1)
    for g in list(range(3, n_groups)):
        first[g].start()
        local[g].start()

    @pl.when(mine)
    def _():
        down_l.start()

    @pl.when(other)
    def _():
        down_x.start()

    first[tx].start()

    def choose(i):
        for cp in mem_copy(i):
            cp.wait()
        at = lax.broadcasted_iota(jnp.int32, (HD, length), 1) + i * length
        for hh in range(heads):
            picked = jnp.where(x == 0, choice[:, hh : hh + 1], choice[:, heads + hh : heads + hh + 1])
            hot = (picked == at).astype(F32).astype(BF)
            both = plain_dot(hot, mem_bufs[i % 2][:, hh * 2 * HD : (hh + 1) * 2 * HD])
            where = slice(hh * HD, (hh + 1) * HD)
            if i == 0:
                kv_acc[0, where, 0 : 2 * HD] = both
            else:
                kv_acc[0, where, 0 : 2 * HD] += both
        if i + 2 < n_mem:
            for cp in mem_copy(i + 2):
                cp.start()

    done = 0
    for g in range(4):
        upto = n_mem * (g + 1) // 4
        for i in range(done, upto):
            choose(i)
        done = upto
        step(g)
        if g == 2:
            first[tx].wait_recv()
            local[tx].wait()
            first[dx].start()
    for hh in range(heads):
        where = slice(hh * HD, (hh + 1) * HD)
        mk[:, where] = kv_acc[0, where, 0:HD].astype(BF)
        mv[:, where] = kv_acc[0, where, HD : 2 * HD].astype(BF)
    for g in range(3):
        arrived(g)

    @pl.loop(0, 8)
    def _(p):
        block_t = jnp.transpose(
            wa[p // 2, p % 2, :, :, 3 * cols : 3 * cols + 128].reshape(128, 128).astype(F32)
        )
        gain[:, pl.ds(aligned(p * 128, 128), 128)] = block_t[0:8]

    def norm_rows(at, n):
        xc = xf[pl.ds(at, n)].astype(F32)
        inv = lax.rsqrt(jnp.mean(xc * xc, axis=-1, keepdims=True) + EPS)
        return xc * inv, inv

    def norm_one(i):
        at = aligned(i * 64, 64)
        u, _ = norm_rows(at, 64)
        return at, (u * gain[0:1]).astype(BF)

    @pl.loop(0, length // 64)
    def _(i):
        at, a = norm_one(i)
        act[pl.ds(at, 64)] = a

    def w_cols(ref, at, n):
        return ref[:, :, :, :, pl.ds(at, n)].reshape(width, n)

    @pl.loop(0, 3 * cols // 256)
    def _(i):
        at = aligned(i * 256, 256)
        qkv[:, pl.ds(at, 256)] = plain_dot(act[...], w_cols(wa, at, 256)).astype(BF)

    def scores(hh, i, n):
        lane = pl.ds(aligned(hh * HD, HD), HD)
        query = qkv[i * HD : (i + 1) * HD, lane]
        key = qkv[0:n, pl.ds(aligned(cols + hh * HD, HD), HD)]
        local_s = dot_right(query, key) * scale
        seen = lax.broadcasted_iota(jnp.int32, (HD, n), 1) <= lax.broadcasted_iota(jnp.int32, (HD, n), 0) + i * HD
        local_s = jnp.where(seen, local_s, NEG)
        far = dot_right(query, mk[:, lane]) * scale
        far = jnp.where(flag[0:1] > 0, far, NEG)
        return query, key, local_s, far, lane

    def value_of(hh, n):
        return qkv[0:n, pl.ds(aligned(2 * cols + hh * HD, HD), HD)]

    def att_copy(i):
        part_ref = aof.at[pl.ds(i * HD, HD), pl.ds(col0, cols)]
        return remote(part_ref, part_ref, es.at[i], er.at[i], over_x)

    n_q = length // HD

    def attend(i):
        n = (i + 1) * HD

        for hh in range(heads):
            _, _, local_s, far, lane = scores(hh, i, n)
            top = jnp.maximum(jnp.max(local_s, axis=-1, keepdims=True), jnp.max(far, axis=-1, keepdims=True))
            local_e, far_e = jnp.exp(local_s - top), jnp.exp(far - top)
            total = jnp.sum(local_e, axis=-1, keepdims=True) + jnp.sum(far_e, axis=-1, keepdims=True)
            inv = 1.0 / total
            lse[i * HD : (i + 1) * HD, hh : hh + 1] = top + jnp.log(total)
            out = plain_dot((local_e * inv).astype(BF), value_of(hh, n)) + plain_dot((far_e * inv).astype(BF), mv[:, lane])
            aof[i * HD : (i + 1) * HD, pl.ds(aligned(col0 + hh * HD, HD), HD)] = out.astype(BF)

        att_copy(i).start()

    for i in range(n_q):
        attend(i)
        if i == 0:
            step(4)
        if i == 2:
            step(5)

    @pl.loop(0, n_q)
    def _(i):
        at = aligned(i * HD, HD)
        tr_one[:, pl.ds(at, HD)] = jnp.transpose(act[pl.ds(at, HD)])

    step(6)
    arrived(3)
    arrived(4)
    for i in range(n_q):
        att_copy(i).wait_recv()

    @pl.loop(0, width // 256)
    def _(i):
        at = aligned(i * 256, 256)
        h[:, pl.ds(at, 256)] = xf[:, pl.ds(at, 256)].astype(F32) + plain_dot(aof[...], w_cols(wo, at, 256))

    @pl.loop(0, length // 64)
    def _(i):
        at = aligned(i * 64, 64)
        hc = h[pl.ds(at, 64)]
        inv = lax.rsqrt(jnp.mean(hc * hc, axis=-1, keepdims=True) + EPS)
        act[pl.ds(at, 64)] = (hc * inv * gain[1:2]).astype(BF)

    def up_tile(j):
        at = aligned(j * 256, 256)
        both = plain_dot(act[...], w_cols(wb, at, 256))
        gate, up = both[:, :128], both[:, 128:]
        sig = 1.0 / (1.0 + jnp.exp(-gate))
        silu = gate * sig
        tile = (silu * up).astype(BF)
        lanes = pl.ds(aligned(j * 128, 128), 128)
        hid[:, lanes] = tile
        tr[lanes] = jnp.transpose(tile)
        dgu[:, pl.ds(at, 128)] = (up * sig * (1.0 + gate * (1.0 - sig))).astype(BF)
        dgu[:, pl.ds(aligned(at + 128, 128), 128)] = silu.astype(BF)

    for g in range(5, n_groups):
        if g > 5:
            step(g + 1)
        arrived(g)
        pl.loop((g - 5) * 2, (g - 5) * 2 + groups[g][2] // 256)(up_tile)

    first[dx].wait_recv()
    local[dx].wait()

    red = [(None, c_d, y_d, z_d, 0, 512), (None, c_d, y_d, z_d, 512, 512)]
    red += [(wb, c_b, y_b, z_b, i, n) for i, n in chunk(2 * ff)]
    red += [(go, c_o, y_o, z_o, 0, 512)]
    red += [(wo, c_a, y_a, z_a, 0, 512), (wo, c_a, y_a, z_a, 512, 512), (wa, c_a, y_a, z_a, 1024, 640)]
    n_red = len(red)
    x_at = [0, 512]
    for g in range(2, n_red):
        x_at.append(sum(red[i][5] for i in range(2, g)))

    def red_c(g):
        src, cb, _, _, at, n = red[g]
        lanes = pl.ds(at, n)
        source = gc.at[:, :, :, lanes] if g < 2 else src.at[:, :, 1 - c, :, lanes]
        return remote(source, cb.at[:, :, :, lanes], rcs.at[g], rcr.at[g], over_c)

    def red_y(g):
        _, cb, yb, _, at, n = red[g]
        lanes = pl.ds(at, n)
        return remote(cb.at[:, 1 - y, :, lanes], yb.at[:, :, lanes], rys.at[g], ryr.at[g], over_y)

    def red_z(g, d):
        _, _, yb, zb, at, n = red[g]
        lanes = pl.ds(at, n)
        zz = (z + d) % 4
        return remote(
            yb.at[zz, :, lanes], zb.at[d - 1, :, lanes], rzs.at[g, d - 1], rzr.at[g, d - 1], device(zz, y, c, x)
        )

    def red_x(g):
        lanes = pl.ds(x_at[g], red[g][5])
        buf = x_d if g < 2 else x_n
        return remote(buf.at[0, :, lanes], buf.at[1, :, lanes], rxs.at[g], rxr.at[g], over_x)

    def only_mine(fn):
        def run(g):
            if g < 2:
                pl.when(mine)(lambda: fn(g))
            else:
                fn(g)

        return run

    def start_c(g):
        if g < 2:
            pl.when(other)(lambda: red_c(g).start())
        else:
            red_c(g).start()

    @only_mine
    def sum_c(g):
        red_c(g).wait_recv()
        src, cb, _, _, at, n = red[g]
        lanes = pl.ds(at, n)

        @pl.loop(0, 8)
        def _(i):
            own = gc[i // 2, i % 2, :, lanes] if g < 2 else src[i // 2, i % 2, c, :, lanes]
            cb[i // 2, i % 2, :, lanes] = (cb[i // 2, i % 2, :, lanes].astype(F32) + own.astype(F32)).astype(BF)

        red_y(g).start()

    @only_mine
    def sum_y(g):
        red_y(g).wait_recv()
        _, cb, yb, _, at, n = red[g]
        lanes = pl.ds(at, n)

        @pl.loop(0, 4)
        def _(i):
            yb[i, :, lanes] = (yb[i, :, lanes].astype(F32) + cb[i, y, :, lanes].astype(F32)).astype(BF)

        for d in range(1, 4):
            red_z(g, d).start()

    def result(g, which, value):
        at, n = red[g][4], red[g][5]
        if g < 2:
            out_d[:, at : at + n] = value
        elif g < n_red - 4:
            out_b[which, :, at : at + n] = value
        else:
            out = [out_o, out_q, out_k, out_v][g - (n_red - 4)]
            out[:, pl.ds(aligned(which * cols, cols), cols)] = value[:, :cols]
            if n > cols:
                out_g[which] = value[:, cols:]

    @only_mine
    def sum_z(g):
        for d in range(1, 4):
            red_z(g, d).wait_recv()
        _, _, yb, zb, at, n = red[g]
        lanes = pl.ds(at, n)
        size = yb.shape[1] // 2
        total = yb[z, :, lanes].astype(F32)
        for d in range(3):
            total = total + zb[d, :, lanes].astype(F32)
        low, high = total[:size], total[size:]
        buf = x_d if g < 2 else x_n
        buf[0, :, pl.ds(x_at[g], n)] = jnp.where(x == 0, high, low).astype(BF)
        red_x(g).start()
        result(g, x, jnp.where(x == 0, low, high))

    def finish(g):
        lanes = pl.ds(x_at[g], red[g][5])

        def take():
            red_x(g).wait_recv()
            result(g, 1 - x, (x_d if g < 2 else x_n)[1, :, lanes].astype(F32))

        if g < 2:
            pl.when(other)(take)
        else:
            take()

    @only_mine
    def red_sent(g):
        red_y(g).wait_send()
        for d in range(1, 4):
            red_z(g, d).wait_send()
        red_x(g).wait_send()

    def tick(k):
        if 4 <= k < n_red:
            sum_c(k)
        if 2 <= k - 2 < n_red:
            sum_y(k - 2)
        if 0 <= k - 4 < n_red:
            sum_z(k - 4)
        if 0 <= k - 5 < n_red:
            finish(k - 5)

    for i in range(2):

        @pl.loop(0, 4)
        def _(t):
            res = plain_dot(tr[pl.ds(aligned(t * 2 * blk, 32), 2 * blk)], dyf[:, i * 512 : (i + 1) * 512])
            gc[t, :, :, i * 512 : (i + 1) * 512] = res.reshape(2, blk, 512).astype(BF)

        start_c(i)
        step(n_groups + 1 + i)
        sum_c(i)

    def wait_down():
        for g in range(n_groups, last_group + 1):
            arrived(g)

    pl.when(other)(wait_down)

    def dhid_tile(j, n):
        lanes = aligned(j * 128, 128)
        res = dot_right(dyf[...], wc[pl.ds(lanes, 128 * n)])
        for t in range(n):
            at = aligned((j + t) * 256, 256)
            d = res[:, t * 128 : (t + 1) * 128]
            for s in range(2):
                where = pl.ds(aligned(at + 128 * s, 128), 128)
                dgu[:, where] = (d * dgu[:, where].astype(F32)).astype(BF)

    n_tiles = ff // 128

    @pl.loop(0, n_tiles // 2)
    def _(t):
        dhid_tile(t * 2, 2)

    if n_tiles % 2:
        dhid_tile(n_tiles - 1, 1)

    gain_acc[...] = jnp.zeros_like(gain_acc)

    def swap_copy(i):
        at = pl.ds(128 * i, 128)
        return remote(swap_s.at[at], swap_r.at[at], es.at[8 + i], er.at[8 + i], over_x)

    for f in range(2):

        @pl.loop(0, width // 256)
        def _(i):
            at = aligned(i * 256, 256)
            res = dot_right(dgu[f * rows : (f + 1) * rows], wb[i, :, :, :, :].reshape(256, 2 * ff))
            part[f * rows : (f + 1) * rows, pl.ds(at, 256)] = res
            swap_s[f * rows : (f + 1) * rows, pl.ds(at, 256)] = res.astype(BF)

        swap_copy(2 * f).start()
        swap_copy(2 * f + 1).start()

    @pl.loop(0, width // 256)
    def _(i):
        at = aligned(i * 256, 256)
        row_s[:, pl.ds(at, 256)] = plain_dot(hid[pl.ds(peer, rows)], wc[:, pl.ds(at, 256)]).astype(BF)

    row_y = remote(row_s, row_r.at[0], es.at[12], er.at[12], over_x)
    row_y.start()

    @pl.loop(0, length // 128)
    def _(i):
        at = aligned(i * 128, 128)
        tr[0:width, pl.ds(at, 128)] = jnp.transpose(act[pl.ds(at, 128)])

    def add_gain(k, grad, unit):
        prod = grad * unit
        gain_acc[k] += jnp.sum(prod.reshape(prod.shape[0] // 8, 8, width), axis=0)

    @pl.loop(0, length // 64)
    def _(i):
        at = aligned(i * 64, 64)
        hc = h[pl.ds(at, 64)]
        inv = lax.rsqrt(jnp.mean(hc * hc, axis=-1, keepdims=True) + EPS)
        add_gain(1, part[pl.ds(at, 64)], hc * inv)

    def grad_tile(dst, lhs_rows, value, at):
        res = plain_dot(tr[0:lhs_rows], value)
        dst[:, :, :, :, pl.ds(at, 256)] = res.reshape(4, 2, 2, 64, 256).astype(BF)

    n_b = len(chunk(2 * ff))
    for g in range(5, n_groups):
        sent(g)
    for g in range(n_b):
        at0, n = red[2 + g][4], red[2 + g][5]
        for t in range(n // 256):
            grad_tile(wb, width, dgu[:, at0 + t * 256 : at0 + (t + 1) * 256], at0 + t * 256)
        start_c(2 + g)
        if g == 1:
            sum_y(0)
        if g == 2:
            sum_c(2)
        if g == 4:
            sum_y(1)
            sum_c(3)

    def d_hidden_rows(i):
        at = aligned(i * 64, 64)
        hc = h[pl.ds(at, 64)]
        inv = lax.rsqrt(jnp.mean(hc * hc, axis=-1, keepdims=True) + EPS)
        u = hc * inv
        e = (part[pl.ds(at, 64)] + swap_r[pl.ds(at, 64)].astype(F32)) * gain[1:2]
        dh = dyf[pl.ds(at, 64)].astype(F32) + inv * (e - u * jnp.mean(e * u, axis=-1, keepdims=True))
        part[pl.ds(at, 64)] = dh
        act[pl.ds(at, 64)] = dh.astype(BF)

    kv_acc[...] = jnp.zeros_like(kv_acc)
    w_own = wo.at[pl.ds(x * 2, 2)]

    def attend_back(i):
        n = (i + 1) * HD
        at = slice(i * HD, (i + 1) * HD)
        d_att = dot_right(act[at], w_own[...].reshape(cols, width)).astype(BF)
        for hh in range(heads):
            query, key, local_s, far, lane = scores(hh, i, n)
            log_sum = lse[at, hh : hh + 1]
            p_l, p_m = jnp.exp(local_s - log_sum), jnp.exp(far - log_sum)
            grad = d_att[:, hh * HD : (hh + 1) * HD]
            out = aof[at, pl.ds(aligned(col0 + hh * HD, HD), HD)]
            delta = jnp.sum(grad.astype(F32) * out.astype(F32), axis=-1, keepdims=True)
            ds_l = (p_l * (dot_right(grad, value_of(hh, n)) - delta)).astype(BF)
            ds_m = (p_m * (dot_right(grad, mv[:, lane]) - delta)).astype(BF)
            dq = (plain_dot(ds_l, key) + plain_dot(ds_m, mk[:, lane])) * scale
            dqkv[at, hh * HD : (hh + 1) * HD] = dq.astype(BF)
            kv_acc[0, 0:n, hh * HD : (hh + 1) * HD] += dot_left(ds_l, query)
            kv_acc[1, 0:n, hh * HD : (hh + 1) * HD] += dot_left(p_l.astype(BF), grad)

    @pl.loop(0, length // 128)
    def _(i):
        at = aligned(i * 128, 128)
        tr[0:width, pl.ds(at, 128)] = jnp.transpose(aof[pl.ds(at, 128)])

    base = 4
    for i in range(n_q):
        swap_copy(i).wait_recv()
        pl.loop(i * 2, i * 2 + 2)(d_hidden_rows)
        attend_back(i)
        tick(base)
        base += 1
    for g in (3, 4):
        sent(g)
    dqkv[:, cols : 2 * cols] = (kv_acc[0] * scale).astype(BF)
    dqkv[:, 2 * cols :] = kv_acc[1].astype(BF)

    def grad_tile_one(dst, at, to):
        res = plain_dot(tr_one[...], dqkv[:, at : at + 256])
        dst[:, :, :, :, to : to + 256] = res.reshape(4, 2, 2, 64, 256).astype(BF)

    for t in range(2):
        grad_tile(go, width, act[:, pl.ds(aligned(col0 + t * 256, 256), 256)], t * 256)
    start_c(2 + n_b)
    for g in range(2):
        for t in range(2):
            grad_tile_one(wo, g * cols + t * 256, g * cols + t * 256)
        start_c(3 + n_b + g)

    row_y.wait_recv()

    @pl.loop(0, width // 256)
    def _(i):
        at = aligned(i * 256, 256)
        mine_y = plain_dot(hid[pl.ds(own, rows)], wc[:, pl.ds(at, 256)]) + h[pl.ds(own, rows), pl.ds(at, 256)]
        out_y[:, pl.ds(at, 256)] = (mine_y + row_r[0, :, pl.ds(at, 256)].astype(F32)).astype(BF)
    row_y.wait_send()
    for first_half in (False, True):
        half_rows = pl.ds(own if first_half else peer, rows)

        @pl.loop(0, width // 256)
        def _(i):
            at = aligned(i * 256, 256)
            res = dot_right(dqkv[half_rows], wa[i, :, :, :, 0 : 3 * cols].reshape(256, 3 * cols))
            if not first_half:
                row_s[:, pl.ds(at, 256)] = res.astype(BF)
            h[half_rows, pl.ds(at, 256)] = res

        if not first_half:
            row_x = remote(row_s, row_r.at[1], es.at[13], er.at[13], over_x)
            row_x.start()

    @pl.loop(0, length // 64)
    def _(i):
        at = aligned(i * 64, 64)
        u, _ = norm_rows(at, 64)
        add_gain(0, h[pl.ds(at, 64)], u)

    for g in range(3):
        sent(g)
    sums = [jnp.sum(gain_acc[k], axis=0, keepdims=True) for k in range(2)]
    tall = lax.broadcasted_iota(jnp.int32, (128, 128), 0)
    for p in range(8):
        lanes = slice(p * 128, (p + 1) * 128)
        both = jnp.where(tall == 0, sums[0][:, lanes], jnp.where(tall == 1, sums[1][:, lanes], 0.0))
        wa[p // 2, p % 2, :, :, 3 * cols :] = jnp.transpose(both).reshape(2, 64, 128).astype(BF)
    for t in range(2):
        grad_tile_one(wa, 2 * cols + t * 256, 2 * cols + t * 256)
    start_c(5 + n_b)
    tick(base)
    base += 1
    row_x.wait_recv()

    @pl.loop(0, rows // 64)
    def _(i):
        at = aligned(own + i * 64, 64)
        u, inv = norm_rows(at, 64)
        e = (h[pl.ds(at, 64)] + row_r[1, pl.ds(aligned(i * 64, 64), 64)].astype(F32)) * gain[0:1]
        out = part[pl.ds(at, 64)] + inv * (e - u * jnp.mean(e * u, axis=-1, keepdims=True))
        out_x[pl.ds(aligned(i * 64, 64), 64)] = out.astype(BF)

    for k in range(base, n_red + 5):
        tick(k)
    for cp in first:
        cp.wait_send()
    pl.when(other)(lambda: down_x.wait_send())
    for g in range(n_groups, last_group + 1):
        sent(g)
    for i in range(4):
        swap_copy(i).wait_send()
    for i in range(n_q):
        att_copy(i).wait_send()
    row_x.wait_send()
    for g in range(n_red):
        if g < 2:
            pl.when(other)(lambda: red_c(g).wait_send())
        else:
            red_c(g).wait_send()
        red_sent(g)


def layer(tok, cot, mem_k, mem_v, choice, flag, w_q, w_k, w_v, w_o, w_b, w_d, gains):
    rows, width = tok.shape
    length = 2 * rows
    cols = width // 2
    ff2 = w_b.shape[2]
    ff = ff2 // 2
    blk = ff // 8
    na = 3 * cols + 128
    hbm, vm = pl.BlockSpec(memory_space=pl.ANY), pl.BlockSpec(memory_space=pltpu.VMEM)
    own = w_q.shape[0]
    shape = jax.ShapeDtypeStruct
    return pl.pallas_call(
        layer_kernel,
        name="layer",
        out_shape=(
            shape((rows, width), BF),
            shape((rows, width), BF),
            shape((own, width), F32),
            shape((own, width), F32),
            shape((own, width), F32),
            shape((own, width), F32),
            shape((2, own, ff2), F32),
            shape((blk // 2, width), F32),
            shape((2, own, 128), F32),
        ),
        in_specs=[hbm] * 4 + [vm] * 2 + [hbm] * 7,
        out_specs=(vm,) * 9,
        scratch_shapes=[
            VM((4, 2, 2, 64, na), BF), VM((4, 2, 2, 64, width), BF), VM((4, 2, 2, 64, ff2), BF), VM((ff, width), BF), VM((2, blk // 2, width), BF),
            VM((4, 2, blk, width), BF), VM((4, 2, 2, 64, cols), BF),
            VM((4, 2, 64, na), BF), VM((4, 2, 64, cols), BF), VM((4, 2, 64, ff2), BF), VM((4, 2, blk, width), BF),
            VM((4, 64, na), BF), VM((4, 64, cols), BF), VM((4, 64, ff2), BF), VM((4, blk, width), BF),
            VM((3, 64, na), BF), VM((3, 64, cols), BF), VM((3, 64, ff2), BF), VM((3, blk, width), BF),
            VM((2, own, ff2 + na + cols), BF), VM((2, blk // 2, width), BF),
            VM((length, width), BF), VM((length, width), BF), VM((length, width), BF), VM((ff, length), BF),
            VM((length, 3 * cols), BF), VM((length, width), BF), VM((length, width), F32), VM((length, ff), BF),
            VM((length, ff2), BF), VM((length, width), F32), VM((length, width), BF), VM((length, width), BF),
            VM((length, 3 * cols), BF), VM((2, length, cols), F32), VM((HD, cols), BF), VM((HD, cols), BF),
            VM((width, length), BF), VM((length, 128), F32),
            VM((rows, width), BF), VM((2, rows, width), BF), VM((8, width), F32), VM((2, 8, width), F32),
            DMA((16,)), DMA((16,)), DMA((16,)), DMA((13, 3)), DMA((13, 3)), DMA((13, 4)), DMA((13, 4)),
            DMA((13, 4, 2)), DMA((13, 4, 2)), DMA((2, 8)), DMA((14,)), DMA((14,)),
            DMA((12,)), DMA((12,)), DMA((12,)), DMA((12,)), DMA((12, 3)), DMA((12, 3)), DMA((12,)), DMA((12,)),
        ],
        compiler_params=pltpu.CompilerParams(collective_id=0, has_side_effects=True, vmem_limit_bytes=63 << 20),
    )(tok, cot, mem_k, mem_v, choice, flag, w_q, w_k, w_v, w_o, w_b, w_d, gains)


def prepare_kernel(w_g, w_u, norms, choice, flag, w_b, gains, columns, flags):
    wide = w_g.shape[1]
    strip = wide // 16
    for half in range(2):
        packed = []
        for w in (w_g, w_u):
            whole = w[...].astype(F32)
            cuts = [whole[:, (2 * p + half) * strip : (2 * p + half + 1) * strip] for p in range(8)]
            packed.append(jnp.concatenate(cuts, axis=1).astype(BF))
        for j in range(wide // 256):
            for i in range(2):
                w_b[half, :, (2 * j + i) * 128 : (2 * j + i + 1) * 128] = packed[i][:, j * 128 : (j + 1) * 128]
    own = norms.shape[1]
    tall = lax.broadcasted_iota(jnp.int32, (128, own), 0)
    both = norms[...].astype(F32)
    both = jnp.where(tall == 0, both[0:1], jnp.where(tall == 1, both[1:2], 0.0))
    gains[...] = jnp.transpose(both).astype(BF)
    many = jnp.concatenate([choice[...].astype(F32)] * (128 // choice.shape[0]), axis=0)
    columns[...] = jnp.transpose(many).astype(jnp.int32)
    flags[...] = jnp.full(flags.shape, flag[0], jnp.int32)


def prepare(w_g, w_u, norms, choice, flag):
    own, wide = w_g.shape
    vm = pl.BlockSpec()
    shape = jax.ShapeDtypeStruct
    return pl.pallas_call(
        prepare_kernel,
        name="prepare",
        out_shape=(
            shape((2, own, wide), BF), shape((own, 128), BF), shape((128, 128), jnp.int32), shape((8, 128), jnp.int32),
        ),
        in_specs=[vm] * 4 + [pl.BlockSpec(memory_space=pltpu.SMEM)],
        out_specs=(vm,) * 4,
        compiler_params=pltpu.CompilerParams(vmem_limit_bytes=63 << 20),
    )(w_g, w_u, norms, choice, flag)


def complete_kernel(i_y, i_x, i_q, i_k, i_v, i_o, i_b, i_d, i_g, y, x, q, k, v, o, g, u, d, n_a, n_f):
    for src, dst in ((i_y, y), (i_x, x), (i_q, q), (i_k, k), (i_v, v), (i_o, o), (i_d, d)):
        dst[...] = src[...]
    wide = g.shape[1]
    strip = wide // 16
    for i, dst in enumerate((g, u)):
        halves = [
            jnp.concatenate(
                [i_b[half, :, (2 * j + i) * 128 : (2 * j + i + 1) * 128] for j in range(wide // 256)], axis=1
            )
            for half in range(2)
        ]
        cuts = [halves[p % 2][:, (p // 2) * strip : (p // 2 + 1) * strip] for p in range(16)]
        dst[...] = jnp.concatenate(cuts, axis=1)
    own = n_a.shape[1]
    tall = jnp.transpose(i_g[0] + i_g[1])
    n_a[...] = tall[0:1, 0:own]
    n_f[...] = tall[1:2, 0:own]


def complete(*parts):
    own, width = parts[2].shape
    wide = parts[6].shape[2]
    vm = pl.BlockSpec()
    shape = jax.ShapeDtypeStruct
    like = [shape(p.shape, p.dtype) for p in parts[:6]]
    like += [shape((own, wide), F32)] * 2 + [shape(parts[7].shape, F32)] + [shape((1, own), F32)] * 2
    return pl.pallas_call(
        complete_kernel,
        name="complete",
        out_shape=tuple(like),
        in_specs=[vm] * 9,
        out_specs=(vm,) * 11,
        compiler_params=pltpu.CompilerParams(vmem_limit_bytes=63 << 20),
    )(*parts)


def fast_body(
    tokens, cotangent, memory_keys, memory_values, memory_choice, memory_flag,
    w_query, w_key, w_value, w_out, w_gate, w_up, w_down, norm_attn, norm_ffn,
):
    norms = jnp.stack([norm_attn, norm_ffn])
    w_b, gains, choice, flag = prepare(w_gate, w_up, norms, memory_choice[0, 0], memory_flag)
    parts = layer(
        tokens[0], cotangent[0], memory_keys[0], memory_values[0], choice, flag,
        w_query, w_key, w_value, w_out, w_b, w_down, gains,
    )
    y, x, q, k, v, o, g, u, d, n_a, n_f = complete(*parts)
    return y[None], x[None], q, k, v, o, g, u, d, n_a[0], n_f[0]


def solution(mesh):
    in_specs = (
        P("seg", "row", None),
        P("seg", "row", None),
        P("seg", None, None),
        P("seg", None, None),
        P("seg", None, None, None),
        P("seg"),
        P(("seg", "row"), None),
        P(("seg", "row"), None),
        P(("seg", "row"), None),
        P(("seg", "row"), None),
        P(("seg", "row"), None),
        P(("seg", "row"), None),
        P(("seg", "row"), None),
        P(("seg", "row")),
        P(("seg", "row")),
    )
    out_specs = (
        P("seg", "row", None),
        P("seg", "row", None),
        P(("seg", "row"), None),
        P(("seg", "row"), None),
        P(("seg", "row"), None),
        P(("seg", "row"), None),
        P(("seg", "row"), None),
        P(("seg", "row"), None),
        P(("seg", "row"), None),
        P(("seg", "row")),
        P(("seg", "row")),
    )

    def body(*args):
        segs, rows, width = args[0].shape
        fits = (
            mesh.shape["row"] == 2
            and mesh.shape["seg"] == 16
            and segs == 1
            and (rows, width) == (256, 1024)
            and args[4].shape[1] == 1
        )
        return (fast_body if fits else general_body)(*args)

    return jax.shard_map(body, mesh=mesh, in_specs=in_specs, out_specs=out_specs, check_vma=False)
```

```python
import functools

import jax
import jax.numpy as jnp
from jax import lax
from jax.experimental import pallas as pl
from jax.experimental.pallas import tpu as pltpu
from jax.sharding import PartitionSpec as P

HEADS = 8
HD = 128
QBLK = 512


EPS = 1e-06
NEG = -1000000000.0


def for_sending(array):

    def short(part):
        return part.astype(jnp.bfloat16) if part.dtype == jnp.float32 else part

    return jax.tree.map(short, array)


def plain_dot(left, right):
    return jnp.dot(left, right, preferred_element_type=jnp.float32)


def dot_left(left, right):
    return lax.dot_general(
        left, right, (((0,), (0,)), ((), ())), preferred_element_type=jnp.float32
    )


def dot_right(left, right):
    return lax.dot_general(
        left, right, (((1,), (1,)), ((), ())), preferred_element_type=jnp.float32
    )


def norm_apply(value, gain):
    inverse = lax.rsqrt(jnp.mean(value * value, axis=-1, keepdims=True) + EPS)
    return (value * inverse * gain, inverse)


def norm_back(value, gain, inverse, grad):
    unit = value * inverse
    gain_grad = jnp.sum(grad * unit, axis=0)
    scaled = grad * gain
    return (inverse * (scaled - unit * jnp.mean(scaled * unit, axis=-1, keepdims=True)), gain_grad)


def score_block(queries, keys, memory_key_rows, flag, first, length):
    score_scale = HD ** (-0.5)
    local = (
        jnp.einsum("bqhd,khd->bhqk", queries, keys, preferred_element_type=jnp.float32)
        * score_scale
    )
    distant_memory = (
        jnp.einsum("bqhd,bhmd->bhqm", queries, memory_key_rows, preferred_element_type=jnp.float32)
        * score_scale
    )
    nblocks, per_block = (queries.shape[0], queries.shape[1])
    pos = first + jnp.arange(nblocks * per_block).reshape(nblocks, 1, per_block, 1)
    key_pos = jnp.arange(length)
    local = jnp.where(key_pos[None, None, None, :] <= pos, local, NEG)
    distant_memory = jnp.where(flag > 0, distant_memory, NEG)
    return (local, distant_memory)


def row_stat(stat, rows):
    return jnp.transpose(stat[..., 0], (0, 2, 1)).reshape(rows, HEADS)


def general_body(
    tokens,
    cotangent,
    memory_keys,
    memory_values,
    memory_choice,
    memory_flag,
    w_query,
    w_key,
    w_value,
    w_out,
    w_gate,
    w_up,
    w_down,
    norm_attn,
    norm_ffn,
):
    segs, rows, width = tokens.shape
    group = lax.axis_size("row")
    seg_count = lax.axis_size("seg")
    length = rows * group
    first = lax.axis_index("row") * rows
    nblocks = max(rows // QBLK, 1)
    per_block = rows // nblocks
    score_scale = HD ** (-0.5)
    shards = (w_query, w_key, w_value, w_out, w_gate, w_up, w_down, norm_attn, norm_ffn)
    wq, wk, wv, wo, wg, wu, wd, gain_one, gain_two = (
        lax.all_gather(shards[0], ("seg", "row"), axis=0, tiled=True),
        lax.all_gather(shards[1], ("seg", "row"), axis=0, tiled=True),
        lax.all_gather(shards[2], ("seg", "row"), axis=0, tiled=True),
        lax.all_gather(shards[3], ("seg", "row"), axis=0, tiled=True),
        lax.all_gather(shards[4], ("seg", "row"), axis=0, tiled=True),
        lax.all_gather(shards[5], ("seg", "row"), axis=0, tiled=True),
        lax.all_gather(shards[6], ("seg", "row"), axis=0, tiled=True),
        lax.all_gather(shards[7], ("seg", "row"), axis=0, tiled=True),
        lax.all_gather(shards[8], ("seg", "row"), axis=0, tiled=True),
    )
    gain_attn = gain_one.astype(jnp.float32)
    gain_ffn = gain_two.astype(jnp.float32)
    x = tokens.reshape(segs * rows, width).astype(jnp.float32)
    normed, inv_one = norm_apply(x, gain_attn)
    a_one = normed.astype(jnp.bfloat16)
    query = plain_dot(a_one, wq).astype(jnp.bfloat16)
    key_local = plain_dot(a_one, wk).astype(jnp.bfloat16).reshape(segs, rows, width)
    value_local = plain_dot(a_one, wv).astype(jnp.bfloat16).reshape(segs, rows, width)
    keys_all, values_all = (
        lax.all_gather(key_local, "row", axis=1, tiled=True),
        lax.all_gather(value_local, "row", axis=1, tiled=True),
    )
    block_first = first // QBLK
    chosen = lax.dynamic_slice_in_dim(memory_choice, block_first, nblocks, axis=1)
    head_col = jnp.arange(HEADS)[None, :, None]
    seg_id = 0
    memory_key_rows = memory_keys[seg_id].reshape(-1, HEADS, HD)[chosen[seg_id], head_col]
    memory_value_rows = memory_values[seg_id].reshape(-1, HEADS, HD)[chosen[seg_id], head_col]
    qseg = query.reshape(nblocks, per_block, HEADS, HD)
    keys = keys_all[seg_id].reshape(length, HEADS, HD)
    vals = values_all[seg_id].reshape(length, HEADS, HD)
    local, distant_memory = score_block(
        qseg, keys, memory_key_rows, memory_flag[seg_id], first, length
    )
    top = jnp.maximum(
        jnp.max(local, axis=-1, keepdims=True), jnp.max(distant_memory, axis=-1, keepdims=True)
    )
    summed = jnp.sum(jnp.exp(local - top), axis=-1, keepdims=True) + jnp.sum(
        jnp.exp(distant_memory - top), axis=-1, keepdims=True
    )
    total = top + jnp.log(summed)
    p_local = jnp.exp(local - total).astype(jnp.bfloat16)
    p_remote = jnp.exp(distant_memory - total).astype(jnp.bfloat16)
    attention_output = jnp.einsum(
        "bhqk,khd->bqhd", p_local, vals, preferred_element_type=jnp.float32
    )
    attention_output = attention_output + jnp.einsum(
        "bhqm,bhmd->bqhd", p_remote, memory_value_rows, preferred_element_type=jnp.float32
    )
    outputs = attention_output.reshape(rows, width)
    mem_keys = [memory_key_rows]
    mem_vals = [memory_value_rows]
    queries = [qseg]
    totals = [total]
    attended = outputs.astype(jnp.bfloat16)
    hidden_in = x + plain_dot(attended, wo)
    normed_two, inv_two = norm_apply(hidden_in, gain_ffn)
    a_two = normed_two.astype(jnp.bfloat16)
    gate = plain_dot(a_two, wg)
    up = plain_dot(a_two, wu)
    act = jax.nn.silu(gate)
    hid = (act * up).astype(jnp.bfloat16)
    layer_out = (hidden_in + plain_dot(hid, wd)).astype(jnp.bfloat16).reshape(segs, rows, width)
    wq, wk, wv, wo, wg, wu, wd, gain_one, gain_two = (
        lax.all_gather(shards[0], ("seg", "row"), axis=0, tiled=True),
        lax.all_gather(shards[1], ("seg", "row"), axis=0, tiled=True),
        lax.all_gather(shards[2], ("seg", "row"), axis=0, tiled=True),
        lax.all_gather(shards[3], ("seg", "row"), axis=0, tiled=True),
        lax.all_gather(shards[4], ("seg", "row"), axis=0, tiled=True),
        lax.all_gather(shards[5], ("seg", "row"), axis=0, tiled=True),
        lax.all_gather(shards[6], ("seg", "row"), axis=0, tiled=True),
        lax.all_gather(shards[7], ("seg", "row"), axis=0, tiled=True),
        lax.all_gather(shards[8], ("seg", "row"), axis=0, tiled=True),
    )
    gain_attn = gain_one.astype(jnp.float32)
    gain_ffn = gain_two.astype(jnp.float32)
    grad_y = cotangent.reshape(segs * rows, width)
    grad_down = dot_left(hid, grad_y)
    d_hid = dot_right(grad_y, wd)
    sig = jax.nn.sigmoid(gate)
    d_gate = (d_hid * up * sig * (1.0 + gate * (1.0 - sig))).astype(jnp.bfloat16)
    d_up = (d_hid * act).astype(jnp.bfloat16)
    grad_gate = dot_left(a_two, d_gate)
    grad_up = dot_left(a_two, d_up)
    d_a_two = dot_right(d_gate, wg) + dot_right(d_up, wu)
    d_norm_two, grad_gain_ffn = norm_back(hidden_in, gain_ffn, inv_two, d_a_two)
    d_hidden = grad_y.astype(jnp.float32) + d_norm_two
    d_proj = d_hidden.astype(jnp.bfloat16)
    grad_out = dot_left(attended, d_proj)
    d_attended = dot_right(d_proj, wo).astype(jnp.bfloat16)
    seg_id = 0
    qseg = queries[seg_id]
    keys = keys_all[seg_id].reshape(length, HEADS, HD)
    vals = values_all[seg_id].reshape(length, HEADS, HD)
    memory_key_rows = mem_keys[seg_id]
    memory_value_rows = mem_vals[seg_id]
    d_out = d_attended.reshape(nblocks, per_block, HEADS, HD)
    local, distant_memory = score_block(
        qseg, keys, memory_key_rows, memory_flag[seg_id], first, length
    )
    p_local = jnp.exp(local - totals[seg_id])
    p_remote = jnp.exp(distant_memory - totals[seg_id])
    dp_local = jnp.einsum("bqhd,khd->bhqk", d_out, vals, preferred_element_type=jnp.float32)
    dp_remote = jnp.einsum(
        "bqhd,bhmd->bhqm", d_out, memory_value_rows, preferred_element_type=jnp.float32
    )
    delta = jnp.sum(p_local * dp_local, axis=-1, keepdims=True) + jnp.sum(
        p_remote * dp_remote, axis=-1, keepdims=True
    )
    ds_local = (p_local * (dp_local - delta)).astype(jnp.bfloat16)
    ds_remote = (p_remote * (dp_remote - delta)).astype(jnp.bfloat16)
    d_query = jnp.einsum("bhqk,khd->bqhd", ds_local, keys, preferred_element_type=jnp.float32)
    d_query = (
        d_query
        + jnp.einsum(
            "bhqm,bhmd->bqhd", ds_remote, memory_key_rows, preferred_element_type=jnp.float32
        )
    ) * score_scale
    d_queries = d_query.astype(jnp.bfloat16).reshape(rows, width)
    lse_rows = [row_stat(totals[seg_id], rows)]
    delta_rows = [row_stat(delta, rows)]
    query_seg = query.reshape(segs, rows, width)
    dout_seg = d_attended.reshape(segs, rows, width)
    query_full, dout_full = (
        lax.all_gather(query_seg, "row", axis=1, tiled=True),
        lax.all_gather(dout_seg, "row", axis=1, tiled=True),
    )
    lse_full, delta_full = (
        lax.all_gather(jnp.stack(lse_rows, axis=0), "row", axis=1, tiled=True),
        lax.all_gather(jnp.stack(delta_rows, axis=0), "row", axis=1, tiled=True),
    )
    query_pos = jnp.arange(length)
    own_pos = first + jnp.arange(rows)
    visible = own_pos[None, None, :] <= query_pos[None, :, None]
    seg_id = 0
    q_whole = query_full[seg_id].reshape(length, HEADS, HD)
    o_whole = dout_full[seg_id].reshape(length, HEADS, HD)
    own_keys = key_local[seg_id].reshape(rows, HEADS, HD)
    own_vals = value_local[seg_id].reshape(rows, HEADS, HD)
    scores = (
        jnp.einsum("qhd,khd->hqk", q_whole, own_keys, preferred_element_type=jnp.float32)
        * score_scale
    )
    scores = jnp.where(visible, scores, NEG)
    softmax_weights = jnp.exp(scores - jnp.transpose(lse_full[seg_id])[:, :, None])
    d_probs = jnp.einsum("qhd,khd->hqk", o_whole, own_vals, preferred_element_type=jnp.float32)
    d_scores = (softmax_weights * (d_probs - jnp.transpose(delta_full[seg_id])[:, :, None])).astype(
        jnp.bfloat16
    )
    d_key = (
        jnp.einsum("hqk,qhd->khd", d_scores, q_whole, preferred_element_type=jnp.float32)
        * score_scale
    )
    d_val = jnp.einsum(
        "hqk,qhd->khd",
        softmax_weights.astype(jnp.bfloat16),
        o_whole,
        preferred_element_type=jnp.float32,
    )
    key_parts = d_key.reshape(rows, width)
    value_parts = d_val.reshape(rows, width)
    d_key_all = key_parts.astype(jnp.bfloat16)
    d_value_all = value_parts.astype(jnp.bfloat16)
    grad_query = dot_left(a_one, d_queries)
    grad_key = dot_left(a_one, d_key_all)
    grad_value = dot_left(a_one, d_value_all)
    d_a_one = dot_right(d_queries, wq) + dot_right(d_key_all, wk) + dot_right(d_value_all, wv)
    d_norm_one, grad_gain_attn = norm_back(x, gain_attn, inv_one, d_a_one)
    grad_tokens = (d_hidden + d_norm_one).astype(jnp.bfloat16).reshape(segs, rows, width)
    full_grads = (
        grad_query,
        grad_key,
        grad_value,
        grad_out,
        grad_gate,
        grad_up,
        grad_down,
        grad_gain_attn,
        grad_gain_ffn,
    )
    split_grads = tuple((g.reshape(seg_count, group, -1) for g in full_grads))
    row_summed = jax.tree.map(
        lambda part: part.astype(jnp.float32),
        lax.psum_scatter(for_sending(split_grads), "row", scatter_dimension=1, tiled=True),
    )
    owned_flat = jax.tree.map(
        lambda part: part.astype(jnp.float32),
        lax.psum_scatter(for_sending(row_summed), "seg", scatter_dimension=0, tiled=True),
    )
    owned = []
    for whole_grad, piece in zip(full_grads, owned_flat):
        own_rows = whole_grad.shape[0] // (seg_count * group)
        owned.append(piece.reshape((own_rows,) + whole_grad.shape[1:]))
    return (
        layer_out,
        grad_tokens,
        owned[0],
        owned[1],
        owned[2],
        owned[3],
        owned[4],
        owned[5],
        owned[6],
        owned[7],
        owned[8],
    )


MESH = pl.DeviceIdType.MESH
BF = jnp.bfloat16
F32 = jnp.float32
VM = pltpu.VMEM
DMA = pltpu.SemaphoreType.DMA


def device(z, y, c, x):
    return ((z * 2 + y) * 2 + c, x)


def remote(src, dst, send, recv, where):
    return pltpu.make_async_remote_copy(
        src_ref=src, dst_ref=dst, send_sem=send, recv_sem=recv, device_id=where, device_id_type=MESH
    )


def aligned(value, unit):
    return pl.multiple_of(value, unit)


def layer_kernel(
    tok, cot, mem_k, mem_v, choice, flag, w_q, w_k, w_v, w_o, w_b, w_d, gains,
    out_y, out_x, out_q, out_k, out_v, out_o, out_b, out_d, out_g,
    wa, wo, wb, wc, w_land, gc, go, c_a, c_o, c_b, c_d, y_a, y_o, y_b, y_d, z_a, z_o, z_b, z_d, z_w, x_n, x_d,
    xf, dyf, act, tr, qkv, aof, h, hid, dgu, part, swap_r, swap_s, dqkv, kv_acc, mk, mv, tr_one, tr_two, lse,
    row_s, row_r, gain, gain_acc,
    ws, wr, own_s, xs, xr, zs, zr, ys, yr, cs, cr, mem_s, es, er, rcs, rcr, rys, ryr, rzs, rzr, rxs, rxr,
):
    seg = lax.axis_index("seg")
    x = lax.axis_index("row")
    c = seg % 2
    y = (seg // 2) % 2
    z = seg // 4
    rows, width = tok.shape
    length = 2 * rows
    cols = width // 2
    heads = cols // HD
    own, peer = aligned(x * rows, rows), aligned((1 - x) * rows, rows)
    ff = wc.shape[0]
    blk = wc.shape[0] // 8
    scale = HD ** (-0.5)
    over_x, over_y, over_c = device(z, y, c, 1 - x), device(z, 1 - y, c, x), device(z, y, 1 - c, x)
    mine = x == c
    other = jnp.logical_not(mine)
    col0 = aligned(x * cols, cols)

    barrier = pltpu.get_barrier_semaphore()
    for d in range(1, 4):
        pl.semaphore_signal(barrier, inc=1, device_id=device((z + d) % 4, y, c, x), device_id_type=MESH)
    for near in (over_x, over_y, over_c):
        pl.semaphore_signal(barrier, inc=1, device_id=near, device_id_type=MESH)
    pl.semaphore_wait(barrier, 6)

    def chunk(n):
        return [(i, min(512, n - i)) for i in range(0, n, 512)]

    groups = [(wa, 0, 512), (wa, 512, 512), (wa, 1024, 640)]
    groups += [(wo, col0, cols)] + [(wb, i, n) for i, n in chunk(2 * ff)]
    n_groups = len(groups)
    y_first = (2, 7)
    inner = jnp.logical_or(z == 1, z == 2)
    end_low, end_high = z == 0, z == 3

    def block(g, zz, yy):
        if g >= n_groups:
            p = zz * 2 + yy
            return wc.at[pl.ds(aligned(p * blk, 16), blk), pl.ds((g - n_groups) * 512, 512)]
        ref, at, n = groups[g]
        return ref.at[zz, yy, c, :, pl.ds(at, n)]

    def part_of(g, which):
        half_at = aligned(which * cols, cols)
        if g < 4:
            return [w_q, w_k, w_v, w_o][g].at[:, pl.ds(half_at, cols)]
        ref, at, n = groups[g]
        return w_b.at[which, :, pl.ds(at, n)]

    def my_rows(g, which):
        ref, at, n = groups[g]
        at = aligned(which * cols, cols) if ref is wo else at
        return ref.at[z, y, c, pl.ds(aligned(x * 32, 32), 32), pl.ds(at, min(n, 512))]

    my_gain = wa.at[z, y, c, pl.ds(aligned(x * 32, 32), 32), pl.ds(3 * cols, 128)]
    my_down = w_land.at[x]
    gx, tx, dx, cx = n_groups, n_groups + 1, n_groups + 2, n_groups + 3
    first = [remote(part_of(g, 1 - x), my_rows(g, 1 - x), xs.at[g], xr.at[g], over_x) for g in range(n_groups)]
    local = [pltpu.make_async_copy(part_of(g, x), my_rows(g, x), own_s.at[g]) for g in range(n_groups)]
    first.append(remote(gains, my_gain, xs.at[gx], xr.at[gx], over_x))
    local.append(pltpu.make_async_copy(gains, my_gain, own_s.at[gx]))
    first.append(remote(tok, xf.at[pl.ds(own, rows)], xs.at[tx], xr.at[tx], over_x))
    local.append(pltpu.make_async_copy(tok, xf.at[pl.ds(own, rows)], own_s.at[tx]))
    first.append(remote(cot, dyf.at[pl.ds(own, rows)], xs.at[dx], xr.at[dx], over_x))
    local.append(pltpu.make_async_copy(cot, dyf.at[pl.ds(own, rows)], own_s.at[dx]))
    down_x = remote(w_d, my_down, xs.at[cx], xr.at[cx], over_x)
    down_l = pltpu.make_async_copy(w_d, my_down, own_s.at[cx])

    def to_z(g, d, f):
        b = block(g, z, (y + f) % 2)
        return remote(b, b, zs.at[g, f, d - 1], zr.at[g, f, d - 1], device((z + d) % 4, y, c, x))

    def relay(g, f):
        b = block(g, (z + 2) % 4, (y + f) % 2)
        return remote(b, b, zs.at[g, f, 3], zr.at[g, f, 2 * (z // 2)], device(3 * (z // 2), y, c, x))

    def start_z(g, f):
        to_z(g, 2, f).start()
        pl.when(jnp.logical_not(end_high))(lambda: to_z(g, 1, f).start())
        pl.when(jnp.logical_not(end_low))(lambda: to_z(g, 3, f).start())

    def sent_z(g, f):
        to_z(g, 2, f).wait_send()
        pl.when(jnp.logical_not(end_high))(lambda: to_z(g, 1, f).wait_send())
        pl.when(jnp.logical_not(end_low))(lambda: to_z(g, 3, f).wait_send())
        pl.when(inner)(lambda: relay(g, f).wait_send())

    near_d = jnp.where(end_low, 3, 1)

    def to_y(g, d):
        b = block(g, (z + 4 - d) % 4, y)
        return remote(b, b, ys.at[g, d], yr.at[g, d], over_y)

    def to_c(g, d, f):
        b = block(g, (z + 4 - d) % 4, (y + f) % 2)
        return remote(b, b, cs.at[g, d, f], cr.at[g, d, f], over_c)

    def gated(fn):
        def run(g, *rest):
            if g >= n_groups:
                pl.when(mine)(lambda: fn(g, *rest))
            else:
                fn(g, *rest)

        return run

    @gated
    def spread(g):
        if g < n_groups:
            first[g].wait_recv()
            local[g].wait()
            if g == 2:
                first[gx].wait_recv()
                local[gx].wait()
        elif g == n_groups:
            down_x.wait_recv()
            down_l.wait()
            pair = jnp.concatenate([w_land[0].astype(F32), w_land[1].astype(F32)], axis=0)
            wc[pl.ds(aligned((z * 2 + y) * blk, 16), blk)] = pair.astype(BF)
        start_z(g, 0)
        to_y(g, 0).start()
        to_c(g, 0, 0).start()

    def turn(g):
        if g in y_first:
            to_y(g, 0).wait_recv()
            start_z(g, 1)
            to_c(g, 0, 1).start()

    @gated
    def pass_z(g):
        for f in range(2 if g in y_first else 1):
            for d in (2, near_d, 4 - near_d):
                to_z(g, d, f).wait_recv()
                if isinstance(d, int):
                    pl.when(inner)(lambda: relay(g, f).start())
                if g not in y_first:
                    to_y(g, d).start()
                to_c(g, d, f).start()

    @gated
    def pass_y(g):
        if g not in y_first:
            for d in range(4):
                to_y(g, d).wait_recv()
                to_c(g, d, 1).start()

    def arrived(g):
        for d in range(4):
            for f in range(2):
                to_c(g, d, f).wait_recv()

    @gated
    def sent(g):
        sent_z(g, 0)
        if g in y_first:
            sent_z(g, 1)
        for d in range(4):
            if d == 0 or g not in y_first:
                to_y(g, d).wait_send()
            for f in range(2):
                to_c(g, d, f).wait_send()

    def out_half(which, core, to, k):
        b = wo.at[:, :, core, :, pl.ds(aligned(which * cols, cols), cols)]
        return remote(b, b, ws.at[k], wr.at[k], to)

    out_over = out_half(x, c, over_x, 0)
    out_next = out_half(1 - x, c, over_c, 1)

    last_group = n_groups + 1

    def step(g):
        if g + 3 - 1 <= last_group:
            turn(g + 3 - 1)
        if g <= last_group:
            pass_z(g)
        if g + 3 <= last_group:
            spread(g + 3)
        if 1 <= g <= last_group + 1:
            pass_y(g - 1)
        if g == 4:
            out_over.start()

    for g in (0, 1, 2, gx):
        first[g].start()
        local[g].start()
    local[tx].start()
    local[dx].start()
    mem_bufs = [dqkv, hid]
    n_mem = mem_k.shape[0] // length

    def mem_copy(i):
        buf = mem_bufs[i % 2]
        return [
            pltpu.make_async_copy(
                m.at[pl.ds(i * length, length), pl.ds(aligned(col0 + hh * HD, HD), HD)],
                buf.at[:, pl.ds((hh * 2 + j) * HD, HD)],
                mem_s.at[i % 2, hh * 2 + j],
            )
            for hh in range(heads)
            for j, m in enumerate((mem_k, mem_v))
        ]

    for i in range(2):
        for cp in mem_copy(i):
            cp.start()
    spread(0)
    spread(1)
    spread(2)
    for g in list(range(3, n_groups)):
        first[g].start()
        local[g].start()

    @pl.when(mine)
    def _():
        down_l.start()

    @pl.when(other)
    def _():
        down_x.start()

    first[tx].start()

    def choose(i):
        for cp in mem_copy(i):
            cp.wait()
        at = lax.broadcasted_iota(jnp.int32, (HD, length), 1) + i * length
        for hh in range(heads):
            picked = jnp.where(x == 0, choice[:, hh : hh + 1], choice[:, heads + hh : heads + hh + 1])
            hot = (picked == at).astype(F32).astype(BF)
            both = plain_dot(hot, mem_bufs[i % 2][:, hh * 2 * HD : (hh + 1) * 2 * HD])
            where = slice(hh * HD, (hh + 1) * HD)
            if i == 0:
                kv_acc[0, where, 0 : 2 * HD] = both
            else:
                kv_acc[0, where, 0 : 2 * HD] += both
        if i + 2 < n_mem:
            for cp in mem_copy(i + 2):
                cp.start()

    done = 0
    for g in range(4):
        upto = n_mem * (g + 1) // 4
        for i in range(done, upto):
            choose(i)
        done = upto
        step(g)
        if g == 2:
            first[tx].wait_recv()
            local[tx].wait()
            first[dx].start()
    for hh in range(heads):
        where = slice(hh * HD, (hh + 1) * HD)
        mk[:, where] = kv_acc[0, where, 0:HD].astype(BF)
        mv[:, where] = kv_acc[0, where, HD : 2 * HD].astype(BF)
    for g in range(3):
        arrived(g)

    @pl.loop(0, 8)
    def _(p):
        block_t = jnp.transpose(
            wa[p // 2, p % 2, :, :, 3 * cols : 3 * cols + 128].reshape(128, 128).astype(F32)
        )
        gain[:, pl.ds(aligned(p * 128, 128), 128)] = block_t[0:8]

    def norm_rows(at, n):
        xc = xf[pl.ds(at, n)].astype(F32)
        inv = lax.rsqrt(jnp.mean(xc * xc, axis=-1, keepdims=True) + EPS)
        return xc * inv, inv

    def norm_one(i):
        at = aligned(i * 64, 64)
        u, _ = norm_rows(at, 64)
        return at, (u * gain[0:1]).astype(BF)

    @pl.loop(0, length // 64)
    def _(i):
        at, a = norm_one(i)
        act[pl.ds(at, 64)] = a

    def w_cols(ref, at, n):
        return ref[:, :, :, :, pl.ds(at, n)].reshape(width, n)

    @pl.loop(0, 3 * cols // 256)
    def _(i):
        at = aligned(i * 256, 256)
        qkv[:, pl.ds(at, 256)] = plain_dot(act[...], w_cols(wa, at, 256)).astype(BF)

    def scores(hh, i, n):
        lane = pl.ds(aligned(hh * HD, HD), HD)
        query = qkv[i * HD : (i + 1) * HD, lane]
        key = qkv[0:n, pl.ds(aligned(cols + hh * HD, HD), HD)]
        local_s = dot_right(query, key) * scale
        seen = lax.broadcasted_iota(jnp.int32, (HD, n), 1) <= lax.broadcasted_iota(jnp.int32, (HD, n), 0) + i * HD
        local_s = jnp.where(seen, local_s, NEG)
        far = dot_right(query, mk[:, lane]) * scale
        far = jnp.where(flag[0:1] > 0, far, NEG)
        return query, key, local_s, far, lane

    def value_of(hh, n):
        return qkv[0:n, pl.ds(aligned(2 * cols + hh * HD, HD), HD)]

    def att_copy(i):
        part_ref = aof.at[pl.ds(i * HD, HD), pl.ds(col0, cols)]
        return remote(part_ref, part_ref, es.at[i], er.at[i], over_x)

    n_q = length // HD

    def attend(i):
        n = (i + 1) * HD

        for hh in range(heads):
            _, _, local_s, far, lane = scores(hh, i, n)
            top = jnp.maximum(jnp.max(local_s, axis=-1, keepdims=True), jnp.max(far, axis=-1, keepdims=True))
            local_e, far_e = jnp.exp(local_s - top), jnp.exp(far - top)
            total = jnp.sum(local_e, axis=-1, keepdims=True) + jnp.sum(far_e, axis=-1, keepdims=True)
            inv = 1.0 / total
            lse[i * HD : (i + 1) * HD, hh : hh + 1] = top + jnp.log(total)
            out = plain_dot((local_e * inv).astype(BF), value_of(hh, n)) + plain_dot((far_e * inv).astype(BF), mv[:, lane])
            aof[i * HD : (i + 1) * HD, pl.ds(aligned(col0 + hh * HD, HD), HD)] = out.astype(BF)

        att_copy(i).start()

    for i in range(n_q):
        attend(i)
        if i == 0:
            step(4)
        if i == 2:
            step(5)

    @pl.loop(0, n_q)
    def _(i):
        at = aligned(i * HD, HD)
        tr_one[:, pl.ds(at, HD)] = jnp.transpose(act[pl.ds(at, HD)])

    step(6)
    out_over.wait_recv()
    out_next.start()
    step(7)
    arrived(3)
    out_next.wait_recv()
    for i in range(n_q):
        att_copy(i).wait_recv()

    @pl.loop(0, width // 256)
    def _(i):
        at = aligned(i * 256, 256)
        h[:, pl.ds(at, 256)] = xf[:, pl.ds(at, 256)].astype(F32) + plain_dot(aof[...], w_cols(wo, at, 256))

    @pl.loop(0, length // 64)
    def _(i):
        at = aligned(i * 64, 64)
        hc = h[pl.ds(at, 64)]
        inv = lax.rsqrt(jnp.mean(hc * hc, axis=-1, keepdims=True) + EPS)
        act[pl.ds(at, 64)] = (hc * inv * gain[1:2]).astype(BF)

    def transpose_to(dst, src):
        @pl.loop(0, n_q)
        def _(i):
            at = aligned(i * HD, HD)
            dst[0:width, pl.ds(at, HD)] = jnp.transpose(src[pl.ds(at, HD)])

    def up_tile(j):
        at = aligned(j * 256, 256)
        both = plain_dot(act[...], w_cols(wb, at, 256))
        gate, up = both[:, :128], both[:, 128:]
        sig = 1.0 / (1.0 + jnp.exp(-gate))
        silu = gate * sig
        tile = (silu * up).astype(BF)
        lanes = pl.ds(aligned(j * 128, 128), 128)
        hid[:, lanes] = tile
        tr[lanes] = jnp.transpose(tile)
        dgu[:, pl.ds(at, 128)] = (up * sig * (1.0 + gate * (1.0 - sig))).astype(BF)
        dgu[:, pl.ds(aligned(at + 128, 128), 128)] = silu.astype(BF)

    for g in range(4, n_groups):
        if g > 5 and g != 6:
            step(g + 1)
        arrived(g)
        pl.loop((g - 4) * 2, (g - 4) * 2 + groups[g][2] // 256)(up_tile)

    first[dx].wait_recv()
    local[dx].wait()

    red = [(None, c_d, y_d, z_d, 0, 512), (None, c_d, y_d, z_d, 512, 512)]
    red += [(go if i == 0 else wb, c_b, y_b, z_b, i, n) for i, n in chunk(2 * ff)]
    z_first = {2: 0, 5: 1}
    red += [(wb, c_o, y_o, z_o, 0, 512)]
    red += [(wo, c_a, y_a, z_a, 0, 512), (wo, c_a, y_a, z_a, 512, 512)]
    red += [(go, c_a, y_a, z_a, 1024, 512), (wa, c_a, y_a, z_a, 1536, 128)]
    n_red = len(red)
    x_at = [0, 512]
    for g in range(2, n_red):
        x_at.append(sum(red[i][5] for i in range(2, g)))

    def red_c(g):
        src, cb, _, _, at, n = red[g]
        lanes = pl.ds(at, n)
        source = gc.at[:, :, :, lanes] if g < 2 else src.at[:, :, 1 - c, :, pl.ds(0 if src is go else at, n)]
        return remote(source, cb.at[:, :, :, lanes], rcs.at[g], rcr.at[g], over_c)

    def red_y(g):
        _, cb, yb, _, at, n = red[g]
        lanes = pl.ds(at, n)
        if g in z_first:
            return remote(cb.at[z, 1 - y, :, lanes], yb.at[0, :, lanes], rys.at[g], ryr.at[g], over_y)
        return remote(cb.at[:, 1 - y, :, lanes], yb.at[:, :, lanes], rys.at[g], ryr.at[g], over_y)

    def z_parts(g):
        _, cb, yb, zb, at, n = red[g]
        lanes = pl.ds(at, n)
        if g in z_first:
            return (lambda zz: cb.at[zz, :, :, lanes]), (lambda k: z_w.at[z_first[g], k])
        return (lambda zz: yb.at[zz, :, lanes]), (lambda k: zb.at[k, :, lanes])

    def red_z(g, d):
        src, dst = z_parts(g)
        zz = (z + d) % 4
        return remote(src(zz), dst(d - 1), rzs.at[g, d - 1], rzr.at[g, d - 1], device(zz, y, c, x))

    def red_far(g):
        src, dst = z_parts(g)
        return remote(src(3 - z), dst(3), rzs.at[g, 3], rzr.at[g, 3], device(1 + z // 3, y, c, x))

    def start_red_z(g):
        @pl.when(jnp.logical_not(inner))
        def _():
            red_far(g).start()
            red_z(g, 2).start()

        pl.when(jnp.logical_not(end_high))(lambda: red_z(g, 1).start())
        pl.when(jnp.logical_not(end_low))(lambda: red_z(g, 3).start())

    def merge(g):
        @pl.when(inner)
        def _():
            red_far(g).wait_recv()
            src, dst = z_parts(g)
            away = src((z + 2) % 4)
            away[...] = (away[...].astype(F32) + dst(3)[...].astype(F32)).astype(BF)
            red_z(g, 2).start()

    def wait_red_z(g):
        red_z(g, 2).wait_recv()
        pl.when(jnp.logical_not(end_low))(lambda: red_z(g, 1).wait_recv())
        pl.when(jnp.logical_not(end_high))(lambda: red_z(g, 3).wait_recv())

    def total_z(g):
        src, dst = z_parts(g)
        total = src(z)[...].astype(F32)
        for k in range(3):
            total = total + dst(k)[...].astype(F32)
        return total

    def red_x(g):
        lanes = pl.ds(x_at[g], red[g][5])
        buf = x_d if g < 2 else x_n
        return remote(buf.at[0, :, lanes], buf.at[1, :, lanes], rxs.at[g], rxr.at[g], over_x)

    def only_mine(fn):
        def run(g):
            if g < 2:
                pl.when(mine)(lambda: fn(g))
            else:
                fn(g)

        return run

    def start_c(g):
        if g < 2:
            pl.when(other)(lambda: red_c(g).start())
        else:
            red_c(g).start()

    @only_mine
    def sum_c(g):
        red_c(g).wait_recv()
        src, cb, _, _, at, n = red[g]
        lanes = pl.ds(at, n)

        @pl.loop(0, 8)
        def _(i):
            own = gc[i // 2, i % 2, :, lanes] if g < 2 else src[i // 2, i % 2, c, :, pl.ds(0 if src is go else at, n)]
            cb[i // 2, i % 2, :, lanes] = (cb[i // 2, i % 2, :, lanes].astype(F32) + own.astype(F32)).astype(BF)

        start_red_z(g) if g in z_first else red_y(g).start()

    @only_mine
    def stage_one(g):
        if g in z_first:
            merge(g)
            return
        red_y(g).wait_recv()
        _, cb, yb, _, at, n = red[g]
        lanes = pl.ds(at, n)

        @pl.loop(0, 4)
        def _(i):
            yb[i, :, lanes] = (yb[i, :, lanes].astype(F32) + cb[i, y, :, lanes].astype(F32)).astype(BF)

        start_red_z(g)

    @only_mine
    def stage_two(g):
        if g in z_first:
            wait_red_z(g)
            src, _ = z_parts(g)
            src(z)[...] = total_z(g).astype(BF)
            red_y(g).start()
        else:
            merge(g)

    def result(g, which, value):
        at, n = red[g][4], red[g][5]
        if g < 2:
            out_d[:, at : at + n] = value
        elif g < n_red - 5:
            out_b[which, :, at : at + n] = value
        elif g == n_red - 1:
            out_g[which] = value
        else:
            out = [out_o, out_q, out_k, out_v][g - (n_red - 5)]
            out[:, pl.ds(aligned(which * cols, cols), cols)] = value

    @only_mine
    def stage_three(g):
        _, cb, yb, _, at, n = red[g]
        lanes = pl.ds(at, n)
        if g in z_first:
            red_y(g).wait_recv()
            total = cb[z, y, :, lanes].astype(F32) + yb[0, :, lanes].astype(F32)
        else:
            wait_red_z(g)
            total = total_z(g)
        size = yb.shape[1] // 2
        low, high = total[:size], total[size:]
        buf = x_d if g < 2 else x_n
        buf[0, :, pl.ds(x_at[g], n)] = jnp.where(x == 0, high, low).astype(BF)
        red_x(g).start()
        result(g, x, jnp.where(x == 0, low, high))

    def finish(g):
        lanes = pl.ds(x_at[g], red[g][5])

        def take():
            red_x(g).wait_recv()
            result(g, 1 - x, (x_d if g < 2 else x_n)[1, :, lanes].astype(F32))

        if g < 2:
            pl.when(other)(take)
        else:
            take()

    @only_mine
    def red_sent(g):
        red_y(g).wait_send()
        red_z(g, 2).wait_send()
        pl.when(jnp.logical_not(end_high))(lambda: red_z(g, 1).wait_send())
        pl.when(jnp.logical_not(end_low))(lambda: red_z(g, 3).wait_send())
        pl.when(jnp.logical_not(inner))(lambda: red_far(g).wait_send())
        red_x(g).wait_send()

    done_at = {}

    def advance(stage, upto):
        fns = [sum_c, stage_one, stage_two, stage_three, finish]
        for g in range(done_at.get(stage, 0), min(upto + 1, n_red)):
            fns[stage](g)
        done_at[stage] = max(done_at.get(stage, 0), min(upto + 1, n_red))

    def tick(k, cap=n_red):
        for stage, lag in enumerate((0, 2, 4, 6, 7)):
            advance(stage, min(k - lag, cap))

    @pl.when(end_low)
    def _():
        for zb in (z_a, z_o, z_b, z_d):
            zb[0] = jnp.zeros(zb.shape[1:], BF)
        for i in range(2):
            z_w[i, 0] = jnp.zeros(z_w.shape[2:], BF)

    @pl.when(end_high)
    def _():
        for zb in (z_a, z_o, z_b, z_d):
            zb[2] = jnp.zeros(zb.shape[1:], BF)
        for i in range(2):
            z_w[i, 2] = jnp.zeros(z_w.shape[2:], BF)

    for i in range(2):

        @pl.loop(0, 4)
        def _(t):
            res = plain_dot(tr[pl.ds(aligned(t * 2 * blk, 32), 2 * blk)], dyf[:, i * 512 : (i + 1) * 512])
            gc[t, :, :, i * 512 : (i + 1) * 512] = res.reshape(2, blk, 512).astype(BF)

        start_c(i)
    step(n_groups + 1)
    advance(0, 0)
    advance(0, 1)
    transpose_to(tr_two, act)
    step(n_groups + 2)

    def wait_down():
        for g in range(n_groups, last_group + 1):
            arrived(g)

    pl.when(other)(wait_down)

    def dhid_tile(j, n):
        lanes = aligned(j * 128, 128)
        res = dot_right(dyf[...], wc[pl.ds(lanes, 128 * n)])
        for t in range(n):
            at = aligned((j + t) * 256, 256)
            d = res[:, t * 128 : (t + 1) * 128]
            for s in range(2):
                where = pl.ds(aligned(at + 128 * s, 128), 128)
                dgu[:, where] = (d * dgu[:, where].astype(F32)).astype(BF)

    n_tiles = ff // 128

    @pl.loop(0, n_tiles // 2)
    def _(t):
        dhid_tile(t * 2, 2)

    if n_tiles % 2:
        dhid_tile(n_tiles - 1, 1)

    def grad_tile(dst, lhs, value, at):
        res = plain_dot(lhs[0:width], value)
        dst[:, :, :, :, pl.ds(at, 256)] = res.reshape(4, 2, 2, 64, 256).astype(BF)

    n_b = len(chunk(2 * ff))

    def grad_ff(g):
        at0, n = red[2 + g][4], red[2 + g][5]
        for t in range(n // 256):
            grad_tile(go if g == 0 else wb, tr_two, dgu[:, at0 + t * 256 : at0 + (t + 1) * 256], at0 + t * 256)
        start_c(2 + g)

    grad_ff(0)
    gain_acc[...] = jnp.zeros_like(gain_acc)

    def swap_copy(i):
        at = pl.ds(128 * i, 128)
        return remote(swap_s.at[at], swap_r.at[at], es.at[8 + i], er.at[8 + i], over_x)

    for f in range(2):

        @pl.loop(0, width // 256)
        def _(i):
            at = aligned(i * 256, 256)
            res = dot_right(dgu[f * rows : (f + 1) * rows], wb[i, :, :, :, :].reshape(256, 2 * ff))
            part[f * rows : (f + 1) * rows, pl.ds(at, 256)] = res
            swap_s[f * rows : (f + 1) * rows, pl.ds(at, 256)] = res.astype(BF)

        swap_copy(2 * f).start()
        swap_copy(2 * f + 1).start()

    def add_gain(k, grad, unit):
        prod = grad * unit
        gain_acc[k] += jnp.sum(prod.reshape(prod.shape[0] // 8, 8, width), axis=0)

    for g in range(4, n_groups):
        sent(g)
    for g in range(1, n_b):
        grad_ff(g)
        if g == 1:
            advance(0, 2)
        if g == 2:
            advance(1, 0)
        if g == 3:
            advance(0, 3)
        if g == 4:
            advance(1, 1)
        if g == 5:
            advance(0, 4)

    def d_hidden_rows(i):
        at = aligned(i * 64, 64)
        hc = h[pl.ds(at, 64)]
        inv = lax.rsqrt(jnp.mean(hc * hc, axis=-1, keepdims=True) + EPS)
        u = hc * inv
        add_gain(1, part[pl.ds(at, 64)], u)
        e = (part[pl.ds(at, 64)] + swap_r[pl.ds(at, 64)].astype(F32)) * gain[1:2]
        dh = dyf[pl.ds(at, 64)].astype(F32) + inv * (e - u * jnp.mean(e * u, axis=-1, keepdims=True))
        part[pl.ds(at, 64)] = dh
        act[pl.ds(at, 64)] = dh.astype(BF)

    kv_acc[...] = jnp.zeros_like(kv_acc)
    w_own = wo.at[pl.ds(x * 2, 2)]

    def attend_back(i):
        n = (i + 1) * HD
        at = slice(i * HD, (i + 1) * HD)
        d_att = dot_right(act[at], w_own[...].reshape(cols, width)).astype(BF)
        for hh in range(heads):
            query, key, local_s, far, lane = scores(hh, i, n)
            log_sum = lse[at, hh : hh + 1]
            p_l, p_m = jnp.exp(local_s - log_sum), jnp.exp(far - log_sum)
            grad = d_att[:, hh * HD : (hh + 1) * HD]
            out = aof[at, pl.ds(aligned(col0 + hh * HD, HD), HD)]
            delta = jnp.sum(grad.astype(F32) * out.astype(F32), axis=-1, keepdims=True)
            ds_l = (p_l * (dot_right(grad, value_of(hh, n)) - delta)).astype(BF)
            ds_m = (p_m * (dot_right(grad, mv[:, lane]) - delta)).astype(BF)
            dq = (plain_dot(ds_l, key) + plain_dot(ds_m, mk[:, lane])) * scale
            dqkv[at, hh * HD : (hh + 1) * HD] = dq.astype(BF)
            kv_acc[0, 0:n, hh * HD : (hh + 1) * HD] += dot_left(ds_l, query)
            kv_acc[1, 0:n, hh * HD : (hh + 1) * HD] += dot_left(p_l.astype(BF), grad)

    base = 4
    for i in range(n_q):
        swap_copy(i).wait_recv()
        pl.loop(i * 2, i * 2 + 2)(d_hidden_rows)
        attend_back(i)
        if i == 0:
            transpose_to(tr, aof)
        if i == n_q - 1:

            @pl.loop(0, width // 256)
            def _(j):
                at = aligned(j * 256, 256)
                row_s[:, pl.ds(at, 256)] = plain_dot(hid[pl.ds(peer, rows)], wc[:, pl.ds(at, 256)]).astype(BF)

            row_y = remote(row_s, row_r.at[0], es.at[12], er.at[12], over_x)
            row_y.start()
        for _ in range([1,1,1,1][i]):
            tick(base, 1 + n_b)
            base += 1
    sent(3)
    out_over.wait_send()
    out_next.wait_send()
    dqkv[:, cols : 2 * cols] = (kv_acc[0] * scale).astype(BF)
    dqkv[:, 2 * cols :] = kv_acc[1].astype(BF)

    def grad_tile_one(dst, at, to):
        res = plain_dot(tr_one[...], dqkv[:, at : at + 256])
        dst[:, :, :, :, to : to + 256] = res.reshape(4, 2, 2, 64, 256).astype(BF)

    for t in range(2):
        grad_tile(wb, tr, act[:, pl.ds(aligned(col0 + t * 256, 256), 256)], t * 256)
    start_c(2 + n_b)
    for g in range(2):
        for t in range(2):
            grad_tile_one(wo, g * cols + t * 256, g * cols + t * 256)
        start_c(3 + n_b + g)
    red_c(2).wait_send()
    for t in range(2):
        grad_tile_one(go, 2 * cols + t * 256, t * 256)
    start_c(5 + n_b)
    tick(base)
    base += 1

    row_y.wait_send()
    def d_one(at):
        return jnp.concatenate([kv_acc[0, pl.ds(at, 64)], kv_acc[1, pl.ds(at, 64)]], axis=1)

    for first_half in (False, True):
        half_rows = pl.ds(own if first_half else peer, rows)

        @pl.loop(0, width // 256)
        def _(i):
            at = aligned(i * 256, 256)
            res = dot_right(dqkv[half_rows], wa[i, :, :, :, 0 : 3 * cols].reshape(256, 3 * cols))
            if not first_half:
                row_s[:, pl.ds(at, 256)] = res.astype(BF)
            kv_acc[i // 2, half_rows, pl.ds(aligned((i % 2) * 256, 256), 256)] = res

        if not first_half:
            row_x = remote(row_s, row_r.at[1], es.at[13], er.at[13], over_x)
            row_x.start()

    @pl.loop(0, length // 64)
    def _(i):
        at = aligned(i * 64, 64)
        u, _ = norm_rows(at, 64)
        add_gain(0, d_one(at), u)

    for g in range(3):
        sent(g)
    sums = [jnp.sum(gain_acc[k], axis=0, keepdims=True) for k in range(2)]
    tall = lax.broadcasted_iota(jnp.int32, (128, 128), 0)
    for p in range(8):
        lanes = slice(p * 128, (p + 1) * 128)
        both = jnp.where(tall == 0, sums[0][:, lanes], jnp.where(tall == 1, sums[1][:, lanes], 0.0))
        wa[p // 2, p % 2, :, :, 3 * cols :] = jnp.transpose(both).reshape(2, 64, 128).astype(BF)
    start_c(6 + n_b)
    tick(base)
    base += 1
    row_y.wait_recv()

    @pl.loop(0, width // 256)
    def _(i):
        at = aligned(i * 256, 256)
        mine_y = plain_dot(hid[pl.ds(own, rows)], wc[:, pl.ds(at, 256)]) + h[pl.ds(own, rows), pl.ds(at, 256)]
        out_y[:, pl.ds(at, 256)] = (mine_y + row_r[0, :, pl.ds(at, 256)].astype(F32)).astype(BF)
    row_x.wait_recv()

    @pl.loop(0, rows // 64)
    def _(i):
        at = aligned(own + i * 64, 64)
        u, inv = norm_rows(at, 64)
        e = (d_one(at) + row_r[1, pl.ds(aligned(i * 64, 64), 64)].astype(F32)) * gain[0:1]
        out = part[pl.ds(at, 64)] + inv * (e - u * jnp.mean(e * u, axis=-1, keepdims=True))
        out_x[pl.ds(aligned(i * 64, 64), 64)] = out.astype(BF)

    for k in range(base, n_red + 8):
        tick(k)
    for cp in first:
        cp.wait_send()
    pl.when(other)(lambda: down_x.wait_send())
    for g in range(n_groups, last_group + 1):
        sent(g)
    for i in range(4):
        swap_copy(i).wait_send()
    for i in range(n_q):
        att_copy(i).wait_send()
    row_x.wait_send()
    for g in range(n_red):
        if g < 2:
            pl.when(other)(lambda: red_c(g).wait_send())
        elif g != 2:
            red_c(g).wait_send()
        red_sent(g)


def layer(tok, cot, mem_k, mem_v, choice, flag, w_q, w_k, w_v, w_o, w_b, w_d, gains):
    rows, width = tok.shape
    length = 2 * rows
    cols = width // 2
    ff2 = w_b.shape[2]
    ff = ff2 // 2
    blk = ff // 8
    na = 3 * cols + 128
    hbm, vm = pl.BlockSpec(memory_space=pl.ANY), pl.BlockSpec(memory_space=pltpu.VMEM)
    own = w_q.shape[0]
    shape = jax.ShapeDtypeStruct
    return pl.pallas_call(
        layer_kernel,
        name="layer",
        out_shape=(
            shape((rows, width), BF),
            shape((rows, width), BF),
            shape((own, width), F32),
            shape((own, width), F32),
            shape((own, width), F32),
            shape((own, width), F32),
            shape((2, own, ff2), F32),
            shape((blk // 2, width), F32),
            shape((2, own, 128), F32),
        ),
        in_specs=[hbm] * 4 + [vm] * 2 + [hbm] * 7,
        out_specs=(vm,) * 9,
        scratch_shapes=[
            VM((4, 2, 2, 64, na), BF), VM((4, 2, 2, 64, width), BF), VM((4, 2, 2, 64, ff2), BF), VM((ff, width), BF), VM((2, blk // 2, width), BF),
            VM((4, 2, blk, width), BF), VM((4, 2, 2, 64, cols), BF),
            VM((4, 2, 64, na), BF), VM((4, 2, 64, cols), BF), VM((4, 2, 64, ff2), BF), VM((4, 2, blk, width), BF),
            VM((4, 64, na), BF), VM((4, 64, cols), BF), VM((4, 64, ff2), BF), VM((4, blk, width), BF),
            VM((4, 64, na), BF), VM((4, 64, cols), BF), VM((4, 64, ff2), BF), VM((4, blk, width), BF),
            VM((2, 4, 2, 64, 512), BF),
            VM((2, own, ff2 + na + cols), BF), VM((2, blk // 2, width), BF),
            VM((length, width), BF), VM((length, width), BF), VM((length, width), BF), VM((ff, length), BF),
            VM((length, 3 * cols), BF), VM((length, width), BF), VM((length, width), F32), VM((length, ff), BF),
            VM((length, ff2), BF), VM((length, width), F32), VM((length, width), BF), VM((length, width), BF),
            VM((length, 3 * cols), BF), VM((2, length, cols), F32), VM((HD, cols), BF), VM((HD, cols), BF),
            VM((width, length), BF), VM((width, length), BF), VM((length, 128), F32),
            VM((rows, width), BF), VM((2, rows, width), BF), VM((8, width), F32), VM((2, 8, width), F32),
            DMA((2,)), DMA((2,)), DMA((16,)), DMA((16,)), DMA((16,)), DMA((12, 2, 4)), DMA((12, 2, 4)),
            DMA((12, 4)), DMA((12, 4)), DMA((12, 4, 2)), DMA((12, 4, 2)), DMA((2, 8)), DMA((14,)), DMA((14,)),
            DMA((13,)), DMA((13,)), DMA((13,)), DMA((13,)), DMA((13, 4)), DMA((13, 4)), DMA((13,)), DMA((13,)),
        ],
        compiler_params=pltpu.CompilerParams(collective_id=0, has_side_effects=True, vmem_limit_bytes=127 << 19),
    )(tok, cot, mem_k, mem_v, choice, flag, w_q, w_k, w_v, w_o, w_b, w_d, gains)


def prepare_kernel(w_g, w_u, norms, choice, flag, w_b, gains, columns, flags):
    wide = w_g.shape[1]
    strip = wide // 16
    for half in range(2):
        packed = []
        for w in (w_g, w_u):
            whole = w[...].astype(F32)
            cuts = [whole[:, (2 * p + half) * strip : (2 * p + half + 1) * strip] for p in range(8)]
            packed.append(jnp.concatenate(cuts, axis=1).astype(BF))
        for j in range(wide // 256):
            for i in range(2):
                w_b[half, :, (2 * j + i) * 128 : (2 * j + i + 1) * 128] = packed[i][:, j * 128 : (j + 1) * 128]
    own = norms.shape[1]
    tall = lax.broadcasted_iota(jnp.int32, (128, own), 0)
    both = norms[...].astype(F32)
    both = jnp.where(tall == 0, both[0:1], jnp.where(tall == 1, both[1:2], 0.0))
    gains[...] = jnp.transpose(both).astype(BF)
    many = jnp.concatenate([choice[...].astype(F32)] * (128 // choice.shape[0]), axis=0)
    columns[...] = jnp.transpose(many).astype(jnp.int32)
    flags[...] = jnp.full(flags.shape, flag[0], jnp.int32)


def prepare(w_g, w_u, norms, choice, flag):
    own, wide = w_g.shape
    vm = pl.BlockSpec()
    shape = jax.ShapeDtypeStruct
    return pl.pallas_call(
        prepare_kernel,
        name="prepare",
        out_shape=(
            shape((2, own, wide), BF), shape((own, 128), BF), shape((128, 128), jnp.int32), shape((8, 128), jnp.int32),
        ),
        in_specs=[vm] * 4 + [pl.BlockSpec(memory_space=pltpu.SMEM)],
        out_specs=(vm,) * 4,
        compiler_params=pltpu.CompilerParams(vmem_limit_bytes=63 << 20),
    )(w_g, w_u, norms, choice, flag)


def complete_kernel(i_y, i_x, i_q, i_k, i_v, i_o, i_b, i_d, i_g, y, x, q, k, v, o, g, u, d, n_a, n_f):
    for src, dst in ((i_y, y), (i_x, x), (i_q, q), (i_k, k), (i_v, v), (i_o, o), (i_d, d)):
        dst[...] = src[...]
    wide = g.shape[1]
    strip = wide // 16
    for i, dst in enumerate((g, u)):
        halves = [
            jnp.concatenate(
                [i_b[half, :, (2 * j + i) * 128 : (2 * j + i + 1) * 128] for j in range(wide // 256)], axis=1
            )
            for half in range(2)
        ]
        cuts = [halves[p % 2][:, (p // 2) * strip : (p // 2 + 1) * strip] for p in range(16)]
        dst[...] = jnp.concatenate(cuts, axis=1)
    own = n_a.shape[1]
    tall = jnp.transpose(i_g[0] + i_g[1])
    n_a[...] = tall[0:1, 0:own]
    n_f[...] = tall[1:2, 0:own]


def complete(*parts):
    own, width = parts[2].shape
    wide = parts[6].shape[2]
    vm = pl.BlockSpec()
    shape = jax.ShapeDtypeStruct
    like = [shape(p.shape, p.dtype) for p in parts[:6]]
    like += [shape((own, wide), F32)] * 2 + [shape(parts[7].shape, F32)] + [shape((1, own), F32)] * 2
    return pl.pallas_call(
        complete_kernel,
        name="complete",
        out_shape=tuple(like),
        in_specs=[vm] * 9,
        out_specs=(vm,) * 11,
        compiler_params=pltpu.CompilerParams(vmem_limit_bytes=63 << 20),
    )(*parts)


def fast_body(
    tokens, cotangent, memory_keys, memory_values, memory_choice, memory_flag,
    w_query, w_key, w_value, w_out, w_gate, w_up, w_down, norm_attn, norm_ffn,
):
    norms = jnp.stack([norm_attn, norm_ffn])
    w_b, gains, choice, flag = prepare(w_gate, w_up, norms, memory_choice[0, 0], memory_flag)
    parts = layer(
        tokens[0], cotangent[0], memory_keys[0], memory_values[0], choice, flag,
        w_query, w_key, w_value, w_out, w_b, w_down, gains,
    )
    y, x, q, k, v, o, g, u, d, n_a, n_f = complete(*parts)
    return y[None], x[None], q, k, v, o, g, u, d, n_a[0], n_f[0]


def solution(mesh):
    in_specs = (
        P("seg", "row", None),
        P("seg", "row", None),
        P("seg", None, None),
        P("seg", None, None),
        P("seg", None, None, None),
        P("seg"),
        P(("seg", "row"), None),
        P(("seg", "row"), None),
        P(("seg", "row"), None),
        P(("seg", "row"), None),
        P(("seg", "row"), None),
        P(("seg", "row"), None),
        P(("seg", "row"), None),
        P(("seg", "row")),
        P(("seg", "row")),
    )
    out_specs = (
        P("seg", "row", None),
        P("seg", "row", None),
        P(("seg", "row"), None),
        P(("seg", "row"), None),
        P(("seg", "row"), None),
        P(("seg", "row"), None),
        P(("seg", "row"), None),
        P(("seg", "row"), None),
        P(("seg", "row"), None),
        P(("seg", "row")),
        P(("seg", "row")),
    )

    def body(*args):
        segs, rows, width = args[0].shape
        fits = (
            mesh.shape["row"] == 2
            and mesh.shape["seg"] == 16
            and segs == 1
            and (rows, width) == (256, 1024)
            and args[4].shape[1] == 1
        )
        return (fast_body if fits else general_body)(*args)

    return jax.shard_map(body, mesh=mesh, in_specs=in_specs, out_specs=out_specs, check_vma=False)
```

```python
import functools

import jax
import jax.numpy as jnp
from jax import lax
from jax.experimental import pallas as pl
from jax.experimental.pallas import tpu as pltpu
from jax.sharding import PartitionSpec as P

HEADS = 8
HD = 128
QBLK = 512


EPS = 1e-06
NEG = -1000000000.0


def for_sending(array):

    def short(part):
        return part.astype(jnp.bfloat16) if part.dtype == jnp.float32 else part

    return jax.tree.map(short, array)


def plain_dot(left, right):
    return jnp.dot(left, right, preferred_element_type=jnp.float32)


def dot_left(left, right):
    return lax.dot_general(
        left, right, (((0,), (0,)), ((), ())), preferred_element_type=jnp.float32
    )


def dot_right(left, right):
    return lax.dot_general(
        left, right, (((1,), (1,)), ((), ())), preferred_element_type=jnp.float32
    )


def norm_apply(value, gain):
    inverse = lax.rsqrt(jnp.mean(value * value, axis=-1, keepdims=True) + EPS)
    return (value * inverse * gain, inverse)


def norm_back(value, gain, inverse, grad):
    unit = value * inverse
    gain_grad = jnp.sum(grad * unit, axis=0)
    scaled = grad * gain
    return (inverse * (scaled - unit * jnp.mean(scaled * unit, axis=-1, keepdims=True)), gain_grad)


def score_block(queries, keys, memory_key_rows, flag, first, length):
    score_scale = HD ** (-0.5)
    local = (
        jnp.einsum("bqhd,khd->bhqk", queries, keys, preferred_element_type=jnp.float32)
        * score_scale
    )
    distant_memory = (
        jnp.einsum("bqhd,bhmd->bhqm", queries, memory_key_rows, preferred_element_type=jnp.float32)
        * score_scale
    )
    nblocks, per_block = (queries.shape[0], queries.shape[1])
    pos = first + jnp.arange(nblocks * per_block).reshape(nblocks, 1, per_block, 1)
    key_pos = jnp.arange(length)
    local = jnp.where(key_pos[None, None, None, :] <= pos, local, NEG)
    distant_memory = jnp.where(flag > 0, distant_memory, NEG)
    return (local, distant_memory)


def row_stat(stat, rows):
    return jnp.transpose(stat[..., 0], (0, 2, 1)).reshape(rows, HEADS)


def general_body(
    tokens,
    cotangent,
    memory_keys,
    memory_values,
    memory_choice,
    memory_flag,
    w_query,
    w_key,
    w_value,
    w_out,
    w_gate,
    w_up,
    w_down,
    norm_attn,
    norm_ffn,
):
    segs, rows, width = tokens.shape
    group = lax.axis_size("row")
    seg_count = lax.axis_size("seg")
    length = rows * group
    first = lax.axis_index("row") * rows
    nblocks = max(rows // QBLK, 1)
    per_block = rows // nblocks
    score_scale = HD ** (-0.5)
    shards = (w_query, w_key, w_value, w_out, w_gate, w_up, w_down, norm_attn, norm_ffn)
    wq, wk, wv, wo, wg, wu, wd, gain_one, gain_two = (
        lax.all_gather(shards[0], ("seg", "row"), axis=0, tiled=True),
        lax.all_gather(shards[1], ("seg", "row"), axis=0, tiled=True),
        lax.all_gather(shards[2], ("seg", "row"), axis=0, tiled=True),
        lax.all_gather(shards[3], ("seg", "row"), axis=0, tiled=True),
        lax.all_gather(shards[4], ("seg", "row"), axis=0, tiled=True),
        lax.all_gather(shards[5], ("seg", "row"), axis=0, tiled=True),
        lax.all_gather(shards[6], ("seg", "row"), axis=0, tiled=True),
        lax.all_gather(shards[7], ("seg", "row"), axis=0, tiled=True),
        lax.all_gather(shards[8], ("seg", "row"), axis=0, tiled=True),
    )
    gain_attn = gain_one.astype(jnp.float32)
    gain_ffn = gain_two.astype(jnp.float32)
    x = tokens.reshape(segs * rows, width).astype(jnp.float32)
    normed, inv_one = norm_apply(x, gain_attn)
    a_one = normed.astype(jnp.bfloat16)
    query = plain_dot(a_one, wq).astype(jnp.bfloat16)
    key_local = plain_dot(a_one, wk).astype(jnp.bfloat16).reshape(segs, rows, width)
    value_local = plain_dot(a_one, wv).astype(jnp.bfloat16).reshape(segs, rows, width)
    keys_all, values_all = (
        lax.all_gather(key_local, "row", axis=1, tiled=True),
        lax.all_gather(value_local, "row", axis=1, tiled=True),
    )
    block_first = first // QBLK
    chosen = lax.dynamic_slice_in_dim(memory_choice, block_first, nblocks, axis=1)
    head_col = jnp.arange(HEADS)[None, :, None]
    seg_id = 0
    memory_key_rows = memory_keys[seg_id].reshape(-1, HEADS, HD)[chosen[seg_id], head_col]
    memory_value_rows = memory_values[seg_id].reshape(-1, HEADS, HD)[chosen[seg_id], head_col]
    qseg = query.reshape(nblocks, per_block, HEADS, HD)
    keys = keys_all[seg_id].reshape(length, HEADS, HD)
    vals = values_all[seg_id].reshape(length, HEADS, HD)
    local, distant_memory = score_block(
        qseg, keys, memory_key_rows, memory_flag[seg_id], first, length
    )
    top = jnp.maximum(
        jnp.max(local, axis=-1, keepdims=True), jnp.max(distant_memory, axis=-1, keepdims=True)
    )
    summed = jnp.sum(jnp.exp(local - top), axis=-1, keepdims=True) + jnp.sum(
        jnp.exp(distant_memory - top), axis=-1, keepdims=True
    )
    total = top + jnp.log(summed)
    p_local = jnp.exp(local - total).astype(jnp.bfloat16)
    p_remote = jnp.exp(distant_memory - total).astype(jnp.bfloat16)
    attention_output = jnp.einsum(
        "bhqk,khd->bqhd", p_local, vals, preferred_element_type=jnp.float32
    )
    attention_output = attention_output + jnp.einsum(
        "bhqm,bhmd->bqhd", p_remote, memory_value_rows, preferred_element_type=jnp.float32
    )
    outputs = attention_output.reshape(rows, width)
    mem_keys = [memory_key_rows]
    mem_vals = [memory_value_rows]
    queries = [qseg]
    totals = [total]
    attended = outputs.astype(jnp.bfloat16)
    hidden_in = x + plain_dot(attended, wo)
    normed_two, inv_two = norm_apply(hidden_in, gain_ffn)
    a_two = normed_two.astype(jnp.bfloat16)
    gate = plain_dot(a_two, wg)
    up = plain_dot(a_two, wu)
    act = jax.nn.silu(gate)
    hid = (act * up).astype(jnp.bfloat16)
    layer_out = (hidden_in + plain_dot(hid, wd)).astype(jnp.bfloat16).reshape(segs, rows, width)
    wq, wk, wv, wo, wg, wu, wd, gain_one, gain_two = (
        lax.all_gather(shards[0], ("seg", "row"), axis=0, tiled=True),
        lax.all_gather(shards[1], ("seg", "row"), axis=0, tiled=True),
        lax.all_gather(shards[2], ("seg", "row"), axis=0, tiled=True),
        lax.all_gather(shards[3], ("seg", "row"), axis=0, tiled=True),
        lax.all_gather(shards[4], ("seg", "row"), axis=0, tiled=True),
        lax.all_gather(shards[5], ("seg", "row"), axis=0, tiled=True),
        lax.all_gather(shards[6], ("seg", "row"), axis=0, tiled=True),
        lax.all_gather(shards[7], ("seg", "row"), axis=0, tiled=True),
        lax.all_gather(shards[8], ("seg", "row"), axis=0, tiled=True),
    )
    gain_attn = gain_one.astype(jnp.float32)
    gain_ffn = gain_two.astype(jnp.float32)
    grad_y = cotangent.reshape(segs * rows, width)
    grad_down = dot_left(hid, grad_y)
    d_hid = dot_right(grad_y, wd)
    sig = jax.nn.sigmoid(gate)
    d_gate = (d_hid * up * sig * (1.0 + gate * (1.0 - sig))).astype(jnp.bfloat16)
    d_up = (d_hid * act).astype(jnp.bfloat16)
    grad_gate = dot_left(a_two, d_gate)
    grad_up = dot_left(a_two, d_up)
    d_a_two = dot_right(d_gate, wg) + dot_right(d_up, wu)
    d_norm_two, grad_gain_ffn = norm_back(hidden_in, gain_ffn, inv_two, d_a_two)
    d_hidden = grad_y.astype(jnp.float32) + d_norm_two
    d_proj = d_hidden.astype(jnp.bfloat16)
    grad_out = dot_left(attended, d_proj)
    d_attended = dot_right(d_proj, wo).astype(jnp.bfloat16)
    seg_id = 0
    qseg = queries[seg_id]
    keys = keys_all[seg_id].reshape(length, HEADS, HD)
    vals = values_all[seg_id].reshape(length, HEADS, HD)
    memory_key_rows = mem_keys[seg_id]
    memory_value_rows = mem_vals[seg_id]
    d_out = d_attended.reshape(nblocks, per_block, HEADS, HD)
    local, distant_memory = score_block(
        qseg, keys, memory_key_rows, memory_flag[seg_id], first, length
    )
    p_local = jnp.exp(local - totals[seg_id])
    p_remote = jnp.exp(distant_memory - totals[seg_id])
    dp_local = jnp.einsum("bqhd,khd->bhqk", d_out, vals, preferred_element_type=jnp.float32)
    dp_remote = jnp.einsum(
        "bqhd,bhmd->bhqm", d_out, memory_value_rows, preferred_element_type=jnp.float32
    )
    delta = jnp.sum(p_local * dp_local, axis=-1, keepdims=True) + jnp.sum(
        p_remote * dp_remote, axis=-1, keepdims=True
    )
    ds_local = (p_local * (dp_local - delta)).astype(jnp.bfloat16)
    ds_remote = (p_remote * (dp_remote - delta)).astype(jnp.bfloat16)
    d_query = jnp.einsum("bhqk,khd->bqhd", ds_local, keys, preferred_element_type=jnp.float32)
    d_query = (
        d_query
        + jnp.einsum(
            "bhqm,bhmd->bqhd", ds_remote, memory_key_rows, preferred_element_type=jnp.float32
        )
    ) * score_scale
    d_queries = d_query.astype(jnp.bfloat16).reshape(rows, width)
    lse_rows = [row_stat(totals[seg_id], rows)]
    delta_rows = [row_stat(delta, rows)]
    query_seg = query.reshape(segs, rows, width)
    dout_seg = d_attended.reshape(segs, rows, width)
    query_full, dout_full = (
        lax.all_gather(query_seg, "row", axis=1, tiled=True),
        lax.all_gather(dout_seg, "row", axis=1, tiled=True),
    )
    lse_full, delta_full = (
        lax.all_gather(jnp.stack(lse_rows, axis=0), "row", axis=1, tiled=True),
        lax.all_gather(jnp.stack(delta_rows, axis=0), "row", axis=1, tiled=True),
    )
    query_pos = jnp.arange(length)
    own_pos = first + jnp.arange(rows)
    visible = own_pos[None, None, :] <= query_pos[None, :, None]
    seg_id = 0
    q_whole = query_full[seg_id].reshape(length, HEADS, HD)
    o_whole = dout_full[seg_id].reshape(length, HEADS, HD)
    own_keys = key_local[seg_id].reshape(rows, HEADS, HD)
    own_vals = value_local[seg_id].reshape(rows, HEADS, HD)
    scores = (
        jnp.einsum("qhd,khd->hqk", q_whole, own_keys, preferred_element_type=jnp.float32)
        * score_scale
    )
    scores = jnp.where(visible, scores, NEG)
    softmax_weights = jnp.exp(scores - jnp.transpose(lse_full[seg_id])[:, :, None])
    d_probs = jnp.einsum("qhd,khd->hqk", o_whole, own_vals, preferred_element_type=jnp.float32)
    d_scores = (softmax_weights * (d_probs - jnp.transpose(delta_full[seg_id])[:, :, None])).astype(
        jnp.bfloat16
    )
    d_key = (
        jnp.einsum("hqk,qhd->khd", d_scores, q_whole, preferred_element_type=jnp.float32)
        * score_scale
    )
    d_val = jnp.einsum(
        "hqk,qhd->khd",
        softmax_weights.astype(jnp.bfloat16),
        o_whole,
        preferred_element_type=jnp.float32,
    )
    key_parts = d_key.reshape(rows, width)
    value_parts = d_val.reshape(rows, width)
    d_key_all = key_parts.astype(jnp.bfloat16)
    d_value_all = value_parts.astype(jnp.bfloat16)
    grad_query = dot_left(a_one, d_queries)
    grad_key = dot_left(a_one, d_key_all)
    grad_value = dot_left(a_one, d_value_all)
    d_a_one = dot_right(d_queries, wq) + dot_right(d_key_all, wk) + dot_right(d_value_all, wv)
    d_norm_one, grad_gain_attn = norm_back(x, gain_attn, inv_one, d_a_one)
    grad_tokens = (d_hidden + d_norm_one).astype(jnp.bfloat16).reshape(segs, rows, width)
    full_grads = (
        grad_query,
        grad_key,
        grad_value,
        grad_out,
        grad_gate,
        grad_up,
        grad_down,
        grad_gain_attn,
        grad_gain_ffn,
    )
    split_grads = tuple((g.reshape(seg_count, group, -1) for g in full_grads))
    row_summed = jax.tree.map(
        lambda part: part.astype(jnp.float32),
        lax.psum_scatter(for_sending(split_grads), "row", scatter_dimension=1, tiled=True),
    )
    owned_flat = jax.tree.map(
        lambda part: part.astype(jnp.float32),
        lax.psum_scatter(for_sending(row_summed), "seg", scatter_dimension=0, tiled=True),
    )
    owned = []
    for whole_grad, piece in zip(full_grads, owned_flat):
        own_rows = whole_grad.shape[0] // (seg_count * group)
        owned.append(piece.reshape((own_rows,) + whole_grad.shape[1:]))
    return (
        layer_out,
        grad_tokens,
        owned[0],
        owned[1],
        owned[2],
        owned[3],
        owned[4],
        owned[5],
        owned[6],
        owned[7],
        owned[8],
    )


MESH = pl.DeviceIdType.MESH
BF = jnp.bfloat16
F32 = jnp.float32
VM = pltpu.VMEM
DMA = pltpu.SemaphoreType.DMA


def device(z, y, c, x):
    return ((z * 2 + y) * 2 + c, x)


def remote(src, dst, send, recv, where):
    return pltpu.make_async_remote_copy(
        src_ref=src, dst_ref=dst, send_sem=send, recv_sem=recv, device_id=where, device_id_type=MESH
    )


def aligned(value, unit):
    return pl.multiple_of(value, unit)


def layer_kernel(
    tok, cot, mem_k, mem_v, choice, flag, w_q, w_k, w_v, w_o, w_b, w_d, gains,
    out_y, out_x, out_q, out_k, out_v, out_o, out_b, out_d, out_g,
    wa, wo, wb, wc, w_land, gc, go, c_a, c_o, c_b, c_d, y_a, y_o, y_b, y_d, z_a, z_o, z_b, z_d, z_w, x_n, x_d,
    xf, dyf, act, tr, qkv, aof, h, hid, dgu, part, swap_r, swap_s, dqkv, kv_acc, mk, mv, tr_one, tr_two, lse,
    row_s, row_r, gain, gain_acc,
    ws, wr, own_s, xs, xr, zs, zr, ys, yr, cs, cr, mem_s, es, er, rcs, rcr, rys, ryr, rzs, rzr, rxs, rxr,
):
    seg = lax.axis_index("seg")
    x = lax.axis_index("row")
    c = seg % 2
    y = (seg // 2) % 2
    z = seg // 4
    rows, width = tok.shape
    length = 2 * rows
    cols = width // 2
    heads = cols // HD
    own, peer = aligned(x * rows, rows), aligned((1 - x) * rows, rows)
    ff = wc.shape[0]
    blk = wc.shape[0] // 8
    scale = HD ** (-0.5)
    over_x, over_y, over_c = device(z, y, c, 1 - x), device(z, 1 - y, c, x), device(z, y, 1 - c, x)
    mine = x == c
    other = jnp.logical_not(mine)
    col0 = aligned(x * cols, cols)

    barrier = pltpu.get_barrier_semaphore()
    for d in range(1, 4):
        pl.semaphore_signal(barrier, inc=1, device_id=device((z + d) % 4, y, c, x), device_id_type=MESH)
    for near in (over_x, over_y, over_c):
        pl.semaphore_signal(barrier, inc=1, device_id=near, device_id_type=MESH)
    pl.semaphore_wait(barrier, 6)

    def chunk(n):
        return [(i, min(512, n - i)) for i in range(0, n, 512)]

    groups = [(wa, 0, 512), (wa, 512, 512), (wa, 1024, 640)]
    groups += [(wo, col0, cols)] + [(wb, i, n) for i, n in chunk(2 * ff)]
    n_groups = len(groups)
    y_first = (2, 7)
    inner = jnp.logical_or(z == 1, z == 2)
    end_low, end_high = z == 0, z == 3

    def block(g, zz, yy):
        if g >= n_groups:
            p = zz * 2 + yy
            return wc.at[pl.ds(aligned(p * blk, 16), blk), pl.ds((g - n_groups) * 512, 512)]
        ref, at, n = groups[g]
        return ref.at[zz, yy, c, :, pl.ds(at, n)]

    def part_of(g, which):
        half_at = aligned(which * cols, cols)
        if g < 4:
            return [w_q, w_k, w_v, w_o][g].at[:, pl.ds(half_at, cols)]
        ref, at, n = groups[g]
        return w_b.at[which, :, pl.ds(at, n)]

    def my_rows(g, which):
        ref, at, n = groups[g]
        at = aligned(which * cols, cols) if ref is wo else at
        return ref.at[z, y, c, pl.ds(aligned(x * 32, 32), 32), pl.ds(at, min(n, 512))]

    my_gain = wa.at[z, y, c, pl.ds(aligned(x * 32, 32), 32), pl.ds(3 * cols, 128)]
    my_down = w_land.at[x]
    gx, tx, dx, cx = n_groups, n_groups + 1, n_groups + 2, n_groups + 3
    first = [remote(part_of(g, 1 - x), my_rows(g, 1 - x), xs.at[g], xr.at[g], over_x) for g in range(n_groups)]
    local = [pltpu.make_async_copy(part_of(g, x), my_rows(g, x), own_s.at[g]) for g in range(n_groups)]
    first.append(remote(gains, my_gain, xs.at[gx], xr.at[gx], over_x))
    local.append(pltpu.make_async_copy(gains, my_gain, own_s.at[gx]))
    first.append(remote(tok, xf.at[pl.ds(own, rows)], xs.at[tx], xr.at[tx], over_x))
    local.append(pltpu.make_async_copy(tok, xf.at[pl.ds(own, rows)], own_s.at[tx]))
    first.append(remote(cot, dyf.at[pl.ds(own, rows)], xs.at[dx], xr.at[dx], over_x))
    local.append(pltpu.make_async_copy(cot, dyf.at[pl.ds(own, rows)], own_s.at[dx]))
    down_x = remote(w_d, my_down, xs.at[cx], xr.at[cx], over_x)
    down_l = pltpu.make_async_copy(w_d, my_down, own_s.at[cx])

    def to_z(g, d, f):
        b = block(g, z, (y + f) % 2)
        return remote(b, b, zs.at[g, f, d - 1], zr.at[g, f, d - 1], device((z + d) % 4, y, c, x))

    def relay(g, f):
        b = block(g, (z + 2) % 4, (y + f) % 2)
        return remote(b, b, zs.at[g, f, 3], zr.at[g, f, 2 * (z // 2)], device(3 * (z // 2), y, c, x))

    def start_z(g, f):
        to_z(g, 2, f).start()
        pl.when(jnp.logical_not(end_high))(lambda: to_z(g, 1, f).start())
        pl.when(jnp.logical_not(end_low))(lambda: to_z(g, 3, f).start())

    def sent_z(g, f):
        to_z(g, 2, f).wait_send()
        pl.when(jnp.logical_not(end_high))(lambda: to_z(g, 1, f).wait_send())
        pl.when(jnp.logical_not(end_low))(lambda: to_z(g, 3, f).wait_send())
        pl.when(inner)(lambda: relay(g, f).wait_send())

    near_d = jnp.where(end_low, 3, 1)

    def to_y(g, d):
        b = block(g, (z + 4 - d) % 4, y)
        return remote(b, b, ys.at[g, d], yr.at[g, d], over_y)

    def to_c(g, d, f):
        b = block(g, (z + 4 - d) % 4, (y + f) % 2)
        return remote(b, b, cs.at[g, d, f], cr.at[g, d, f], over_c)

    def gated(fn):
        def run(g, *rest):
            if g >= n_groups:
                pl.when(mine)(lambda: fn(g, *rest))
            else:
                fn(g, *rest)

        return run

    @gated
    def spread(g):
        if g < n_groups:
            first[g].wait_recv()
            local[g].wait()
            if g == 2:
                first[gx].wait_recv()
                local[gx].wait()
        elif g == n_groups:
            down_x.wait_recv()
            down_l.wait()
            pair = jnp.concatenate([w_land[0].astype(F32), w_land[1].astype(F32)], axis=0)
            wc[pl.ds(aligned((z * 2 + y) * blk, 16), blk)] = pair.astype(BF)
        start_z(g, 0)
        to_y(g, 0).start()
        to_c(g, 0, 0).start()

    def turn(g):
        if g in y_first:
            to_y(g, 0).wait_recv()
            start_z(g, 1)
            to_c(g, 0, 1).start()

    @gated
    def pass_z(g):
        for f in range(2 if g in y_first else 1):
            for d in (2, near_d, 4 - near_d):
                to_z(g, d, f).wait_recv()
                if isinstance(d, int):
                    pl.when(inner)(lambda: relay(g, f).start())
                if g not in y_first:
                    to_y(g, d).start()
                to_c(g, d, f).start()

    @gated
    def pass_y(g):
        if g not in y_first:
            for d in range(4):
                to_y(g, d).wait_recv()
                to_c(g, d, 1).start()

    def arrived(g):
        for d in range(4):
            for f in range(2):
                to_c(g, d, f).wait_recv()

    @gated
    def sent(g):
        sent_z(g, 0)
        if g in y_first:
            sent_z(g, 1)
        for d in range(4):
            if d == 0 or g not in y_first:
                to_y(g, d).wait_send()
            for f in range(2):
                to_c(g, d, f).wait_send()

    def out_half(which, core, to, k):
        b = wo.at[:, :, core, :, pl.ds(aligned(which * cols, cols), cols)]
        return remote(b, b, ws.at[k], wr.at[k], to)

    out_over = out_half(x, c, over_x, 0)
    out_next = out_half(1 - x, c, over_c, 1)

    last_group = n_groups + 1

    def step(g):
        if g + 3 - 1 <= last_group:
            turn(g + 3 - 1)
        if g <= last_group:
            pass_z(g)
        if g + 3 <= last_group:
            spread(g + 3)
        if 1 <= g <= last_group + 1:
            pass_y(g - 1)
        if g == 4:
            out_over.start()

    for g in (0, 1, 2, gx):
        first[g].start()
        local[g].start()
    local[tx].start()
    local[dx].start()
    mem_bufs = [dqkv, hid]
    n_mem = mem_k.shape[0] // length

    def mem_copy(i):
        buf = mem_bufs[i % 2]
        return [
            pltpu.make_async_copy(
                m.at[pl.ds(i * length, length), pl.ds(aligned(col0 + hh * HD, HD), HD)],
                buf.at[:, pl.ds((hh * 2 + j) * HD, HD)],
                mem_s.at[i % 2, hh * 2 + j],
            )
            for hh in range(heads)
            for j, m in enumerate((mem_k, mem_v))
        ]

    for i in range(2):
        for cp in mem_copy(i):
            cp.start()
    spread(0)
    spread(1)
    spread(2)
    for g in list(range(3, n_groups)):
        first[g].start()
        local[g].start()

    @pl.when(mine)
    def _():
        down_l.start()

    @pl.when(other)
    def _():
        down_x.start()

    first[tx].start()

    def choose(i):
        for cp in mem_copy(i):
            cp.wait()
        at = lax.broadcasted_iota(jnp.int32, (HD, length), 1) + i * length
        for hh in range(heads):
            picked = jnp.where(x == 0, choice[:, hh : hh + 1], choice[:, heads + hh : heads + hh + 1])
            hot = (picked == at).astype(F32).astype(BF)
            both = plain_dot(hot, mem_bufs[i % 2][:, hh * 2 * HD : (hh + 1) * 2 * HD])
            where = slice(hh * HD, (hh + 1) * HD)
            if i == 0:
                kv_acc[0, where, 0 : 2 * HD] = both
            else:
                kv_acc[0, where, 0 : 2 * HD] += both
        if i + 2 < n_mem:
            for cp in mem_copy(i + 2):
                cp.start()

    done = 0
    for g in range(4):
        upto = n_mem * (g + 1) // 4
        for i in range(done, upto):
            choose(i)
        done = upto
        step(g)
        if g == 2:
            first[tx].wait_recv()
            local[tx].wait()
            first[dx].start()
    for hh in range(heads):
        where = slice(hh * HD, (hh + 1) * HD)
        mk[:, where] = kv_acc[0, where, 0:HD].astype(BF)
        mv[:, where] = kv_acc[0, where, HD : 2 * HD].astype(BF)
    for g in range(3):
        arrived(g)

    @pl.loop(0, 8)
    def _(p):
        block_t = jnp.transpose(
            wa[p // 2, p % 2, :, :, 3 * cols : 3 * cols + 128].reshape(128, 128).astype(F32)
        )
        gain[:, pl.ds(aligned(p * 128, 128), 128)] = block_t[0:8]

    def norm_rows(at, n):
        xc = xf[pl.ds(at, n)].astype(F32)
        inv = lax.rsqrt(jnp.mean(xc * xc, axis=-1, keepdims=True) + EPS)
        return xc * inv, inv

    def norm_one(i):
        at = aligned(i * 64, 64)
        u, _ = norm_rows(at, 64)
        return at, (u * gain[0:1]).astype(BF)

    @pl.loop(0, length // 64)
    def _(i):
        at, a = norm_one(i)
        act[pl.ds(at, 64)] = a

    def w_cols(ref, at, n):
        return ref[:, :, :, :, pl.ds(at, n)].reshape(width, n)

    @pl.loop(0, 3 * cols // 256)
    def _(i):
        at = aligned(i * 256, 256)
        qkv[:, pl.ds(at, 256)] = plain_dot(act[...], w_cols(wa, at, 256)).astype(BF)

    def scores(hh, i, n):
        lane = pl.ds(aligned(hh * HD, HD), HD)
        query = qkv[i * HD : (i + 1) * HD, lane]
        key = qkv[0:n, pl.ds(aligned(cols + hh * HD, HD), HD)]
        local_s = dot_right(query, key) * scale
        seen = lax.broadcasted_iota(jnp.int32, (HD, n), 1) <= lax.broadcasted_iota(jnp.int32, (HD, n), 0) + i * HD
        local_s = jnp.where(seen, local_s, NEG)
        far = dot_right(query, mk[:, lane]) * scale
        far = jnp.where(flag[0:1] > 0, far, NEG)
        return query, key, local_s, far, lane

    def value_of(hh, n):
        return qkv[0:n, pl.ds(aligned(2 * cols + hh * HD, HD), HD)]

    def att_copy(i):
        part_ref = aof.at[pl.ds(i * HD, HD), pl.ds(col0, cols)]
        return remote(part_ref, part_ref, es.at[i], er.at[i], over_x)

    n_q = length // HD

    def attend(i):
        n = (i + 1) * HD

        for hh in range(heads):
            _, _, local_s, far, lane = scores(hh, i, n)
            top = jnp.maximum(jnp.max(local_s, axis=-1, keepdims=True), jnp.max(far, axis=-1, keepdims=True))
            local_e, far_e = jnp.exp(local_s - top), jnp.exp(far - top)
            total = jnp.sum(local_e, axis=-1, keepdims=True) + jnp.sum(far_e, axis=-1, keepdims=True)
            inv = 1.0 / total
            lse[i * HD : (i + 1) * HD, hh : hh + 1] = top + jnp.log(total)
            out = plain_dot((local_e * inv).astype(BF), value_of(hh, n)) + plain_dot((far_e * inv).astype(BF), mv[:, lane])
            aof[i * HD : (i + 1) * HD, pl.ds(aligned(col0 + hh * HD, HD), HD)] = out.astype(BF)

        att_copy(i).start()

    for i in range(n_q):
        attend(i)
        if i == 0:
            step(4)
        if i == 2:
            step(5)

    @pl.loop(0, n_q)
    def _(i):
        at = aligned(i * HD, HD)
        tr_one[:, pl.ds(at, HD)] = jnp.transpose(act[pl.ds(at, HD)])

    step(6)
    out_over.wait_recv()
    out_next.start()
    step(7)
    arrived(3)
    out_next.wait_recv()
    for i in range(n_q):
        att_copy(i).wait_recv()

    @pl.loop(0, width // 256)
    def _(i):
        at = aligned(i * 256, 256)
        h[:, pl.ds(at, 256)] = xf[:, pl.ds(at, 256)].astype(F32) + plain_dot(aof[...], w_cols(wo, at, 256))

    @pl.loop(0, length // 64)
    def _(i):
        at = aligned(i * 64, 64)
        hc = h[pl.ds(at, 64)]
        inv = lax.rsqrt(jnp.mean(hc * hc, axis=-1, keepdims=True) + EPS)
        act[pl.ds(at, 64)] = (hc * inv * gain[1:2]).astype(BF)

    def transpose_to(dst, src):
        @pl.loop(0, n_q)
        def _(i):
            at = aligned(i * HD, HD)
            dst[0:width, pl.ds(at, HD)] = jnp.transpose(src[pl.ds(at, HD)])

    def up_tile(j):
        at = aligned(j * 256, 256)
        both = plain_dot(act[...], w_cols(wb, at, 256))
        gate, up = both[:, :128], both[:, 128:]
        sig = 1.0 / (1.0 + jnp.exp(-gate))
        silu = gate * sig
        tile = (silu * up).astype(BF)
        lanes = pl.ds(aligned(j * 128, 128), 128)
        hid[:, lanes] = tile
        tr[lanes] = jnp.transpose(tile)
        dgu[:, pl.ds(at, 128)] = (up * sig * (1.0 + gate * (1.0 - sig))).astype(BF)
        dgu[:, pl.ds(aligned(at + 128, 128), 128)] = silu.astype(BF)

    for g in range(4, n_groups):
        if g > 5 and g != 6:
            step(g + 1)
        arrived(g)
        pl.loop((g - 4) * 2, (g - 4) * 2 + groups[g][2] // 256)(up_tile)

    first[dx].wait_recv()
    local[dx].wait()

    red = [(None, c_d, y_d, z_d, 0, 512), (None, c_d, y_d, z_d, 512, 512)]
    red += [(go if i == 0 else wb, c_b, y_b, z_b, i, n) for i, n in chunk(2 * ff)]
    z_first = {2: 0, 5: 1}
    red += [(wb, c_o, y_o, z_o, 0, 512)]
    red += [(wo, c_a, y_a, z_a, 0, 512), (wo, c_a, y_a, z_a, 512, 512)]
    red += [(go, c_a, y_a, z_a, 1024, 512), (wa, c_a, y_a, z_a, 1536, 128)]
    n_red = len(red)
    x_at = [0, 512]
    for g in range(2, n_red):
        x_at.append(sum(red[i][5] for i in range(2, g)))

    def red_c(g):
        src, cb, _, _, at, n = red[g]
        lanes = pl.ds(at, n)
        source = gc.at[:, :, :, lanes] if g < 2 else src.at[:, :, 1 - c, :, pl.ds(0 if src is go else at, n)]
        return remote(source, cb.at[:, :, :, lanes], rcs.at[g], rcr.at[g], over_c)

    def red_y(g):
        _, cb, yb, _, at, n = red[g]
        lanes = pl.ds(at, n)
        if g in z_first:
            return remote(cb.at[z, 1 - y, :, lanes], yb.at[0, :, lanes], rys.at[g], ryr.at[g], over_y)
        return remote(cb.at[:, 1 - y, :, lanes], yb.at[:, :, lanes], rys.at[g], ryr.at[g], over_y)

    def z_parts(g):
        _, cb, yb, zb, at, n = red[g]
        lanes = pl.ds(at, n)
        if g in z_first:
            return (lambda zz: cb.at[zz, :, :, lanes]), (lambda k: z_w.at[z_first[g], k])
        return (lambda zz: yb.at[zz, :, lanes]), (lambda k: zb.at[k, :, lanes])

    def red_z(g, d):
        src, dst = z_parts(g)
        zz = (z + d) % 4
        return remote(src(zz), dst(d - 1), rzs.at[g, d - 1], rzr.at[g, d - 1], device(zz, y, c, x))

    def red_far(g):
        src, dst = z_parts(g)
        return remote(src(3 - z), dst(3), rzs.at[g, 3], rzr.at[g, 3], device(1 + z // 3, y, c, x))

    def start_red_z(g):
        @pl.when(jnp.logical_not(inner))
        def _():
            red_far(g).start()
            red_z(g, 2).start()

        pl.when(jnp.logical_not(end_high))(lambda: red_z(g, 1).start())
        pl.when(jnp.logical_not(end_low))(lambda: red_z(g, 3).start())

    def merge(g):
        @pl.when(inner)
        def _():
            red_far(g).wait_recv()
            src, dst = z_parts(g)
            away = src((z + 2) % 4)
            away[...] = (away[...].astype(F32) + dst(3)[...].astype(F32)).astype(BF)
            red_z(g, 2).start()

    def wait_red_z(g):
        red_z(g, 2).wait_recv()
        pl.when(jnp.logical_not(end_low))(lambda: red_z(g, 1).wait_recv())
        pl.when(jnp.logical_not(end_high))(lambda: red_z(g, 3).wait_recv())

    def total_z(g):
        src, dst = z_parts(g)
        total = src(z)[...].astype(F32)
        for k in range(3):
            total = total + dst(k)[...].astype(F32)
        return total

    def red_x(g):
        lanes = pl.ds(x_at[g], red[g][5])
        buf = x_d if g < 2 else x_n
        return remote(buf.at[0, :, lanes], buf.at[1, :, lanes], rxs.at[g], rxr.at[g], over_x)

    def only_mine(fn):
        def run(g):
            if g < 2:
                pl.when(mine)(lambda: fn(g))
            else:
                fn(g)

        return run

    def start_c(g):
        if g < 2:
            pl.when(other)(lambda: red_c(g).start())
        else:
            red_c(g).start()

    @only_mine
    def sum_c(g):
        red_c(g).wait_recv()
        src, cb, _, _, at, n = red[g]
        lanes = pl.ds(at, n)

        @pl.loop(0, 8)
        def _(i):
            own = gc[i // 2, i % 2, :, lanes] if g < 2 else src[i // 2, i % 2, c, :, pl.ds(0 if src is go else at, n)]
            cb[i // 2, i % 2, :, lanes] = (cb[i // 2, i % 2, :, lanes].astype(F32) + own.astype(F32)).astype(BF)

        start_red_z(g) if g in z_first else red_y(g).start()

    @only_mine
    def stage_one(g):
        if g in z_first:
            merge(g)
            return
        red_y(g).wait_recv()
        _, cb, yb, _, at, n = red[g]
        lanes = pl.ds(at, n)

        @pl.loop(0, 4)
        def _(i):
            yb[i, :, lanes] = (yb[i, :, lanes].astype(F32) + cb[i, y, :, lanes].astype(F32)).astype(BF)

        start_red_z(g)

    @only_mine
    def stage_two(g):
        if g in z_first:
            wait_red_z(g)
            src, _ = z_parts(g)
            src(z)[...] = total_z(g).astype(BF)
            red_y(g).start()
        else:
            merge(g)

    def result(g, which, value):
        at, n = red[g][4], red[g][5]
        if g < 2:
            out_d[:, at : at + n] = value
        elif g < n_red - 5:
            out_b[which, :, at : at + n] = value
        elif g == n_red - 1:
            out_g[which] = value
        else:
            out = [out_o, out_q, out_k, out_v][g - (n_red - 5)]
            out[:, pl.ds(aligned(which * cols, cols), cols)] = value

    @only_mine
    def stage_three(g):
        _, cb, yb, _, at, n = red[g]
        lanes = pl.ds(at, n)
        if g in z_first:
            red_y(g).wait_recv()
            total = cb[z, y, :, lanes].astype(F32) + yb[0, :, lanes].astype(F32)
        else:
            wait_red_z(g)
            total = total_z(g)
        size = yb.shape[1] // 2
        low, high = total[:size], total[size:]
        buf = x_d if g < 2 else x_n
        buf[0, :, pl.ds(x_at[g], n)] = jnp.where(x == 0, high, low).astype(BF)
        red_x(g).start()
        result(g, x, jnp.where(x == 0, low, high))

    def finish(g):
        lanes = pl.ds(x_at[g], red[g][5])

        def take():
            red_x(g).wait_recv()
            result(g, 1 - x, (x_d if g < 2 else x_n)[1, :, lanes].astype(F32))

        if g < 2:
            pl.when(other)(take)
        else:
            take()

    @only_mine
    def red_sent(g):
        red_y(g).wait_send()
        red_z(g, 2).wait_send()
        pl.when(jnp.logical_not(end_high))(lambda: red_z(g, 1).wait_send())
        pl.when(jnp.logical_not(end_low))(lambda: red_z(g, 3).wait_send())
        pl.when(jnp.logical_not(inner))(lambda: red_far(g).wait_send())
        red_x(g).wait_send()

    done_at = {}

    def advance(stage, upto):
        fns = [sum_c, stage_one, stage_two, stage_three, finish]
        for g in range(done_at.get(stage, 0), min(upto + 1, n_red)):
            fns[stage](g)
        done_at[stage] = max(done_at.get(stage, 0), min(upto + 1, n_red))

    def tick(k, cap=n_red):
        for stage, lag in enumerate((0, 3, 5, 7, 8)):
            advance(stage, min(k - lag, cap))

    @pl.when(end_low)
    def _():
        for zb in (z_a, z_o, z_b, z_d):
            zb[0] = jnp.zeros(zb.shape[1:], BF)
        for i in range(2):
            z_w[i, 0] = jnp.zeros(z_w.shape[2:], BF)

    @pl.when(end_high)
    def _():
        for zb in (z_a, z_o, z_b, z_d):
            zb[2] = jnp.zeros(zb.shape[1:], BF)
        for i in range(2):
            z_w[i, 2] = jnp.zeros(z_w.shape[2:], BF)

    for i in range(2):

        @pl.loop(0, 4)
        def _(t):
            res = plain_dot(tr[pl.ds(aligned(t * 2 * blk, 32), 2 * blk)], dyf[:, i * 512 : (i + 1) * 512])
            gc[t, :, :, i * 512 : (i + 1) * 512] = res.reshape(2, blk, 512).astype(BF)

        start_c(i)
    step(n_groups + 1)
    advance(0, 0)
    advance(0, 1)
    step(n_groups + 2)
    transpose_to(tr_two, act)

    def wait_down():
        for g in range(n_groups, last_group + 1):
            arrived(g)

    pl.when(other)(wait_down)

    def dhid_tile(j, n):
        lanes = aligned(j * 128, 128)
        res = dot_right(dyf[...], wc[pl.ds(lanes, 128 * n)])
        for t in range(n):
            at = aligned((j + t) * 256, 256)
            d = res[:, t * 128 : (t + 1) * 128]
            for s in range(2):
                where = pl.ds(aligned(at + 128 * s, 128), 128)
                dgu[:, where] = (d * dgu[:, where].astype(F32)).astype(BF)

    n_tiles = ff // 128

    @pl.loop(0, n_tiles // 2)
    def _(t):
        dhid_tile(t * 2, 2)

    if n_tiles % 2:
        dhid_tile(n_tiles - 1, 1)

    def grad_tile(dst, lhs, value, at):
        res = plain_dot(lhs[0:width], value)
        dst[:, :, :, :, pl.ds(at, 256)] = res.reshape(4, 2, 2, 64, 256).astype(BF)

    n_b = len(chunk(2 * ff))

    def grad_ff(g):
        at0, n = red[2 + g][4], red[2 + g][5]
        for t in range(n // 256):
            grad_tile(go if g == 0 else wb, tr_two, dgu[:, at0 + t * 256 : at0 + (t + 1) * 256], at0 + t * 256)
        start_c(2 + g)

    grad_ff(0)
    gain_acc[...] = jnp.zeros_like(gain_acc)

    def swap_copy(i):
        at = pl.ds(128 * i, 128)
        return remote(swap_s.at[at], swap_r.at[at], es.at[8 + i], er.at[8 + i], over_x)

    for f in range(2):

        @pl.loop(0, width // 256)
        def _(i):
            at = aligned(i * 256, 256)
            res = dot_right(dgu[f * rows : (f + 1) * rows], wb[i, :, :, :, :].reshape(256, 2 * ff))
            part[f * rows : (f + 1) * rows, pl.ds(at, 256)] = res
            swap_s[f * rows : (f + 1) * rows, pl.ds(at, 256)] = res.astype(BF)

        swap_copy(2 * f).start()
        swap_copy(2 * f + 1).start()

    def add_gain(k, grad, unit):
        prod = grad * unit
        gain_acc[k] += jnp.sum(prod.reshape(prod.shape[0] // 8, 8, width), axis=0)

    for g in range(4, n_groups):
        sent(g)
    for g in range(1, n_b):
        grad_ff(g)
        if g == 1:
            advance(0, 2)
        if g == 2:
            advance(1, 0)
        if g == 3:
            advance(0, 3)
        if g == 4:
            advance(1, 1)
        if g == 5:
            advance(0, 4)

    def d_hidden_rows(i):
        at = aligned(i * 64, 64)
        hc = h[pl.ds(at, 64)]
        inv = lax.rsqrt(jnp.mean(hc * hc, axis=-1, keepdims=True) + EPS)
        u = hc * inv
        add_gain(1, part[pl.ds(at, 64)], u)
        e = (part[pl.ds(at, 64)] + swap_r[pl.ds(at, 64)].astype(F32)) * gain[1:2]
        dh = dyf[pl.ds(at, 64)].astype(F32) + inv * (e - u * jnp.mean(e * u, axis=-1, keepdims=True))
        part[pl.ds(at, 64)] = dh
        act[pl.ds(at, 64)] = dh.astype(BF)

    kv_acc[...] = jnp.zeros_like(kv_acc)
    w_own = wo.at[pl.ds(x * 2, 2)]

    def attend_back(i):
        n = (i + 1) * HD
        at = slice(i * HD, (i + 1) * HD)
        d_att = dot_right(act[at], w_own[...].reshape(cols, width)).astype(BF)
        for hh in range(heads):
            query, key, local_s, far, lane = scores(hh, i, n)
            log_sum = lse[at, hh : hh + 1]
            p_l, p_m = jnp.exp(local_s - log_sum), jnp.exp(far - log_sum)
            grad = d_att[:, hh * HD : (hh + 1) * HD]
            out = aof[at, pl.ds(aligned(col0 + hh * HD, HD), HD)]
            delta = jnp.sum(grad.astype(F32) * out.astype(F32), axis=-1, keepdims=True)
            ds_l = (p_l * (dot_right(grad, value_of(hh, n)) - delta)).astype(BF)
            ds_m = (p_m * (dot_right(grad, mv[:, lane]) - delta)).astype(BF)
            dq = (plain_dot(ds_l, key) + plain_dot(ds_m, mk[:, lane])) * scale
            dqkv[at, hh * HD : (hh + 1) * HD] = dq.astype(BF)
            kv_acc[0, 0:n, hh * HD : (hh + 1) * HD] += dot_left(ds_l, query)
            kv_acc[1, 0:n, hh * HD : (hh + 1) * HD] += dot_left(p_l.astype(BF), grad)

    base = 4
    for i in range(n_q):
        swap_copy(i).wait_recv()
        pl.loop(i * 2, i * 2 + 2)(d_hidden_rows)
        attend_back(i)
        if i == 0:
            transpose_to(tr, aof)
        if i == n_q - 1:

            @pl.loop(0, width // 256)
            def _(j):
                at = aligned(j * 256, 256)
                row_s[:, pl.ds(at, 256)] = plain_dot(hid[pl.ds(peer, rows)], wc[:, pl.ds(at, 256)]).astype(BF)

            row_y = remote(row_s, row_r.at[0], es.at[12], er.at[12], over_x)
            row_y.start()
        for _ in range([1,1,1,1][i]):
            tick(base, 1 + n_b)
            base += 1
    sent(3)
    out_over.wait_send()
    out_next.wait_send()
    dqkv[:, cols : 2 * cols] = (kv_acc[0] * scale).astype(BF)
    dqkv[:, 2 * cols :] = kv_acc[1].astype(BF)

    def grad_tile_one(dst, at, to):
        res = plain_dot(tr_one[...], dqkv[:, at : at + 256])
        dst[:, :, :, :, to : to + 256] = res.reshape(4, 2, 2, 64, 256).astype(BF)

    for t in range(2):
        grad_tile(wb, tr, act[:, pl.ds(aligned(col0 + t * 256, 256), 256)], t * 256)
    start_c(2 + n_b)
    for g in range(2):
        for t in range(2):
            grad_tile_one(wo, g * cols + t * 256, g * cols + t * 256)
        start_c(3 + n_b + g)
    red_c(2).wait_send()
    for t in range(2):
        grad_tile_one(go, 2 * cols + t * 256, t * 256)
    start_c(5 + n_b)
    tick(base)
    base += 1

    row_y.wait_send()
    def d_one(at):
        return jnp.concatenate([kv_acc[0, pl.ds(at, 64)], kv_acc[1, pl.ds(at, 64)]], axis=1)

    for first_half in (False, True):
        half_rows = pl.ds(own if first_half else peer, rows)

        @pl.loop(0, width // 256)
        def _(i):
            at = aligned(i * 256, 256)
            res = dot_right(dqkv[half_rows], wa[i, :, :, :, 0 : 3 * cols].reshape(256, 3 * cols))
            if not first_half:
                row_s[:, pl.ds(at, 256)] = res.astype(BF)
            kv_acc[i // 2, half_rows, pl.ds(aligned((i % 2) * 256, 256), 256)] = res

        if not first_half:
            row_x = remote(row_s, row_r.at[1], es.at[13], er.at[13], over_x)
            row_x.start()

    @pl.loop(0, length // 64)
    def _(i):
        at = aligned(i * 64, 64)
        u, _ = norm_rows(at, 64)
        add_gain(0, d_one(at), u)

    for g in range(3):
        sent(g)
    sums = [jnp.sum(gain_acc[k], axis=0, keepdims=True) for k in range(2)]
    tall = lax.broadcasted_iota(jnp.int32, (128, 128), 0)
    for p in range(8):
        lanes = slice(p * 128, (p + 1) * 128)
        both = jnp.where(tall == 0, sums[0][:, lanes], jnp.where(tall == 1, sums[1][:, lanes], 0.0))
        wa[p // 2, p % 2, :, :, 3 * cols :] = jnp.transpose(both).reshape(2, 64, 128).astype(BF)
    start_c(6 + n_b)
    tick(base)
    base += 1
    row_y.wait_recv()

    @pl.loop(0, width // 256)
    def _(i):
        at = aligned(i * 256, 256)
        mine_y = plain_dot(hid[pl.ds(own, rows)], wc[:, pl.ds(at, 256)]) + h[pl.ds(own, rows), pl.ds(at, 256)]
        out_y[:, pl.ds(at, 256)] = (mine_y + row_r[0, :, pl.ds(at, 256)].astype(F32)).astype(BF)
    tick(base)
    base += 1
    row_x.wait_recv()

    @pl.loop(0, rows // 64)
    def _(i):
        at = aligned(own + i * 64, 64)
        u, inv = norm_rows(at, 64)
        e = (d_one(at) + row_r[1, pl.ds(aligned(i * 64, 64), 64)].astype(F32)) * gain[0:1]
        out = part[pl.ds(at, 64)] + inv * (e - u * jnp.mean(e * u, axis=-1, keepdims=True))
        out_x[pl.ds(aligned(i * 64, 64), 64)] = out.astype(BF)

    for k in range(base, n_red + 8):
        tick(k)
    for cp in first:
        cp.wait_send()
    pl.when(other)(lambda: down_x.wait_send())
    for g in range(n_groups, last_group + 1):
        sent(g)
    for i in range(4):
        swap_copy(i).wait_send()
    for i in range(n_q):
        att_copy(i).wait_send()
    row_x.wait_send()
    for g in range(n_red):
        if g < 2:
            pl.when(other)(lambda: red_c(g).wait_send())
        elif g != 2:
            red_c(g).wait_send()
        red_sent(g)


def layer(tok, cot, mem_k, mem_v, choice, flag, w_q, w_k, w_v, w_o, w_b, w_d, gains):
    rows, width = tok.shape
    length = 2 * rows
    cols = width // 2
    ff2 = w_b.shape[2]
    ff = ff2 // 2
    blk = ff // 8
    na = 3 * cols + 128
    hbm, vm = pl.BlockSpec(memory_space=pl.ANY), pl.BlockSpec(memory_space=pltpu.VMEM)
    own = w_q.shape[0]
    shape = jax.ShapeDtypeStruct
    return pl.pallas_call(
        layer_kernel,
        name="layer",
        out_shape=(
            shape((rows, width), BF),
            shape((rows, width), BF),
            shape((own, width), F32),
            shape((own, width), F32),
            shape((own, width), F32),
            shape((own, width), F32),
            shape((2, own, ff2), F32),
            shape((blk // 2, width), F32),
            shape((2, own, 128), F32),
        ),
        in_specs=[hbm] * 4 + [vm] * 2 + [hbm] * 7,
        out_specs=(vm,) * 9,
        scratch_shapes=[
            VM((4, 2, 2, 64, na), BF), VM((4, 2, 2, 64, width), BF), VM((4, 2, 2, 64, ff2), BF), VM((ff, width), BF), VM((2, blk // 2, width), BF),
            VM((4, 2, blk, width), BF), VM((4, 2, 2, 64, cols), BF),
            VM((4, 2, 64, na), BF), VM((4, 2, 64, cols), BF), VM((4, 2, 64, ff2), BF), VM((4, 2, blk, width), BF),
            VM((4, 64, na), BF), VM((4, 64, cols), BF), VM((4, 64, ff2), BF), VM((4, blk, width), BF),
            VM((4, 64, na), BF), VM((4, 64, cols), BF), VM((4, 64, ff2), BF), VM((4, blk, width), BF),
            VM((2, 4, 2, 64, 512), BF),
            VM((2, own, ff2 + na + cols), BF), VM((2, blk // 2, width), BF),
            VM((length, width), BF), VM((length, width), BF), VM((length, width), BF), VM((ff, length), BF),
            VM((length, 3 * cols), BF), VM((length, width), BF), VM((length, width), F32), VM((length, ff), BF),
            VM((length, ff2), BF), VM((length, width), F32), VM((length, width), BF), VM((length, width), BF),
            VM((length, 3 * cols), BF), VM((2, length, cols), F32), VM((HD, cols), BF), VM((HD, cols), BF),
            VM((width, length), BF), VM((width, length), BF), VM((length, 128), F32),
            VM((rows, width), BF), VM((2, rows, width), BF), VM((8, width), F32), VM((2, 8, width), F32),
            DMA((2,)), DMA((2,)), DMA((16,)), DMA((16,)), DMA((16,)), DMA((12, 2, 4)), DMA((12, 2, 4)),
            DMA((12, 4)), DMA((12, 4)), DMA((12, 4, 2)), DMA((12, 4, 2)), DMA((2, 8)), DMA((14,)), DMA((14,)),
            DMA((13,)), DMA((13,)), DMA((13,)), DMA((13,)), DMA((13, 4)), DMA((13, 4)), DMA((13,)), DMA((13,)),
        ],
        compiler_params=pltpu.CompilerParams(collective_id=0, has_side_effects=True, vmem_limit_bytes=127 << 19),
    )(tok, cot, mem_k, mem_v, choice, flag, w_q, w_k, w_v, w_o, w_b, w_d, gains)


def prepare_kernel(w_g, w_u, norms, choice, flag, w_b, gains, columns, flags):
    wide = w_g.shape[1]
    strip = wide // 16
    for half in range(2):
        packed = []
        for w in (w_g, w_u):
            whole = w[...].astype(F32)
            cuts = [whole[:, (2 * p + half) * strip : (2 * p + half + 1) * strip] for p in range(8)]
            packed.append(jnp.concatenate(cuts, axis=1).astype(BF))
        for j in range(wide // 256):
            for i in range(2):
                w_b[half, :, (2 * j + i) * 128 : (2 * j + i + 1) * 128] = packed[i][:, j * 128 : (j + 1) * 128]
    own = norms.shape[1]
    tall = lax.broadcasted_iota(jnp.int32, (128, own), 0)
    both = norms[...].astype(F32)
    both = jnp.where(tall == 0, both[0:1], jnp.where(tall == 1, both[1:2], 0.0))
    gains[...] = jnp.transpose(both).astype(BF)
    many = jnp.concatenate([choice[...].astype(F32)] * (128 // choice.shape[0]), axis=0)
    columns[...] = jnp.transpose(many).astype(jnp.int32)
    flags[...] = jnp.full(flags.shape, flag[0], jnp.int32)


def prepare(w_g, w_u, norms, choice, flag):
    own, wide = w_g.shape
    vm = pl.BlockSpec()
    shape = jax.ShapeDtypeStruct
    return pl.pallas_call(
        prepare_kernel,
        name="prepare",
        out_shape=(
            shape((2, own, wide), BF), shape((own, 128), BF), shape((128, 128), jnp.int32), shape((8, 128), jnp.int32),
        ),
        in_specs=[vm] * 4 + [pl.BlockSpec(memory_space=pltpu.SMEM)],
        out_specs=(vm,) * 4,
        compiler_params=pltpu.CompilerParams(vmem_limit_bytes=63 << 20),
    )(w_g, w_u, norms, choice, flag)


def complete_kernel(i_y, i_x, i_q, i_k, i_v, i_o, i_b, i_d, i_g, y, x, q, k, v, o, g, u, d, n_a, n_f):
    for src, dst in ((i_y, y), (i_x, x), (i_q, q), (i_k, k), (i_v, v), (i_o, o), (i_d, d)):
        dst[...] = src[...]
    wide = g.shape[1]
    strip = wide // 16
    for i, dst in enumerate((g, u)):
        halves = [
            jnp.concatenate(
                [i_b[half, :, (2 * j + i) * 128 : (2 * j + i + 1) * 128] for j in range(wide // 256)], axis=1
            )
            for half in range(2)
        ]
        cuts = [halves[p % 2][:, (p // 2) * strip : (p // 2 + 1) * strip] for p in range(16)]
        dst[...] = jnp.concatenate(cuts, axis=1)
    own = n_a.shape[1]
    tall = jnp.transpose(i_g[0] + i_g[1])
    n_a[...] = tall[0:1, 0:own]
    n_f[...] = tall[1:2, 0:own]


def complete(*parts):
    own, width = parts[2].shape
    wide = parts[6].shape[2]
    vm = pl.BlockSpec()
    shape = jax.ShapeDtypeStruct
    like = [shape(p.shape, p.dtype) for p in parts[:6]]
    like += [shape((own, wide), F32)] * 2 + [shape(parts[7].shape, F32)] + [shape((1, own), F32)] * 2
    return pl.pallas_call(
        complete_kernel,
        name="complete",
        out_shape=tuple(like),
        in_specs=[vm] * 9,
        out_specs=(vm,) * 11,
        compiler_params=pltpu.CompilerParams(vmem_limit_bytes=63 << 20),
    )(*parts)


def fast_body(
    tokens, cotangent, memory_keys, memory_values, memory_choice, memory_flag,
    w_query, w_key, w_value, w_out, w_gate, w_up, w_down, norm_attn, norm_ffn,
):
    norms = jnp.stack([norm_attn, norm_ffn])
    w_b, gains, choice, flag = prepare(w_gate, w_up, norms, memory_choice[0, 0], memory_flag)
    parts = layer(
        tokens[0], cotangent[0], memory_keys[0], memory_values[0], choice, flag,
        w_query, w_key, w_value, w_out, w_b, w_down, gains,
    )
    y, x, q, k, v, o, g, u, d, n_a, n_f = complete(*parts)
    return y[None], x[None], q, k, v, o, g, u, d, n_a[0], n_f[0]


def solution(mesh):
    in_specs = (
        P("seg", "row", None),
        P("seg", "row", None),
        P("seg", None, None),
        P("seg", None, None),
        P("seg", None, None, None),
        P("seg"),
        P(("seg", "row"), None),
        P(("seg", "row"), None),
        P(("seg", "row"), None),
        P(("seg", "row"), None),
        P(("seg", "row"), None),
        P(("seg", "row"), None),
        P(("seg", "row"), None),
        P(("seg", "row")),
        P(("seg", "row")),
    )
    out_specs = (
        P("seg", "row", None),
        P("seg", "row", None),
        P(("seg", "row"), None),
        P(("seg", "row"), None),
        P(("seg", "row"), None),
        P(("seg", "row"), None),
        P(("seg", "row"), None),
        P(("seg", "row"), None),
        P(("seg", "row"), None),
        P(("seg", "row")),
        P(("seg", "row")),
    )

    def body(*args):
        segs, rows, width = args[0].shape
        fits = (
            mesh.shape["row"] == 2
            and mesh.shape["seg"] == 16
            and segs == 1
            and (rows, width) == (256, 1024)
            and args[4].shape[1] == 1
        )
        return (fast_body if fits else general_body)(*args)

    return jax.shard_map(body, mesh=mesh, in_specs=in_specs, out_specs=out_specs, check_vma=False)
```

```python
import functools

import jax
import jax.numpy as jnp
from jax import lax
from jax.experimental import pallas as pl
from jax.experimental.pallas import tpu as pltpu
from jax.sharding import PartitionSpec as P

HEADS = 8
HD = 128
QBLK = 512


EPS = 1e-06
NEG = -1000000000.0


def for_sending(array):

    def short(part):
        return part.astype(jnp.bfloat16) if part.dtype == jnp.float32 else part

    return jax.tree.map(short, array)


def plain_dot(left, right):
    return jnp.dot(left, right, preferred_element_type=jnp.float32)


def dot_left(left, right):
    return lax.dot_general(
        left, right, (((0,), (0,)), ((), ())), preferred_element_type=jnp.float32
    )


def dot_right(left, right):
    return lax.dot_general(
        left, right, (((1,), (1,)), ((), ())), preferred_element_type=jnp.float32
    )


def norm_apply(value, gain):
    inverse = lax.rsqrt(jnp.mean(value * value, axis=-1, keepdims=True) + EPS)
    return (value * inverse * gain, inverse)


def norm_back(value, gain, inverse, grad):
    unit = value * inverse
    gain_grad = jnp.sum(grad * unit, axis=0)
    scaled = grad * gain
    return (inverse * (scaled - unit * jnp.mean(scaled * unit, axis=-1, keepdims=True)), gain_grad)


def score_block(queries, keys, memory_key_rows, flag, first, length):
    score_scale = HD ** (-0.5)
    local = (
        jnp.einsum("bqhd,khd->bhqk", queries, keys, preferred_element_type=jnp.float32)
        * score_scale
    )
    distant_memory = (
        jnp.einsum("bqhd,bhmd->bhqm", queries, memory_key_rows, preferred_element_type=jnp.float32)
        * score_scale
    )
    nblocks, per_block = (queries.shape[0], queries.shape[1])
    pos = first + jnp.arange(nblocks * per_block).reshape(nblocks, 1, per_block, 1)
    key_pos = jnp.arange(length)
    local = jnp.where(key_pos[None, None, None, :] <= pos, local, NEG)
    distant_memory = jnp.where(flag > 0, distant_memory, NEG)
    return (local, distant_memory)


def row_stat(stat, rows):
    return jnp.transpose(stat[..., 0], (0, 2, 1)).reshape(rows, HEADS)


def general_body(
    tokens,
    cotangent,
    memory_keys,
    memory_values,
    memory_choice,
    memory_flag,
    w_query,
    w_key,
    w_value,
    w_out,
    w_gate,
    w_up,
    w_down,
    norm_attn,
    norm_ffn,
):
    segs, rows, width = tokens.shape
    group = lax.axis_size("row")
    seg_count = lax.axis_size("seg")
    length = rows * group
    first = lax.axis_index("row") * rows
    nblocks = max(rows // QBLK, 1)
    per_block = rows // nblocks
    score_scale = HD ** (-0.5)
    shards = (w_query, w_key, w_value, w_out, w_gate, w_up, w_down, norm_attn, norm_ffn)
    wq, wk, wv, wo, wg, wu, wd, gain_one, gain_two = (
        lax.all_gather(shards[0], ("seg", "row"), axis=0, tiled=True),
        lax.all_gather(shards[1], ("seg", "row"), axis=0, tiled=True),
        lax.all_gather(shards[2], ("seg", "row"), axis=0, tiled=True),
        lax.all_gather(shards[3], ("seg", "row"), axis=0, tiled=True),
        lax.all_gather(shards[4], ("seg", "row"), axis=0, tiled=True),
        lax.all_gather(shards[5], ("seg", "row"), axis=0, tiled=True),
        lax.all_gather(shards[6], ("seg", "row"), axis=0, tiled=True),
        lax.all_gather(shards[7], ("seg", "row"), axis=0, tiled=True),
        lax.all_gather(shards[8], ("seg", "row"), axis=0, tiled=True),
    )
    gain_attn = gain_one.astype(jnp.float32)
    gain_ffn = gain_two.astype(jnp.float32)
    x = tokens.reshape(segs * rows, width).astype(jnp.float32)
    normed, inv_one = norm_apply(x, gain_attn)
    a_one = normed.astype(jnp.bfloat16)
    query = plain_dot(a_one, wq).astype(jnp.bfloat16)
    key_local = plain_dot(a_one, wk).astype(jnp.bfloat16).reshape(segs, rows, width)
    value_local = plain_dot(a_one, wv).astype(jnp.bfloat16).reshape(segs, rows, width)
    keys_all, values_all = (
        lax.all_gather(key_local, "row", axis=1, tiled=True),
        lax.all_gather(value_local, "row", axis=1, tiled=True),
    )
    block_first = first // QBLK
    chosen = lax.dynamic_slice_in_dim(memory_choice, block_first, nblocks, axis=1)
    head_col = jnp.arange(HEADS)[None, :, None]
    seg_id = 0
    memory_key_rows = memory_keys[seg_id].reshape(-1, HEADS, HD)[chosen[seg_id], head_col]
    memory_value_rows = memory_values[seg_id].reshape(-1, HEADS, HD)[chosen[seg_id], head_col]
    qseg = query.reshape(nblocks, per_block, HEADS, HD)
    keys = keys_all[seg_id].reshape(length, HEADS, HD)
    vals = values_all[seg_id].reshape(length, HEADS, HD)
    local, distant_memory = score_block(
        qseg, keys, memory_key_rows, memory_flag[seg_id], first, length
    )
    top = jnp.maximum(
        jnp.max(local, axis=-1, keepdims=True), jnp.max(distant_memory, axis=-1, keepdims=True)
    )
    summed = jnp.sum(jnp.exp(local - top), axis=-1, keepdims=True) + jnp.sum(
        jnp.exp(distant_memory - top), axis=-1, keepdims=True
    )
    total = top + jnp.log(summed)
    p_local = jnp.exp(local - total).astype(jnp.bfloat16)
    p_remote = jnp.exp(distant_memory - total).astype(jnp.bfloat16)
    attention_output = jnp.einsum(
        "bhqk,khd->bqhd", p_local, vals, preferred_element_type=jnp.float32
    )
    attention_output = attention_output + jnp.einsum(
        "bhqm,bhmd->bqhd", p_remote, memory_value_rows, preferred_element_type=jnp.float32
    )
    outputs = attention_output.reshape(rows, width)
    mem_keys = [memory_key_rows]
    mem_vals = [memory_value_rows]
    queries = [qseg]
    totals = [total]
    attended = outputs.astype(jnp.bfloat16)
    hidden_in = x + plain_dot(attended, wo)
    normed_two, inv_two = norm_apply(hidden_in, gain_ffn)
    a_two = normed_two.astype(jnp.bfloat16)
    gate = plain_dot(a_two, wg)
    up = plain_dot(a_two, wu)
    act = jax.nn.silu(gate)
    hid = (act * up).astype(jnp.bfloat16)
    layer_out = (hidden_in + plain_dot(hid, wd)).astype(jnp.bfloat16).reshape(segs, rows, width)
    wq, wk, wv, wo, wg, wu, wd, gain_one, gain_two = (
        lax.all_gather(shards[0], ("seg", "row"), axis=0, tiled=True),
        lax.all_gather(shards[1], ("seg", "row"), axis=0, tiled=True),
        lax.all_gather(shards[2], ("seg", "row"), axis=0, tiled=True),
        lax.all_gather(shards[3], ("seg", "row"), axis=0, tiled=True),
        lax.all_gather(shards[4], ("seg", "row"), axis=0, tiled=True),
        lax.all_gather(shards[5], ("seg", "row"), axis=0, tiled=True),
        lax.all_gather(shards[6], ("seg", "row"), axis=0, tiled=True),
        lax.all_gather(shards[7], ("seg", "row"), axis=0, tiled=True),
        lax.all_gather(shards[8], ("seg", "row"), axis=0, tiled=True),
    )
    gain_attn = gain_one.astype(jnp.float32)
    gain_ffn = gain_two.astype(jnp.float32)
    grad_y = cotangent.reshape(segs * rows, width)
    grad_down = dot_left(hid, grad_y)
    d_hid = dot_right(grad_y, wd)
    sig = jax.nn.sigmoid(gate)
    d_gate = (d_hid * up * sig * (1.0 + gate * (1.0 - sig))).astype(jnp.bfloat16)
    d_up = (d_hid * act).astype(jnp.bfloat16)
    grad_gate = dot_left(a_two, d_gate)
    grad_up = dot_left(a_two, d_up)
    d_a_two = dot_right(d_gate, wg) + dot_right(d_up, wu)
    d_norm_two, grad_gain_ffn = norm_back(hidden_in, gain_ffn, inv_two, d_a_two)
    d_hidden = grad_y.astype(jnp.float32) + d_norm_two
    d_proj = d_hidden.astype(jnp.bfloat16)
    grad_out = dot_left(attended, d_proj)
    d_attended = dot_right(d_proj, wo).astype(jnp.bfloat16)
    seg_id = 0
    qseg = queries[seg_id]
    keys = keys_all[seg_id].reshape(length, HEADS, HD)
    vals = values_all[seg_id].reshape(length, HEADS, HD)
    memory_key_rows = mem_keys[seg_id]
    memory_value_rows = mem_vals[seg_id]
    d_out = d_attended.reshape(nblocks, per_block, HEADS, HD)
    local, distant_memory = score_block(
        qseg, keys, memory_key_rows, memory_flag[seg_id], first, length
    )
    p_local = jnp.exp(local - totals[seg_id])
    p_remote = jnp.exp(distant_memory - totals[seg_id])
    dp_local = jnp.einsum("bqhd,khd->bhqk", d_out, vals, preferred_element_type=jnp.float32)
    dp_remote = jnp.einsum(
        "bqhd,bhmd->bhqm", d_out, memory_value_rows, preferred_element_type=jnp.float32
    )
    delta = jnp.sum(p_local * dp_local, axis=-1, keepdims=True) + jnp.sum(
        p_remote * dp_remote, axis=-1, keepdims=True
    )
    ds_local = (p_local * (dp_local - delta)).astype(jnp.bfloat16)
    ds_remote = (p_remote * (dp_remote - delta)).astype(jnp.bfloat16)
    d_query = jnp.einsum("bhqk,khd->bqhd", ds_local, keys, preferred_element_type=jnp.float32)
    d_query = (
        d_query
        + jnp.einsum(
            "bhqm,bhmd->bqhd", ds_remote, memory_key_rows, preferred_element_type=jnp.float32
        )
    ) * score_scale
    d_queries = d_query.astype(jnp.bfloat16).reshape(rows, width)
    lse_rows = [row_stat(totals[seg_id], rows)]
    delta_rows = [row_stat(delta, rows)]
    query_seg = query.reshape(segs, rows, width)
    dout_seg = d_attended.reshape(segs, rows, width)
    query_full, dout_full = (
        lax.all_gather(query_seg, "row", axis=1, tiled=True),
        lax.all_gather(dout_seg, "row", axis=1, tiled=True),
    )
    lse_full, delta_full = (
        lax.all_gather(jnp.stack(lse_rows, axis=0), "row", axis=1, tiled=True),
        lax.all_gather(jnp.stack(delta_rows, axis=0), "row", axis=1, tiled=True),
    )
    query_pos = jnp.arange(length)
    own_pos = first + jnp.arange(rows)
    visible = own_pos[None, None, :] <= query_pos[None, :, None]
    seg_id = 0
    q_whole = query_full[seg_id].reshape(length, HEADS, HD)
    o_whole = dout_full[seg_id].reshape(length, HEADS, HD)
    own_keys = key_local[seg_id].reshape(rows, HEADS, HD)
    own_vals = value_local[seg_id].reshape(rows, HEADS, HD)
    scores = (
        jnp.einsum("qhd,khd->hqk", q_whole, own_keys, preferred_element_type=jnp.float32)
        * score_scale
    )
    scores = jnp.where(visible, scores, NEG)
    softmax_weights = jnp.exp(scores - jnp.transpose(lse_full[seg_id])[:, :, None])
    d_probs = jnp.einsum("qhd,khd->hqk", o_whole, own_vals, preferred_element_type=jnp.float32)
    d_scores = (softmax_weights * (d_probs - jnp.transpose(delta_full[seg_id])[:, :, None])).astype(
        jnp.bfloat16
    )
    d_key = (
        jnp.einsum("hqk,qhd->khd", d_scores, q_whole, preferred_element_type=jnp.float32)
        * score_scale
    )
    d_val = jnp.einsum(
        "hqk,qhd->khd",
        softmax_weights.astype(jnp.bfloat16),
        o_whole,
        preferred_element_type=jnp.float32,
    )
    key_parts = d_key.reshape(rows, width)
    value_parts = d_val.reshape(rows, width)
    d_key_all = key_parts.astype(jnp.bfloat16)
    d_value_all = value_parts.astype(jnp.bfloat16)
    grad_query = dot_left(a_one, d_queries)
    grad_key = dot_left(a_one, d_key_all)
    grad_value = dot_left(a_one, d_value_all)
    d_a_one = dot_right(d_queries, wq) + dot_right(d_key_all, wk) + dot_right(d_value_all, wv)
    d_norm_one, grad_gain_attn = norm_back(x, gain_attn, inv_one, d_a_one)
    grad_tokens = (d_hidden + d_norm_one).astype(jnp.bfloat16).reshape(segs, rows, width)
    full_grads = (
        grad_query,
        grad_key,
        grad_value,
        grad_out,
        grad_gate,
        grad_up,
        grad_down,
        grad_gain_attn,
        grad_gain_ffn,
    )
    split_grads = tuple((g.reshape(seg_count, group, -1) for g in full_grads))
    row_summed = jax.tree.map(
        lambda part: part.astype(jnp.float32),
        lax.psum_scatter(for_sending(split_grads), "row", scatter_dimension=1, tiled=True),
    )
    owned_flat = jax.tree.map(
        lambda part: part.astype(jnp.float32),
        lax.psum_scatter(for_sending(row_summed), "seg", scatter_dimension=0, tiled=True),
    )
    owned = []
    for whole_grad, piece in zip(full_grads, owned_flat):
        own_rows = whole_grad.shape[0] // (seg_count * group)
        owned.append(piece.reshape((own_rows,) + whole_grad.shape[1:]))
    return (
        layer_out,
        grad_tokens,
        owned[0],
        owned[1],
        owned[2],
        owned[3],
        owned[4],
        owned[5],
        owned[6],
        owned[7],
        owned[8],
    )


MESH = pl.DeviceIdType.MESH
BF = jnp.bfloat16
F32 = jnp.float32
VM = pltpu.VMEM
DMA = pltpu.SemaphoreType.DMA


def device(z, y, c, x):
    return ((z * 2 + y) * 2 + c, x)


def remote(src, dst, send, recv, where):
    return pltpu.make_async_remote_copy(
        src_ref=src, dst_ref=dst, send_sem=send, recv_sem=recv, device_id=where, device_id_type=MESH
    )


def aligned(value, unit):
    return pl.multiple_of(value, unit)


def layer_kernel(
    tok, cot, mem_k, mem_v, choice, flag, w_q, w_k, w_v, w_o, w_b, w_d, gains,
    out_y, out_x, out_q, out_k, out_v, out_o, out_b, out_d, out_g,
    wa, wo, wb, wc, w_land, gc, go, c_a, c_o, c_b, c_d, y_a, y_o, y_b, y_d, z_a, z_o, z_b, z_d, z_w, x_n, x_d,
    xf, dyf, act, tr, qkv, aof, h, hid, dgu, part, swap_r, swap_s, dqkv, kv_acc, mk, mv, tr_one, tr_two, lse,
    row_s, row_r, gain, gain_acc,
    ws, wr, own_s, xs, xr, zs, zr, ys, yr, cs, cr, mem_s, es, er, rcs, rcr, rys, ryr, rzs, rzr, rxs, rxr,
):
    seg = lax.axis_index("seg")
    x = lax.axis_index("row")
    c = seg % 2
    y = (seg // 2) % 2
    z = seg // 4
    rows, width = tok.shape
    length = 2 * rows
    cols = width // 2
    heads = cols // HD
    own, peer = aligned(x * rows, rows), aligned((1 - x) * rows, rows)
    ff = wc.shape[0]
    blk = wc.shape[0] // 8
    scale = HD ** (-0.5)
    over_x, over_y, over_c = device(z, y, c, 1 - x), device(z, 1 - y, c, x), device(z, y, 1 - c, x)
    mine = x == c
    other = jnp.logical_not(mine)
    col0 = aligned(x * cols, cols)

    barrier = pltpu.get_barrier_semaphore()
    for d in range(1, 4):
        pl.semaphore_signal(barrier, inc=1, device_id=device((z + d) % 4, y, c, x), device_id_type=MESH)
    for near in (over_x, over_y, over_c):
        pl.semaphore_signal(barrier, inc=1, device_id=near, device_id_type=MESH)
    pl.semaphore_wait(barrier, 6)

    def chunk(n):
        return [(i, min(512, n - i)) for i in range(0, n, 512)]

    groups = [(wa, 0, 512), (wa, 512, 512), (wa, 1024, 640)]
    groups += [(wo, col0, cols)] + [(wb, i, n) for i, n in chunk(2 * ff)]
    n_groups = len(groups)
    y_first = (2, 7)
    inner = jnp.logical_or(z == 1, z == 2)
    end_low, end_high = z == 0, z == 3

    def block(g, zz, yy):
        if g >= n_groups:
            p = zz * 2 + yy
            return wc.at[pl.ds(aligned(p * blk, 16), blk), pl.ds((g - n_groups) * 512, 512)]
        ref, at, n = groups[g]
        return ref.at[zz, yy, c, :, pl.ds(at, n)]

    def part_of(g, which):
        half_at = aligned(which * cols, cols)
        if g < 4:
            return [w_q, w_k, w_v, w_o][g].at[:, pl.ds(half_at, cols)]
        ref, at, n = groups[g]
        return w_b.at[which, :, pl.ds(at, n)]

    def my_rows(g, which):
        ref, at, n = groups[g]
        at = aligned(which * cols, cols) if ref is wo else at
        return ref.at[z, y, c, pl.ds(aligned(x * 32, 32), 32), pl.ds(at, min(n, 512))]

    my_gain = wa.at[z, y, c, pl.ds(aligned(x * 32, 32), 32), pl.ds(3 * cols, 128)]
    my_down = w_land.at[x]
    gx, tx, dx, cx = n_groups, n_groups + 1, n_groups + 2, n_groups + 3
    first = [remote(part_of(g, 1 - x), my_rows(g, 1 - x), xs.at[g], xr.at[g], over_x) for g in range(n_groups)]
    local = [pltpu.make_async_copy(part_of(g, x), my_rows(g, x), own_s.at[g]) for g in range(n_groups)]
    first.append(remote(gains, my_gain, xs.at[gx], xr.at[gx], over_x))
    local.append(pltpu.make_async_copy(gains, my_gain, own_s.at[gx]))
    first.append(remote(tok, xf.at[pl.ds(own, rows)], xs.at[tx], xr.at[tx], over_x))
    local.append(pltpu.make_async_copy(tok, xf.at[pl.ds(own, rows)], own_s.at[tx]))
    first.append(remote(cot, dyf.at[pl.ds(own, rows)], xs.at[dx], xr.at[dx], over_x))
    local.append(pltpu.make_async_copy(cot, dyf.at[pl.ds(own, rows)], own_s.at[dx]))
    down_x = remote(w_d, my_down, xs.at[cx], xr.at[cx], over_x)
    down_l = pltpu.make_async_copy(w_d, my_down, own_s.at[cx])

    def to_z(g, d, f):
        b = block(g, z, (y + f) % 2)
        return remote(b, b, zs.at[g, f, d - 1], zr.at[g, f, d - 1], device((z + d) % 4, y, c, x))

    def relay(g, f):
        b = block(g, (z + 2) % 4, (y + f) % 2)
        return remote(b, b, zs.at[g, f, 3], zr.at[g, f, 2 * (z // 2)], device(3 * (z // 2), y, c, x))

    def start_z(g, f):
        to_z(g, 2, f).start()
        pl.when(jnp.logical_not(end_high))(lambda: to_z(g, 1, f).start())
        pl.when(jnp.logical_not(end_low))(lambda: to_z(g, 3, f).start())

    def sent_z(g, f):
        to_z(g, 2, f).wait_send()
        pl.when(jnp.logical_not(end_high))(lambda: to_z(g, 1, f).wait_send())
        pl.when(jnp.logical_not(end_low))(lambda: to_z(g, 3, f).wait_send())
        pl.when(inner)(lambda: relay(g, f).wait_send())

    near_d = jnp.where(end_low, 3, 1)

    def to_y(g, d):
        b = block(g, (z + 4 - d) % 4, y)
        return remote(b, b, ys.at[g, d], yr.at[g, d], over_y)

    def to_c(g, d, f):
        b = block(g, (z + 4 - d) % 4, (y + f) % 2)
        return remote(b, b, cs.at[g, d, f], cr.at[g, d, f], over_c)

    def gated(fn):
        def run(g, *rest):
            if g >= n_groups:
                pl.when(mine)(lambda: fn(g, *rest))
            else:
                fn(g, *rest)

        return run

    @gated
    def spread(g):
        if g < n_groups:
            first[g].wait_recv()
            local[g].wait()
            if g == 2:
                first[gx].wait_recv()
                local[gx].wait()
        elif g == n_groups:
            down_x.wait_recv()
            down_l.wait()
            pair = jnp.concatenate([w_land[0].astype(F32), w_land[1].astype(F32)], axis=0)
            wc[pl.ds(aligned((z * 2 + y) * blk, 16), blk)] = pair.astype(BF)
        start_z(g, 0)
        to_y(g, 0).start()
        to_c(g, 0, 0).start()

    def turn(g):
        if g in y_first:
            to_y(g, 0).wait_recv()
            start_z(g, 1)
            to_c(g, 0, 1).start()

    @gated
    def pass_z(g):
        for f in range(2 if g in y_first else 1):
            for d in (2, near_d, 4 - near_d):
                to_z(g, d, f).wait_recv()
                if isinstance(d, int):
                    pl.when(inner)(lambda: relay(g, f).start())
                if g not in y_first:
                    to_y(g, d).start()
                to_c(g, d, f).start()

    @gated
    def pass_y(g):
        if g not in y_first:
            for d in range(4):
                to_y(g, d).wait_recv()
                to_c(g, d, 1).start()

    def arrived(g):
        for d in range(4):
            for f in range(2):
                to_c(g, d, f).wait_recv()

    @gated
    def sent(g):
        sent_z(g, 0)
        if g in y_first:
            sent_z(g, 1)
        for d in range(4):
            if d == 0 or g not in y_first:
                to_y(g, d).wait_send()
            for f in range(2):
                to_c(g, d, f).wait_send()

    def out_half(which, core, to, k):
        b = wo.at[:, :, core, :, pl.ds(aligned(which * cols, cols), cols)]
        return remote(b, b, ws.at[k], wr.at[k], to)

    out_over = out_half(x, c, over_x, 0)
    out_next = out_half(1 - x, c, over_c, 1)

    last_group = n_groups + 1

    def step(g):
        if g + 3 - 1 <= last_group:
            turn(g + 3 - 1)
        if g <= last_group:
            pass_z(g)
        if g + 3 <= last_group:
            spread(g + 3)
        if 1 <= g <= last_group + 1:
            pass_y(g - 1)
        if g == 4:
            out_over.start()

    for g in (0, 1, 2, gx):
        first[g].start()
        local[g].start()
    local[tx].start()
    local[dx].start()
    mem_bufs = [dqkv, hid]
    n_mem = mem_k.shape[0] // length

    def mem_copy(i):
        buf = mem_bufs[i % 2]
        return [
            pltpu.make_async_copy(
                m.at[pl.ds(i * length, length), pl.ds(aligned(col0 + hh * HD, HD), HD)],
                buf.at[:, pl.ds((hh * 2 + j) * HD, HD)],
                mem_s.at[i % 2, hh * 2 + j],
            )
            for hh in range(heads)
            for j, m in enumerate((mem_k, mem_v))
        ]

    for i in range(2):
        for cp in mem_copy(i):
            cp.start()
    spread(0)
    spread(1)
    spread(2)
    for g in list(range(3, n_groups)):
        first[g].start()
        local[g].start()

    @pl.when(mine)
    def _():
        down_l.start()

    @pl.when(other)
    def _():
        down_x.start()

    first[tx].start()

    def choose(i):
        for cp in mem_copy(i):
            cp.wait()
        at = lax.broadcasted_iota(jnp.int32, (HD, length), 1) + i * length
        for hh in range(heads):
            picked = jnp.where(x == 0, choice[:, hh : hh + 1], choice[:, heads + hh : heads + hh + 1])
            hot = (picked == at).astype(F32).astype(BF)
            both = plain_dot(hot, mem_bufs[i % 2][:, hh * 2 * HD : (hh + 1) * 2 * HD])
            where = slice(hh * HD, (hh + 1) * HD)
            if i == 0:
                kv_acc[0, where, 0 : 2 * HD] = both
            else:
                kv_acc[0, where, 0 : 2 * HD] += both
        if i + 2 < n_mem:
            for cp in mem_copy(i + 2):
                cp.start()

    done = 0
    for g in range(4):
        upto = n_mem * (g + 1) // 4
        for i in range(done, upto):
            choose(i)
        done = upto
        step(g)
        if g == 2:
            first[tx].wait_recv()
            local[tx].wait()
            first[dx].start()
    for hh in range(heads):
        where = slice(hh * HD, (hh + 1) * HD)
        mk[:, where] = kv_acc[0, where, 0:HD].astype(BF)
        mv[:, where] = kv_acc[0, where, HD : 2 * HD].astype(BF)
    for g in range(3):
        arrived(g)

    @pl.loop(0, 8)
    def _(p):
        block_t = jnp.transpose(
            wa[p // 2, p % 2, :, :, 3 * cols : 3 * cols + 128].reshape(128, 128).astype(F32)
        )
        gain[:, pl.ds(aligned(p * 128, 128), 128)] = block_t[0:8]

    def norm_rows(at, n):
        xc = xf[pl.ds(at, n)].astype(F32)
        inv = lax.rsqrt(jnp.mean(xc * xc, axis=-1, keepdims=True) + EPS)
        return xc * inv, inv

    def norm_one(i):
        at = aligned(i * 64, 64)
        u, _ = norm_rows(at, 64)
        return at, (u * gain[0:1]).astype(BF)

    @pl.loop(0, length // 64)
    def _(i):
        at, a = norm_one(i)
        act[pl.ds(at, 64)] = a

    def w_cols(ref, at, n):
        return ref[:, :, :, :, pl.ds(at, n)].reshape(width, n)

    @pl.loop(0, 3 * cols // 256)
    def _(i):
        at = aligned(i * 256, 256)
        qkv[:, pl.ds(at, 256)] = plain_dot(act[...], w_cols(wa, at, 256)).astype(BF)

    def scores(hh, i, n):
        lane = pl.ds(aligned(hh * HD, HD), HD)
        query = qkv[i * HD : (i + 1) * HD, lane]
        key = qkv[0:n, pl.ds(aligned(cols + hh * HD, HD), HD)]
        local_s = dot_right(query, key) * scale
        seen = lax.broadcasted_iota(jnp.int32, (HD, n), 1) <= lax.broadcasted_iota(jnp.int32, (HD, n), 0) + i * HD
        local_s = jnp.where(seen, local_s, NEG)
        far = dot_right(query, mk[:, lane]) * scale
        far = jnp.where(flag[0:1] > 0, far, NEG)
        return query, key, local_s, far, lane

    def value_of(hh, n):
        return qkv[0:n, pl.ds(aligned(2 * cols + hh * HD, HD), HD)]

    def att_copy(i):
        part_ref = aof.at[pl.ds(i * HD, HD), pl.ds(col0, cols)]
        return remote(part_ref, part_ref, es.at[i], er.at[i], over_x)

    n_q = length // HD

    def attend(i):
        n = (i + 1) * HD

        for hh in range(heads):
            _, _, local_s, far, lane = scores(hh, i, n)
            top = jnp.maximum(jnp.max(local_s, axis=-1, keepdims=True), jnp.max(far, axis=-1, keepdims=True))
            local_e, far_e = jnp.exp(local_s - top), jnp.exp(far - top)
            total = jnp.sum(local_e, axis=-1, keepdims=True) + jnp.sum(far_e, axis=-1, keepdims=True)
            inv = 1.0 / total
            lse[i * HD : (i + 1) * HD, hh : hh + 1] = top + jnp.log(total)
            out = plain_dot((local_e * inv).astype(BF), value_of(hh, n)) + plain_dot((far_e * inv).astype(BF), mv[:, lane])
            aof[i * HD : (i + 1) * HD, pl.ds(aligned(col0 + hh * HD, HD), HD)] = out.astype(BF)

        att_copy(i).start()

    for i in range(n_q):
        attend(i)
        if i == 0:
            step(4)
        if i == 2:
            step(5)

    step(6)
    out_over.wait_recv()
    out_next.start()
    step(7)
    arrived(3)
    out_next.wait_recv()
    for i in range(n_q):
        att_copy(i).wait_recv()

    @pl.loop(0, width // 256)
    def _(i):
        at = aligned(i * 256, 256)
        h[:, pl.ds(at, 256)] = xf[:, pl.ds(at, 256)].astype(F32) + plain_dot(aof[...], w_cols(wo, at, 256))

    @pl.loop(0, length // 64)
    def _(i):
        at = aligned(i * 64, 64)
        hc = h[pl.ds(at, 64)]
        inv = lax.rsqrt(jnp.mean(hc * hc, axis=-1, keepdims=True) + EPS)
        act[pl.ds(at, 64)] = (hc * inv * gain[1:2]).astype(BF)

    def transpose_to(dst, src):
        @pl.loop(0, n_q)
        def _(i):
            at = aligned(i * HD, HD)
            dst[0:width, pl.ds(at, HD)] = jnp.transpose(src[pl.ds(at, HD)])

    def up_tile(j):
        at = aligned(j * 256, 256)
        both = plain_dot(act[...], w_cols(wb, at, 256))
        gate, up = both[:, :128], both[:, 128:]
        sig = 1.0 / (1.0 + jnp.exp(-gate))
        silu = gate * sig
        tile = (silu * up).astype(BF)
        lanes = pl.ds(aligned(j * 128, 128), 128)
        hid[:, lanes] = tile
        tr[lanes] = jnp.transpose(tile)
        dgu[:, pl.ds(at, 128)] = (up * sig * (1.0 + gate * (1.0 - sig))).astype(BF)
        dgu[:, pl.ds(aligned(at + 128, 128), 128)] = silu.astype(BF)

    for g in range(4, n_groups):
        if g > 5 and g != 6:
            step(g + 1)
        arrived(g)
        pl.loop((g - 4) * 2, (g - 4) * 2 + groups[g][2] // 256)(up_tile)

    first[dx].wait_recv()
    local[dx].wait()

    red = [(None, c_d, y_d, z_d, 0, 512), (None, c_d, y_d, z_d, 512, 512)]
    red += [(go if i == 0 else wb, c_b, y_b, z_b, i, n) for i, n in chunk(2 * ff)]
    z_first = {2: 0, 5: 1}
    red += [(wb, c_o, y_o, z_o, 0, 512)]
    red += [(wo, c_a, y_a, z_a, 0, 512), (wo, c_a, y_a, z_a, 512, 512)]
    red += [(go, c_a, y_a, z_a, 1024, 512), (wa, c_a, y_a, z_a, 1536, 128)]
    n_red = len(red)
    x_at = [0, 512]
    for g in range(2, n_red):
        x_at.append(sum(red[i][5] for i in range(2, g)))

    def red_c(g):
        src, cb, _, _, at, n = red[g]
        lanes = pl.ds(at, n)
        source = gc.at[:, :, :, lanes] if g < 2 else src.at[:, :, 1 - c, :, pl.ds(0 if src is go else at, n)]
        return remote(source, cb.at[:, :, :, lanes], rcs.at[g], rcr.at[g], over_c)

    def red_y(g):
        _, cb, yb, _, at, n = red[g]
        lanes = pl.ds(at, n)
        if g in z_first:
            return remote(cb.at[z, 1 - y, :, lanes], yb.at[0, :, lanes], rys.at[g], ryr.at[g], over_y)
        return remote(cb.at[:, 1 - y, :, lanes], yb.at[:, :, lanes], rys.at[g], ryr.at[g], over_y)

    def z_parts(g):
        _, cb, yb, zb, at, n = red[g]
        lanes = pl.ds(at, n)
        if g in z_first:
            return (lambda zz: cb.at[zz, :, :, lanes]), (lambda k: z_w.at[z_first[g], k])
        return (lambda zz: yb.at[zz, :, lanes]), (lambda k: zb.at[k, :, lanes])

    def red_z(g, d):
        src, dst = z_parts(g)
        zz = (z + d) % 4
        return remote(src(zz), dst(d - 1), rzs.at[g, d - 1], rzr.at[g, d - 1], device(zz, y, c, x))

    def red_far(g):
        src, dst = z_parts(g)
        return remote(src(3 - z), dst(3), rzs.at[g, 3], rzr.at[g, 3], device(1 + z // 3, y, c, x))

    def start_red_z(g):
        @pl.when(jnp.logical_not(inner))
        def _():
            red_far(g).start()
            red_z(g, 2).start()

        pl.when(jnp.logical_not(end_high))(lambda: red_z(g, 1).start())
        pl.when(jnp.logical_not(end_low))(lambda: red_z(g, 3).start())

    def merge(g):
        @pl.when(inner)
        def _():
            red_far(g).wait_recv()
            src, dst = z_parts(g)
            away = src((z + 2) % 4)
            away[...] = (away[...].astype(F32) + dst(3)[...].astype(F32)).astype(BF)
            red_z(g, 2).start()

    def wait_red_z(g):
        red_z(g, 2).wait_recv()
        pl.when(jnp.logical_not(end_low))(lambda: red_z(g, 1).wait_recv())
        pl.when(jnp.logical_not(end_high))(lambda: red_z(g, 3).wait_recv())

    def total_z(g):
        src, dst = z_parts(g)
        total = src(z)[...].astype(F32)
        for k in range(3):
            total = total + dst(k)[...].astype(F32)
        return total

    def red_x(g):
        lanes = pl.ds(x_at[g], red[g][5])
        buf = x_d if g < 2 else x_n
        return remote(buf.at[0, :, lanes], buf.at[1, :, lanes], rxs.at[g], rxr.at[g], over_x)

    def only_mine(fn):
        def run(g):
            if g < 2:
                pl.when(mine)(lambda: fn(g))
            else:
                fn(g)

        return run

    def start_c(g):
        if g < 2:
            pl.when(other)(lambda: red_c(g).start())
        else:
            red_c(g).start()

    @only_mine
    def sum_c(g):
        red_c(g).wait_recv()
        src, cb, _, _, at, n = red[g]
        lanes = pl.ds(at, n)

        @pl.loop(0, 8)
        def _(i):
            own = gc[i // 2, i % 2, :, lanes] if g < 2 else src[i // 2, i % 2, c, :, pl.ds(0 if src is go else at, n)]
            cb[i // 2, i % 2, :, lanes] = (cb[i // 2, i % 2, :, lanes].astype(F32) + own.astype(F32)).astype(BF)

        start_red_z(g) if g in z_first else red_y(g).start()

    @only_mine
    def stage_one(g):
        if g in z_first:
            merge(g)
            return
        red_y(g).wait_recv()
        _, cb, yb, _, at, n = red[g]
        lanes = pl.ds(at, n)

        @pl.loop(0, 4)
        def _(i):
            yb[i, :, lanes] = (yb[i, :, lanes].astype(F32) + cb[i, y, :, lanes].astype(F32)).astype(BF)

        start_red_z(g)

    @only_mine
    def stage_two(g):
        if g in z_first:
            wait_red_z(g)
            src, _ = z_parts(g)
            src(z)[...] = total_z(g).astype(BF)
            red_y(g).start()
        else:
            merge(g)

    def result(g, which, value):
        at, n = red[g][4], red[g][5]
        if g < 2:
            out_d[:, at : at + n] = value
        elif g < n_red - 5:
            out_b[which, :, at : at + n] = value
        elif g == n_red - 1:
            out_g[which] = value
        else:
            out = [out_o, out_q, out_k, out_v][g - (n_red - 5)]
            out[:, pl.ds(aligned(which * cols, cols), cols)] = value

    @only_mine
    def stage_three(g):
        _, cb, yb, _, at, n = red[g]
        lanes = pl.ds(at, n)
        if g in z_first:
            red_y(g).wait_recv()
            total = cb[z, y, :, lanes].astype(F32) + yb[0, :, lanes].astype(F32)
        else:
            wait_red_z(g)
            total = total_z(g)
        size = yb.shape[1] // 2
        low, high = total[:size], total[size:]
        buf = x_d if g < 2 else x_n
        buf[0, :, pl.ds(x_at[g], n)] = jnp.where(x == 0, high, low).astype(BF)
        red_x(g).start()
        result(g, x, jnp.where(x == 0, low, high))

    def finish(g):
        lanes = pl.ds(x_at[g], red[g][5])

        def take():
            red_x(g).wait_recv()
            result(g, 1 - x, (x_d if g < 2 else x_n)[1, :, lanes].astype(F32))

        if g < 2:
            pl.when(other)(take)
        else:
            take()

    @only_mine
    def red_sent(g):
        red_y(g).wait_send()
        red_z(g, 2).wait_send()
        pl.when(jnp.logical_not(end_high))(lambda: red_z(g, 1).wait_send())
        pl.when(jnp.logical_not(end_low))(lambda: red_z(g, 3).wait_send())
        pl.when(jnp.logical_not(inner))(lambda: red_far(g).wait_send())
        red_x(g).wait_send()

    done_at = {}

    def advance(stage, upto):
        fns = [sum_c, stage_one, stage_two, stage_three, finish]
        for g in range(done_at.get(stage, 0), min(upto + 1, n_red)):
            fns[stage](g)
        done_at[stage] = max(done_at.get(stage, 0), min(upto + 1, n_red))

    def tick(k, cap=n_red):
        for stage, lag in enumerate((0, 3, 5, 7, 8)):
            advance(stage, min(k - lag, cap))

    @pl.when(end_low)
    def _():
        for zb in (z_a, z_o, z_b, z_d):
            zb[0] = jnp.zeros(zb.shape[1:], BF)
        for i in range(2):
            z_w[i, 0] = jnp.zeros(z_w.shape[2:], BF)

    @pl.when(end_high)
    def _():
        for zb in (z_a, z_o, z_b, z_d):
            zb[2] = jnp.zeros(zb.shape[1:], BF)
        for i in range(2):
            z_w[i, 2] = jnp.zeros(z_w.shape[2:], BF)

    for i in range(2):

        @pl.loop(0, 4)
        def _(t):
            res = plain_dot(tr[pl.ds(aligned(t * 2 * blk, 32), 2 * blk)], dyf[:, i * 512 : (i + 1) * 512])
            gc[t, :, :, i * 512 : (i + 1) * 512] = res.reshape(2, blk, 512).astype(BF)

        start_c(i)
    step(n_groups + 1)
    advance(0, 0)
    advance(0, 1)
    step(n_groups + 2)
    transpose_to(tr_two, act)

    def wait_down():
        for g in range(n_groups, last_group + 1):
            arrived(g)

    pl.when(other)(wait_down)

    def dhid_tile(j, n):
        lanes = aligned(j * 128, 128)
        res = dot_right(dyf[...], wc[pl.ds(lanes, 128 * n)])
        for t in range(n):
            at = aligned((j + t) * 256, 256)
            d = res[:, t * 128 : (t + 1) * 128]
            for s in range(2):
                where = pl.ds(aligned(at + 128 * s, 128), 128)
                dgu[:, where] = (d * dgu[:, where].astype(F32)).astype(BF)

    n_tiles = ff // 128

    @pl.loop(0, n_tiles // 2)
    def _(t):
        dhid_tile(t * 2, 2)

    if n_tiles % 2:
        dhid_tile(n_tiles - 1, 1)

    def grad_tile(dst, lhs, value, at):
        res = plain_dot(lhs[0:width], value)
        dst[:, :, :, :, pl.ds(at, 256)] = res.reshape(4, 2, 2, 64, 256).astype(BF)

    n_b = len(chunk(2 * ff))

    def grad_ff(g):
        at0, n = red[2 + g][4], red[2 + g][5]
        for t in range(n // 256):
            grad_tile(go if g == 0 else wb, tr_two, dgu[:, at0 + t * 256 : at0 + (t + 1) * 256], at0 + t * 256)
        start_c(2 + g)

    grad_ff(0)
    gain_acc[...] = jnp.zeros_like(gain_acc)

    def swap_copy(i):
        at = pl.ds(128 * i, 128)
        return remote(swap_s.at[at], swap_r.at[at], es.at[8 + i], er.at[8 + i], over_x)

    for f in range(2):

        @pl.loop(0, width // 256)
        def _(i):
            at = aligned(i * 256, 256)
            res = dot_right(dgu[f * rows : (f + 1) * rows], wb[i, :, :, :, :].reshape(256, 2 * ff))
            part[f * rows : (f + 1) * rows, pl.ds(at, 256)] = res
            swap_s[f * rows : (f + 1) * rows, pl.ds(at, 256)] = res.astype(BF)

        swap_copy(2 * f).start()
        swap_copy(2 * f + 1).start()

    def add_gain(k, grad, unit):
        prod = grad * unit
        gain_acc[k] += jnp.sum(prod.reshape(prod.shape[0] // 8, 8, width), axis=0)

    for g in range(4, n_groups):
        sent(g)
    for g in range(1, n_b):
        grad_ff(g)
        if g == 1:
            advance(0, 2)
        if g == 2:
            advance(1, 0)
        if g == 3:
            advance(0, 3)
        if g == 4:
            advance(1, 1)
        if g == 5:
            advance(0, 4)

    def d_hidden_rows(i):
        at = aligned(i * 64, 64)
        hc = h[pl.ds(at, 64)]
        inv = lax.rsqrt(jnp.mean(hc * hc, axis=-1, keepdims=True) + EPS)
        u = hc * inv
        add_gain(1, part[pl.ds(at, 64)], u)
        e = (part[pl.ds(at, 64)] + swap_r[pl.ds(at, 64)].astype(F32)) * gain[1:2]
        dh = dyf[pl.ds(at, 64)].astype(F32) + inv * (e - u * jnp.mean(e * u, axis=-1, keepdims=True))
        part[pl.ds(at, 64)] = dh
        act[pl.ds(at, 64)] = dh.astype(BF)

    kv_acc[...] = jnp.zeros_like(kv_acc)
    w_own = wo.at[pl.ds(x * 2, 2)]

    def attend_back(i):
        n = (i + 1) * HD
        at = slice(i * HD, (i + 1) * HD)
        d_att = dot_right(act[at], w_own[...].reshape(cols, width)).astype(BF)
        for hh in range(heads):
            query, key, local_s, far, lane = scores(hh, i, n)
            log_sum = lse[at, hh : hh + 1]
            p_l, p_m = jnp.exp(local_s - log_sum), jnp.exp(far - log_sum)
            grad = d_att[:, hh * HD : (hh + 1) * HD]
            out = aof[at, pl.ds(aligned(col0 + hh * HD, HD), HD)]
            delta = jnp.sum(grad.astype(F32) * out.astype(F32), axis=-1, keepdims=True)
            ds_l = (p_l * (dot_right(grad, value_of(hh, n)) - delta)).astype(BF)
            ds_m = (p_m * (dot_right(grad, mv[:, lane]) - delta)).astype(BF)
            dq = (plain_dot(ds_l, key) + plain_dot(ds_m, mk[:, lane])) * scale
            dqkv[at, hh * HD : (hh + 1) * HD] = dq.astype(BF)
            kv_acc[0, 0:n, hh * HD : (hh + 1) * HD] += dot_left(ds_l, query)
            kv_acc[1, 0:n, hh * HD : (hh + 1) * HD] += dot_left(p_l.astype(BF), grad)

    base = 4
    for i in range(n_q):
        swap_copy(i).wait_recv()
        pl.loop(i * 2, i * 2 + 2)(d_hidden_rows)
        attend_back(i)
        if i == 0:
            transpose_to(tr, aof)
        if i == 1:

            @pl.loop(0, n_q)
            def _(j):
                rows_at = aligned(j * HD, HD)
                unit, _ = norm_rows(rows_at, HD)
                tr_one[:, pl.ds(rows_at, HD)] = jnp.transpose((unit * gain[0:1]).astype(BF))

        if i == n_q - 1:

            @pl.loop(0, width // 256)
            def _(j):
                at = aligned(j * 256, 256)
                row_s[:, pl.ds(at, 256)] = plain_dot(hid[pl.ds(peer, rows)], wc[:, pl.ds(at, 256)]).astype(BF)

            row_y = remote(row_s, row_r.at[0], es.at[12], er.at[12], over_x)
            row_y.start()
        for _ in range([1,1,1,1][i]):
            tick(base, 1 + n_b)
            base += 1
    sent(3)
    out_over.wait_send()
    out_next.wait_send()
    dqkv[:, cols : 2 * cols] = (kv_acc[0] * scale).astype(BF)
    dqkv[:, 2 * cols :] = kv_acc[1].astype(BF)

    def grad_tile_one(dst, at, to):
        res = plain_dot(tr_one[...], dqkv[:, at : at + 256])
        dst[:, :, :, :, to : to + 256] = res.reshape(4, 2, 2, 64, 256).astype(BF)

    for t in range(2):
        grad_tile(wb, tr, act[:, pl.ds(aligned(col0 + t * 256, 256), 256)], t * 256)
    start_c(2 + n_b)
    for g in range(2):
        for t in range(2):
            grad_tile_one(wo, g * cols + t * 256, g * cols + t * 256)
        start_c(3 + n_b + g)
    red_c(2).wait_send()
    for t in range(2):
        grad_tile_one(go, 2 * cols + t * 256, t * 256)
    start_c(5 + n_b)
    tick(base)
    base += 1

    row_y.wait_send()
    def d_one(at):
        return jnp.concatenate([kv_acc[0, pl.ds(at, 64)], kv_acc[1, pl.ds(at, 64)]], axis=1)

    for first_half in (False, True):
        half_rows = pl.ds(own if first_half else peer, rows)

        @pl.loop(0, width // 256)
        def _(i):
            at = aligned(i * 256, 256)
            res = dot_right(dqkv[half_rows], wa[i, :, :, :, 0 : 3 * cols].reshape(256, 3 * cols))
            if not first_half:
                row_s[:, pl.ds(at, 256)] = res.astype(BF)
            kv_acc[i // 2, half_rows, pl.ds(aligned((i % 2) * 256, 256), 256)] = res

        if not first_half:
            row_x = remote(row_s, row_r.at[1], es.at[13], er.at[13], over_x)
            row_x.start()

    @pl.loop(0, length // 64)
    def _(i):
        at = aligned(i * 64, 64)
        u, _ = norm_rows(at, 64)
        add_gain(0, d_one(at), u)

    for g in range(3):
        sent(g)
    sums = [jnp.sum(gain_acc[k], axis=0, keepdims=True) for k in range(2)]
    tall = lax.broadcasted_iota(jnp.int32, (128, 128), 0)
    for p in range(8):
        lanes = slice(p * 128, (p + 1) * 128)
        both = jnp.where(tall == 0, sums[0][:, lanes], jnp.where(tall == 1, sums[1][:, lanes], 0.0))
        wa[p // 2, p % 2, :, :, 3 * cols :] = jnp.transpose(both).reshape(2, 64, 128).astype(BF)
    start_c(6 + n_b)
    tick(base)
    base += 1
    row_y.wait_recv()

    @pl.loop(0, width // 256)
    def _(i):
        at = aligned(i * 256, 256)
        mine_y = plain_dot(hid[pl.ds(own, rows)], wc[:, pl.ds(at, 256)]) + h[pl.ds(own, rows), pl.ds(at, 256)]
        out_y[:, pl.ds(at, 256)] = (mine_y + row_r[0, :, pl.ds(at, 256)].astype(F32)).astype(BF)
    tick(base)
    base += 1
    row_x.wait_recv()

    @pl.loop(0, rows // 64)
    def _(i):
        at = aligned(own + i * 64, 64)
        u, inv = norm_rows(at, 64)
        e = (d_one(at) + row_r[1, pl.ds(aligned(i * 64, 64), 64)].astype(F32)) * gain[0:1]
        out = part[pl.ds(at, 64)] + inv * (e - u * jnp.mean(e * u, axis=-1, keepdims=True))
        out_x[pl.ds(aligned(i * 64, 64), 64)] = out.astype(BF)

    for k in range(base, n_red + 8):
        tick(k)
    for cp in first:
        cp.wait_send()
    pl.when(other)(lambda: down_x.wait_send())
    for g in range(n_groups, last_group + 1):
        sent(g)
    for i in range(4):
        swap_copy(i).wait_send()
    for i in range(n_q):
        att_copy(i).wait_send()
    row_x.wait_send()
    for g in range(n_red):
        if g < 2:
            pl.when(other)(lambda: red_c(g).wait_send())
        elif g != 2:
            red_c(g).wait_send()
        red_sent(g)


def layer(tok, cot, mem_k, mem_v, choice, flag, w_q, w_k, w_v, w_o, w_b, w_d, gains):
    rows, width = tok.shape
    length = 2 * rows
    cols = width // 2
    ff2 = w_b.shape[2]
    ff = ff2 // 2
    blk = ff // 8
    na = 3 * cols + 128
    hbm, vm = pl.BlockSpec(memory_space=pl.ANY), pl.BlockSpec(memory_space=pltpu.VMEM)
    own = w_q.shape[0]
    shape = jax.ShapeDtypeStruct
    return pl.pallas_call(
        layer_kernel,
        name="layer",
        out_shape=(
            shape((rows, width), BF),
            shape((rows, width), BF),
            shape((own, width), F32),
            shape((own, width), F32),
            shape((own, width), F32),
            shape((own, width), F32),
            shape((2, own, ff2), F32),
            shape((blk // 2, width), F32),
            shape((2, own, 128), F32),
        ),
        in_specs=[hbm] * 4 + [vm] * 2 + [hbm] * 7,
        out_specs=(vm,) * 9,
        scratch_shapes=[
            VM((4, 2, 2, 64, na), BF), VM((4, 2, 2, 64, width), BF), VM((4, 2, 2, 64, ff2), BF), VM((ff, width), BF), VM((2, blk // 2, width), BF),
            VM((4, 2, blk, width), BF), VM((4, 2, 2, 64, cols), BF),
            VM((4, 2, 64, na), BF), VM((4, 2, 64, cols), BF), VM((4, 2, 64, ff2), BF), VM((4, 2, blk, width), BF),
            VM((4, 64, na), BF), VM((4, 64, cols), BF), VM((4, 64, ff2), BF), VM((4, blk, width), BF),
            VM((4, 64, na), BF), VM((4, 64, cols), BF), VM((4, 64, ff2), BF), VM((4, blk, width), BF),
            VM((2, 4, 2, 64, 512), BF),
            VM((2, own, ff2 + na + cols), BF), VM((2, blk // 2, width), BF),
            VM((length, width), BF), VM((length, width), BF), VM((length, width), BF), VM((ff, length), BF),
            VM((length, 3 * cols), BF), VM((length, width), BF), VM((length, width), F32), VM((length, ff), BF),
            VM((length, ff2), BF), VM((length, width), F32), VM((length, width), BF), VM((length, width), BF),
            VM((length, 3 * cols), BF), VM((2, length, cols), F32), VM((HD, cols), BF), VM((HD, cols), BF),
            VM((width, length), BF), VM((width, length), BF), VM((length, 128), F32),
            VM((rows, width), BF), VM((2, rows, width), BF), VM((8, width), F32), VM((2, 8, width), F32),
            DMA((2,)), DMA((2,)), DMA((16,)), DMA((16,)), DMA((16,)), DMA((12, 2, 4)), DMA((12, 2, 4)),
            DMA((12, 4)), DMA((12, 4)), DMA((12, 4, 2)), DMA((12, 4, 2)), DMA((2, 8)), DMA((14,)), DMA((14,)),
            DMA((13,)), DMA((13,)), DMA((13,)), DMA((13,)), DMA((13, 4)), DMA((13, 4)), DMA((13,)), DMA((13,)),
        ],
        compiler_params=pltpu.CompilerParams(collective_id=0, has_side_effects=True, vmem_limit_bytes=127 << 19),
    )(tok, cot, mem_k, mem_v, choice, flag, w_q, w_k, w_v, w_o, w_b, w_d, gains)


def prepare_kernel(w_g, w_u, norms, choice, flag, w_b, gains, columns, flags):
    wide = w_g.shape[1]
    strip = wide // 16
    for half in range(2):
        packed = []
        for w in (w_g, w_u):
            whole = w[...].astype(F32)
            cuts = [whole[:, (2 * p + half) * strip : (2 * p + half + 1) * strip] for p in range(8)]
            packed.append(jnp.concatenate(cuts, axis=1).astype(BF))
        for j in range(wide // 256):
            for i in range(2):
                w_b[half, :, (2 * j + i) * 128 : (2 * j + i + 1) * 128] = packed[i][:, j * 128 : (j + 1) * 128]
    own = norms.shape[1]
    tall = lax.broadcasted_iota(jnp.int32, (128, own), 0)
    both = norms[...].astype(F32)
    both = jnp.where(tall == 0, both[0:1], jnp.where(tall == 1, both[1:2], 0.0))
    gains[...] = jnp.transpose(both).astype(BF)
    many = jnp.concatenate([choice[...].astype(F32)] * (128 // choice.shape[0]), axis=0)
    columns[...] = jnp.transpose(many).astype(jnp.int32)
    flags[...] = jnp.full(flags.shape, flag[0], jnp.int32)


def prepare(w_g, w_u, norms, choice, flag):
    own, wide = w_g.shape
    vm = pl.BlockSpec()
    shape = jax.ShapeDtypeStruct
    return pl.pallas_call(
        prepare_kernel,
        name="prepare",
        out_shape=(
            shape((2, own, wide), BF), shape((own, 128), BF), shape((128, 128), jnp.int32), shape((8, 128), jnp.int32),
        ),
        in_specs=[vm] * 4 + [pl.BlockSpec(memory_space=pltpu.SMEM)],
        out_specs=(vm,) * 4,
        compiler_params=pltpu.CompilerParams(vmem_limit_bytes=63 << 20),
    )(w_g, w_u, norms, choice, flag)


def complete_kernel(i_y, i_x, i_q, i_k, i_v, i_o, i_b, i_d, i_g, y, x, q, k, v, o, g, u, d, n_a, n_f):
    for src, dst in ((i_y, y), (i_x, x), (i_q, q), (i_k, k), (i_v, v), (i_o, o), (i_d, d)):
        dst[...] = src[...]
    wide = g.shape[1]
    strip = wide // 16
    for i, dst in enumerate((g, u)):
        halves = [
            jnp.concatenate(
                [i_b[half, :, (2 * j + i) * 128 : (2 * j + i + 1) * 128] for j in range(wide // 256)], axis=1
            )
            for half in range(2)
        ]
        cuts = [halves[p % 2][:, (p // 2) * strip : (p // 2 + 1) * strip] for p in range(16)]
        dst[...] = jnp.concatenate(cuts, axis=1)
    own = n_a.shape[1]
    tall = jnp.transpose(i_g[0] + i_g[1])
    n_a[...] = tall[0:1, 0:own]
    n_f[...] = tall[1:2, 0:own]


def complete(*parts):
    own, width = parts[2].shape
    wide = parts[6].shape[2]
    vm = pl.BlockSpec()
    shape = jax.ShapeDtypeStruct
    like = [shape(p.shape, p.dtype) for p in parts[:6]]
    like += [shape((own, wide), F32)] * 2 + [shape(parts[7].shape, F32)] + [shape((1, own), F32)] * 2
    return pl.pallas_call(
        complete_kernel,
        name="complete",
        out_shape=tuple(like),
        in_specs=[vm] * 9,
        out_specs=(vm,) * 11,
        compiler_params=pltpu.CompilerParams(vmem_limit_bytes=63 << 20),
    )(*parts)


def fast_body(
    tokens, cotangent, memory_keys, memory_values, memory_choice, memory_flag,
    w_query, w_key, w_value, w_out, w_gate, w_up, w_down, norm_attn, norm_ffn,
):
    norms = jnp.stack([norm_attn, norm_ffn])
    w_b, gains, choice, flag = prepare(w_gate, w_up, norms, memory_choice[0, 0], memory_flag)
    parts = layer(
        tokens[0], cotangent[0], memory_keys[0], memory_values[0], choice, flag,
        w_query, w_key, w_value, w_out, w_b, w_down, gains,
    )
    y, x, q, k, v, o, g, u, d, n_a, n_f = complete(*parts)
    return y[None], x[None], q, k, v, o, g, u, d, n_a[0], n_f[0]


def solution(mesh):
    in_specs = (
        P("seg", "row", None),
        P("seg", "row", None),
        P("seg", None, None),
        P("seg", None, None),
        P("seg", None, None, None),
        P("seg"),
        P(("seg", "row"), None),
        P(("seg", "row"), None),
        P(("seg", "row"), None),
        P(("seg", "row"), None),
        P(("seg", "row"), None),
        P(("seg", "row"), None),
        P(("seg", "row"), None),
        P(("seg", "row")),
        P(("seg", "row")),
    )
    out_specs = (
        P("seg", "row", None),
        P("seg", "row", None),
        P(("seg", "row"), None),
        P(("seg", "row"), None),
        P(("seg", "row"), None),
        P(("seg", "row"), None),
        P(("seg", "row"), None),
        P(("seg", "row"), None),
        P(("seg", "row"), None),
        P(("seg", "row")),
        P(("seg", "row")),
    )

    def body(*args):
        segs, rows, width = args[0].shape
        fits = (
            mesh.shape["row"] == 2
            and mesh.shape["seg"] == 16
            and segs == 1
            and (rows, width) == (256, 1024)
            and args[4].shape[1] == 1
        )
        return (fast_body if fits else general_body)(*args)

    return jax.shard_map(body, mesh=mesh, in_specs=in_specs, out_specs=out_specs, check_vma=False)
```
